32 devices in a mesh: fsdp: 4 (over y, x), dp: 8 (over z, core).
Axes of the slice: x: 2, y: 2, z: 4, core: 2. Of those that a mesh axis runs over, the one named last changes fastest.
Arguments:
- tokens: bfloat16 [16384, 1152], P(('fsdp', 'dp')), may hold values from -6 to 6
- conditions: bfloat16 [64, 1152], P(('fsdp', 'dp')), may hold values from -6 to 6
- cotangent: bfloat16 [16384, 1152], P(('fsdp', 'dp')), may hold values from -6 to 6
- slot_mask: int32 [64], P(('fsdp', 'dp')), may hold values from 0 to 1, as said below
- weight_flat: bfloat16 [186624, 128], P(('fsdp', 'dp')), may hold values from -3 to 3
- bias_flat: bfloat16 [17664], P(('fsdp', 'dp')), may hold values from -2 to 2
Outputs:
- out: bfloat16 [16384, 1152], P(('fsdp', 'dp'))
- grad_tokens: float32 [16384, 1152], P(('fsdp', 'dp'))
- grad_conditions: float32 [64, 1152], P(('fsdp', 'dp'))
- grad_weights: float32 [186624, 128], P(('fsdp', 'dp'))
- grad_biases: float32 [17664], P(('fsdp', 'dp'))
The draws below stay inside these ranges and needn't reach their ends.
Inputs may be any that keep to these rules, and one draw needn't show every extreme that they name: `slot_mask`: on each device's 2 image slots the live ones come first; a device has one live image or all 2, and some device has all 2 live in every draw.
All inputs are finite; a program needn't handle non-finite values.
Results may differ from the reference program's by a relative error of at most 0.0095.
Values may be sent and summed in bfloat16 or wider, within the bound.
No kernel may reach another device: no remote copies, remote signals or barrier semaphores. Data moves between devices by JAX's collectives and lax.ppermute only.
A program may use at most 576 MiB of HBM per device.

```python
import math
import jax
import jax.numpy as jnp
from jax import lax

D = 1152
HEADS = 16
HEAD_DIM = 72
FF = 3072
GRID = 16
SLOTS = 2
IMAGES = 64
TOKENS = 16384
BIGROWS = 186624
SMALL = 17664


def draw_weight_flat(key, part):
    place = jnp.arange(BIGROWS * 128, dtype=jnp.int32).reshape(BIGROWS, 128)
    end_qkv = 3 * D * D
    end_out = end_qkv + D * D
    end_ada = end_out + 2 * D * FF + 6 * D * D
    base = 1.0 / math.sqrt(D)
    scales = jnp.where(place < end_qkv, base, jnp.where(place < end_out, 4.0 * base, jnp.where(place < end_ada, base, 1.0 / math.sqrt(FF))))
    raw = jnp.clip(jax.random.normal(key, (BIGROWS, 128), jnp.float32), -3.0, 3.0)
    return (raw * scales).astype(jnp.bfloat16)


def draw_bias_flat(key, part):
    raw = 0.3 * jnp.clip(jax.random.normal(key, (SMALL,), jnp.float32), -4.0, 4.0)
    return raw.astype(jnp.bfloat16)


def draw_slot_mask(key, part):
    devices = IMAGES // SLOTS
    first, second = jax.random.split(key)
    kinds = jax.random.randint(first, (devices,), 0, 3)
    fullest = jax.random.randint(second, (), 0, devices)
    counts = jnp.where(kinds == 0, SLOTS, 1)
    counts = jnp.where(jnp.arange(devices) == fullest, SLOTS, counts)
    return (jnp.arange(SLOTS)[None, :] < counts[:, None]).astype(jnp.int32).reshape(-1)


def levels(rng, dims, shards, smallest, top_value):
    factor_of, own = 1.0, jax.random.fold_in(rng, 6)
    for axis_at, blocks in shards:
        draws = jnp.exp(jax.random.uniform(jax.random.fold_in(own, axis_at), (blocks,), jnp.float32, smallest / len(shards), top_value / len(shards)))
        factor_of = factor_of * jnp.repeat(draws, dims[axis_at] // blocks).reshape([-1 if axis == axis_at else 1 for axis in range(len(dims))])
    return factor_of


def gaussian(rng, extent, spread, most, shards=(), kind=jnp.bfloat16):
    array = spread * jax.random.normal(rng, extent, jnp.float32)
    if shards:
        array = array * levels(rng, extent, shards, -0.22, 0.18)
    return jnp.clip(array, -most, most).astype(kind)


def setup_inputs(seed: int = 0) -> dict:
    key_list = jax.random.split(jax.random.key(seed), 7)
    tokens = gaussian(key_list[0], (TOKENS, D), 1.0, 6.0, ((0, 32),))
    conditions = gaussian(key_list[1], (IMAGES, D), 1.0, 6.0, ((0, 32),))
    cotangent = gaussian(key_list[2], (TOKENS, D), 1.0, 6.0, ((0, 32),))
    slot_mask = draw_slot_mask(jax.random.fold_in(key_list[6], 71), 0)
    weight_flat = draw_weight_flat(jax.random.fold_in(key_list[6], 71), 0)
    bias_flat = draw_bias_flat(jax.random.fold_in(key_list[6], 71), 0)
    return {"tokens": tokens, "conditions": conditions, "cotangent": cotangent, "slot_mask": slot_mask, "weight_flat": weight_flat, "bias_flat": bias_flat}


@jax.custom_vjp
def low(v):
    return lax.optimization_barrier(v.astype(jnp.bfloat16)).astype(jnp.float32)

@jax.custom_vjp
def low_back(v):
    return v

def low_keep(v):
    return (low(v), None)

def low_pass(kept, grad):
    return (grad,)

def back_keep(v):
    return (v, None)

def back_low(kept, grad):
    return (low(grad),)
low.defvjp(low_keep, low_pass)
low_back.defvjp(back_keep, back_low)
eps_norm = 1e-06

def unpack_weights(weight_all, bias_all):
    flat = weight_all.reshape(-1)
    layouts = ((D, 3 * D), (D, D), (D, 2 * FF), (D, 6 * D), (FF, D))
    pieces = []
    offset = 0
    for layout in layouts:
        amount = layout[0] * layout[1]
        pieces.append(flat[offset:offset + amount].reshape(layout))
        offset = offset + amount
    offset = 0
    for amount in (3 * D, D, 2 * FF, 6 * D):
        pieces.append(bias_all[offset:offset + amount])
        offset = offset + amount
    return tuple(pieces)

def rope_tables():
    quarter = HEAD_DIM // 4
    places = jnp.arange(GRID * GRID, dtype=jnp.int32)
    rows_at = (places // GRID).astype(jnp.float32)
    cols_at = (places % GRID).astype(jnp.float32)
    freqs = 10000.0 ** (-jnp.arange(quarter, dtype=jnp.float32) / quarter)
    along_rows = rows_at[:, None] * freqs[None, :]
    along_cols = cols_at[:, None] * freqs[None, :]
    angles = jnp.concatenate([along_rows, along_rows, along_cols, along_cols], axis=1)
    return (jnp.cos(angles)[:, None, :], jnp.sin(angles)[:, None, :])

def turn_half(values):
    quarter = values.shape[-1] // 4
    first = values[..., :quarter]
    second = values[..., quarter:2 * quarter]
    third = values[..., 2 * quarter:3 * quarter]
    fourth = values[..., 3 * quarter:]
    return jnp.concatenate([-second, first, -fourth, third], axis=-1)

def rotate(values, cosines, sines):
    return values * cosines + turn_half(values) * sines

def layer_norm(values):
    centred = values - lax.optimization_barrier(jnp.mean(values, -1, keepdims=True))
    return centred * lax.rsqrt(lax.optimization_barrier(jnp.mean(centred * centred, -1, keepdims=True)) + eps_norm)

def rms_norm(values):
    return values * lax.rsqrt(lax.optimization_barrier(jnp.mean(values * values, -1, keepdims=True)) + eps_norm)

def forward(x_all, cond_all, weight_all, bias_all, mask_all):
    high_precision = lax.Precision.HIGHEST
    query_key_value_weight, projection_weight, feedforward_weight, w_ada, down_weight, query_key_value_bias, projection_bias, feedforward_bias, b_ada = unpack_weights(weight_all, bias_all)
    cosines, sines = rope_tables()
    length = GRID * GRID
    groups = x_all.shape[0] // SLOTS
    scale = 1.0 / math.sqrt(HEAD_DIM)
    heads_shape = (SLOTS, length, HEADS, HEAD_DIM)

    def one_group(x_part, cond_part, mask_part):
        cond_act = low(jax.nn.silu(cond_part))
        modulation = low_back(jnp.dot(cond_act, w_ada, precision=high_precision) + b_ada)
        shift_a, scale_a, gate_a, shift_b, scale_b, gate_b = [modulation[:, None, place * D:(place + 1) * D] for place in range(6)]
        attention_input = low(layer_norm(x_part) * (1.0 + scale_a) + shift_a)
        projected_output = low_back(jnp.einsum('mto,op->mtp', attention_input, query_key_value_weight, precision=high_precision) + query_key_value_bias)
        queries = low(rotate(rms_norm(projected_output[..., :D].reshape(heads_shape)), cosines, sines))
        keys = low(rotate(rms_norm(projected_output[..., D:2 * D].reshape(heads_shape)), cosines, sines))
        values = low(projected_output[..., 2 * D:].reshape(heads_shape))
        scores = low_back(jnp.einsum('slhe,smhe->shlm', queries, keys, precision=high_precision) * scale)
        log_total = jax.nn.logsumexp(scores, axis=-1, keepdims=True)
        probs_low = low(jnp.exp(scores - log_total))
        attention_output = jnp.einsum('shlm,smhe->slhe', probs_low, values, precision=high_precision).reshape(SLOTS, length, D)
        attention_output = low_back(low(attention_output))
        attention_branch = low_back(jnp.einsum('mto,op->mtp', attention_output, projection_weight, precision=high_precision) + projection_bias)
        middle = x_part + gate_a * attention_branch
        feedforward_input = low(layer_norm(middle) * (1.0 + scale_b) + shift_b)
        mixed_tokens = low_back(jnp.einsum('mto,op->mtp', feedforward_input, feedforward_weight, precision=high_precision) + feedforward_bias)
        hidden_state = low(jax.nn.silu(mixed_tokens[..., :FF]) * mixed_tokens[..., FF:])
        feedforward_branch = low_back(jnp.einsum('ijm,mo->ijo', hidden_state, down_weight, precision=high_precision))
        return (middle + gate_b * feedforward_branch) * mask_part[:, None, None]
    checked = jax.checkpoint(one_group)

    def scan_step(carry, inputs):
        return (carry, checked(inputs[0], inputs[1], inputs[2]))
    start = jnp.zeros((), jnp.float32)
    stacked = (x_all.reshape(groups, SLOTS, length, D), cond_all.reshape(groups, SLOTS, D), mask_all.reshape(groups, SLOTS))
    _, results = lax.scan(scan_step, start, stacked)
    return results.reshape(groups * SLOTS, length, D)

def reference(tokens, conditions, cotangent, slot_mask, weight_flat, bias_flat):
    length = GRID * GRID
    x_all = tokens.astype(jnp.float32).reshape(IMAGES, length, D)
    cond_all = conditions.astype(jnp.float32)
    weight_all = weight_flat.astype(jnp.float32)
    bias_all = bias_flat.astype(jnp.float32)
    mask_all = slot_mask.astype(jnp.float32)

    def wrapped(x_in, cond_in, weight_in, bias_in):
        return forward(x_in, cond_in, weight_in, bias_in, mask_all)
    result, pull = jax.vjp(wrapped, x_all, cond_all, weight_all, bias_all)
    grad_x, grad_cond, grad_weight, grad_bias = pull(cotangent.astype(jnp.float32).reshape(IMAGES, length, D))
    return (result.reshape(TOKENS, D).astype(jnp.bfloat16), grad_x.reshape(TOKENS, D), grad_cond, grad_weight, grad_bias)
```

```python
import math

import jax
import jax.numpy as jnp
from jax import lax
from jax.sharding import PartitionSpec as P

D = 1152
HEADS = 16
HEAD_DIM = 72
FF = 3072
GRID = 16


eps_norm = 1e-06


def unpack_weights(weight_all, bias_all):
    flat = weight_all.reshape(-1)
    layouts = ((D, 3 * D), (D, D), (D, 2 * FF), (D, 6 * D), (FF, D))
    pieces = []
    offset = 0
    for layout in layouts:
        amount = layout[0] * layout[1]
        pieces.append(flat[offset : offset + amount].reshape(layout))
        offset = offset + amount
    offset = 0
    for amount in (3 * D, D, 2 * FF, 6 * D):
        pieces.append(bias_all[offset : offset + amount])
        offset = offset + amount
    return tuple(pieces)


def rope_tables():
    quarter = HEAD_DIM // 4
    places = jnp.arange(GRID * GRID, dtype=jnp.int32)
    rows_at = (places // GRID).astype(jnp.float32)
    cols_at = (places % GRID).astype(jnp.float32)
    freqs = 10000.0 ** (-jnp.arange(quarter, dtype=jnp.float32) / quarter)
    along_rows = rows_at[:, None] * freqs[None, :]
    along_cols = cols_at[:, None] * freqs[None, :]
    angles = jnp.concatenate([along_rows, along_rows, along_cols, along_cols], axis=1)
    return (jnp.cos(angles)[:, None, :], jnp.sin(angles)[:, None, :])


def turn_half(values):
    quarter = values.shape[-1] // 4
    first = values[..., :quarter]
    second = values[..., quarter : 2 * quarter]
    third = values[..., 2 * quarter : 3 * quarter]
    fourth = values[..., 3 * quarter :]
    return jnp.concatenate([-second, first, -fourth, third], axis=-1)


def norm_parts(values):
    centred = values - jnp.mean(values, -1, keepdims=True)
    inverse = lax.rsqrt(jnp.mean(centred * centred, -1, keepdims=True) + eps_norm)
    return (centred * inverse, inverse)


def norm_back(grad_normed, normed, inverse):
    return inverse * (
        grad_normed
        - jnp.mean(grad_normed, -1, keepdims=True)
        - normed * jnp.mean(grad_normed * normed, -1, keepdims=True)
    )


def rms_parts(values):
    inverse = lax.rsqrt(jnp.mean(values * values, -1, keepdims=True) + eps_norm)
    return (values * inverse, inverse)


def rms_back(grad_normed, normed, inverse):
    return inverse * (grad_normed - normed * jnp.mean(grad_normed * normed, -1, keepdims=True))


def on_device(tokens, conditions, cotangent, slot_mask, weight_flat, bias_flat):
    f32 = jnp.float32
    bf16 = jnp.bfloat16
    slots = conditions.shape[0]
    length = GRID * GRID
    rows_all = slots * length
    scale = 1.0 / math.sqrt(HEAD_DIM)
    heads_shape = (slots, length, HEADS, HEAD_DIM)
    weight_all, bias_all = (
        lax.all_gather(weight_flat, ("fsdp", "dp"), axis=0, tiled=True),
        lax.all_gather(bias_flat, ("fsdp", "dp"), axis=0, tiled=True),
    )
    (
        query_key_value_weight,
        projection_weight,
        feedforward_weight,
        w_ada,
        down_weight,
        query_key_value_bias,
        projection_bias,
        feedforward_bias,
        b_ada,
    ) = unpack_weights(weight_all, bias_all)
    cosines, sines = rope_tables()
    mask_f = slot_mask.astype(f32)[:, None, None]
    x_f = tokens.astype(f32).reshape(slots, length, D)
    cond_f = conditions.astype(f32)
    cond_act = jax.nn.silu(cond_f).astype(bf16)
    modulation = jnp.dot(cond_act, w_ada, preferred_element_type=f32) + b_ada.astype(f32)
    shift_a, scale_a, gate_a, shift_b, scale_b, gate_b = [
        modulation[:, None, place * D : (place + 1) * D] for place in range(6)
    ]
    normed_a, inv_a = norm_parts(x_f)
    attention_input = (normed_a * (1.0 + scale_a) + shift_a).astype(bf16).reshape(rows_all, D)
    projected_output = (
        jnp.dot(attention_input, query_key_value_weight, preferred_element_type=f32)
        + query_key_value_bias.astype(f32)
    ).reshape(slots, length, 3 * D)
    q_norm, inv_q = rms_parts(projected_output[..., :D].reshape(heads_shape))
    k_norm, inv_k = rms_parts(projected_output[..., D : 2 * D].reshape(heads_shape))
    queries = (q_norm * cosines + turn_half(q_norm) * sines).astype(bf16)
    keys = (k_norm * cosines + turn_half(k_norm) * sines).astype(bf16)
    values = projected_output[..., 2 * D :].reshape(heads_shape).astype(bf16)
    scores = jnp.einsum("slhe,smhe->shlm", queries, keys, preferred_element_type=f32) * scale
    row_max = jnp.max(scores, -1, keepdims=True)
    log_total = row_max + jnp.log(jnp.sum(jnp.exp(scores - row_max), -1, keepdims=True))
    probs_low = jnp.exp(scores - log_total).astype(bf16)
    attention_output = (
        jnp.einsum("shlm,smhe->slhe", probs_low, values, preferred_element_type=f32)
        .astype(bf16)
        .reshape(rows_all, D)
    )
    attention_branch = (
        jnp.dot(attention_output, projection_weight, preferred_element_type=f32)
        + projection_bias.astype(f32)
    ).reshape(slots, length, D)
    middle = x_f + gate_a * attention_branch
    normed_b, inv_b = norm_parts(middle)
    feedforward_input = (normed_b * (1.0 + scale_b) + shift_b).astype(bf16).reshape(rows_all, D)
    mixed_tokens = jnp.dot(
        feedforward_input, feedforward_weight, preferred_element_type=f32
    ) + feedforward_bias.astype(f32)
    gate_part = mixed_tokens[:, :FF]
    up_part = mixed_tokens[:, FF:]
    hidden_state = (jax.nn.silu(gate_part) * up_part).astype(bf16)
    feedforward_branch = jnp.dot(hidden_state, down_weight, preferred_element_type=f32).reshape(
        slots, length, D
    )
    out = ((middle + gate_b * feedforward_branch) * mask_f).astype(bf16).reshape(rows_all, D)
    weight_all, bias_all = (
        lax.all_gather(weight_flat, ("fsdp", "dp"), axis=0, tiled=True),
        lax.all_gather(bias_flat, ("fsdp", "dp"), axis=0, tiled=True),
    )
    (
        query_key_value_weight,
        projection_weight,
        feedforward_weight,
        w_ada,
        down_weight,
        query_key_value_bias,
        projection_bias,
        feedforward_bias,
        b_ada,
    ) = unpack_weights(weight_all, bias_all)
    g_out = cotangent.astype(f32).reshape(slots, length, D) * mask_f
    g_branch_b = (gate_b * g_out).astype(bf16).reshape(rows_all, D)
    g_gate_b = jnp.sum(g_out * feedforward_branch, axis=1)
    grad_down = jnp.einsum("rf,rd->fd", hidden_state, g_branch_b, preferred_element_type=f32)
    g_hidden = jnp.einsum("rd,fd->rf", g_branch_b, down_weight, preferred_element_type=f32)
    sigma_gate = jax.nn.sigmoid(gate_part)
    g_mixed = jnp.concatenate(
        [
            g_hidden * up_part * sigma_gate * (1.0 + gate_part * (1.0 - sigma_gate)),
            g_hidden * (gate_part * sigma_gate),
        ],
        axis=1,
    ).astype(bf16)
    grad_mlp = jnp.einsum("rd,rf->df", feedforward_input, g_mixed, preferred_element_type=f32)
    grad_b_mlp = jnp.sum(g_mixed.astype(f32), axis=0)
    g_input_b = jnp.einsum(
        "rf,df->rd", g_mixed, feedforward_weight, preferred_element_type=f32
    ).reshape(slots, length, D)
    g_shift_b = jnp.sum(g_input_b, axis=1)
    g_scale_b = jnp.sum(g_input_b * normed_b, axis=1)
    g_middle = g_out + norm_back(g_input_b * (1.0 + scale_b), normed_b, inv_b)
    g_branch_a = (gate_a * g_middle).astype(bf16).reshape(rows_all, D)
    g_gate_a = jnp.sum(g_middle * attention_branch, axis=1)
    grad_w_out = jnp.einsum("rd,re->de", attention_output, g_branch_a, preferred_element_type=f32)
    grad_b_out = jnp.sum(g_branch_a.astype(f32), axis=0)
    g_attended = (
        jnp.einsum("re,de->rd", g_branch_a, projection_weight, preferred_element_type=f32)
        .astype(bf16)
        .reshape(heads_shape)
    )
    scores = jnp.einsum("slhe,smhe->shlm", queries, keys, preferred_element_type=f32) * scale
    probs = jnp.exp(scores - log_total)
    probs_low = probs.astype(bf16)
    g_probs = jnp.einsum("slhe,smhe->shlm", g_attended, values, preferred_element_type=f32)
    g_values = jnp.einsum("shlm,slhe->smhe", probs_low, g_attended, preferred_element_type=f32)
    g_scores = (probs * (g_probs - jnp.sum(probs * g_probs, -1, keepdims=True))).astype(bf16)
    g_queries = jnp.einsum("shlm,smhe->slhe", g_scores, keys, preferred_element_type=f32) * scale
    g_keys = jnp.einsum("shlm,slhe->smhe", g_scores, queries, preferred_element_type=f32) * scale
    g_q = rms_back(g_queries * cosines - turn_half(g_queries) * sines, q_norm, inv_q)
    g_k = rms_back(g_keys * cosines - turn_half(g_keys) * sines, k_norm, inv_k)
    g_projected = jnp.concatenate(
        [g_q.reshape(rows_all, D), g_k.reshape(rows_all, D), g_values.reshape(rows_all, D)], axis=1
    ).astype(bf16)
    grad_qkv = jnp.einsum("rd,re->de", attention_input, g_projected, preferred_element_type=f32)
    grad_b_qkv = jnp.sum(g_projected.astype(f32), axis=0)
    g_input_a = jnp.einsum(
        "re,de->rd", g_projected, query_key_value_weight, preferred_element_type=f32
    ).reshape(slots, length, D)
    g_shift_a = jnp.sum(g_input_a, axis=1)
    g_scale_a = jnp.sum(g_input_a * normed_a, axis=1)
    grad_tokens = g_middle + norm_back(g_input_a * (1.0 + scale_a), normed_a, inv_a)
    g_modulation = jnp.concatenate(
        [g_shift_a, g_scale_a, g_gate_a, g_shift_b, g_scale_b, g_gate_b], axis=1
    ).astype(bf16)
    grad_ada = jnp.einsum("sd,se->de", cond_act, g_modulation, preferred_element_type=f32)
    grad_b_ada = jnp.sum(g_modulation.astype(f32), axis=0)
    g_cond = jnp.einsum("se,de->sd", g_modulation, w_ada, preferred_element_type=f32)
    sigma_cond = jax.nn.sigmoid(cond_f)
    grad_conditions = g_cond * sigma_cond * (1.0 + cond_f * (1.0 - sigma_cond))
    grads_big = jnp.concatenate(
        [
            grad_qkv.astype(bf16).reshape(-1),
            grad_w_out.astype(bf16).reshape(-1),
            grad_mlp.astype(bf16).reshape(-1),
            grad_ada.astype(bf16).reshape(-1),
            grad_down.astype(bf16).reshape(-1),
        ]
    ).reshape(-1, 128)
    grads_small = jnp.concatenate([grad_b_qkv, grad_b_out, grad_b_mlp, grad_b_ada])
    part_weights = lax.psum_scatter(
        grads_big, ("fsdp", "dp"), scatter_dimension=0, tiled=True
    ).astype(f32)
    part_biases = lax.psum_scatter(
        grads_small, ("fsdp", "dp"), scatter_dimension=0, tiled=True
    )
    return (out, grad_tokens.reshape(rows_all, D), grad_conditions, part_weights, part_biases)


def solution(mesh):
    return jax.shard_map(
        on_device,
        mesh=mesh,
        in_specs=(
            P(("fsdp", "dp"), None),
            P(("fsdp", "dp"), None),
            P(("fsdp", "dp"), None),
            P(("fsdp", "dp")),
            P(("fsdp", "dp"), None),
            P(("fsdp", "dp")),
        ),
        out_specs=(
            P(("fsdp", "dp"), None),
            P(("fsdp", "dp"), None),
            P(("fsdp", "dp"), None),
            P(("fsdp", "dp"), None),
            P(("fsdp", "dp")),
        ),
        check_vma=False,
    )
```

```python
import math

import jax
import jax.numpy as jnp
from jax import lax
from jax.experimental import pallas as pl
from jax.experimental.pallas import tpu as pltpu
import numpy as np
from jax.sharding import PartitionSpec as P

D = 1152
HEADS = 16
HEAD_DIM = 72
FF = 3072
GRID = 16


eps_norm = 1e-06


def unpack_weights(weight_all, bias_all):
    flat = weight_all.reshape(-1)
    layouts = ((D, 3 * D), (D, D), (D, 2 * FF), (D, 6 * D), (FF, D))
    pieces = []
    offset = 0
    for layout in layouts:
        amount = layout[0] * layout[1]
        pieces.append(flat[offset : offset + amount].reshape(layout))
        offset = offset + amount
    offset = 0
    for amount in (3 * D, D, 2 * FF, 6 * D):
        pieces.append(bias_all[offset : offset + amount])
        offset = offset + amount
    return tuple(pieces)


def rope_tables():
    quarter = HEAD_DIM // 4
    places = jnp.arange(GRID * GRID, dtype=jnp.int32)
    rows_at = (places // GRID).astype(jnp.float32)
    cols_at = (places % GRID).astype(jnp.float32)
    freqs = 10000.0 ** (-jnp.arange(quarter, dtype=jnp.float32) / quarter)
    along_rows = rows_at[:, None] * freqs[None, :]
    along_cols = cols_at[:, None] * freqs[None, :]
    angles = jnp.concatenate([along_rows, along_rows, along_cols, along_cols], axis=1)
    return (jnp.cos(angles)[:, None, :], jnp.sin(angles)[:, None, :])


def turn_half(values):
    quarter = values.shape[-1] // 4
    first = values[..., :quarter]
    second = values[..., quarter : 2 * quarter]
    third = values[..., 2 * quarter : 3 * quarter]
    fourth = values[..., 3 * quarter :]
    return jnp.concatenate([-second, first, -fourth, third], axis=-1)


def norm_parts(values):
    centred = values - jnp.mean(values, -1, keepdims=True)
    inverse = lax.rsqrt(jnp.mean(centred * centred, -1, keepdims=True) + eps_norm)
    return (centred * inverse, inverse)


def norm_back(grad_normed, normed, inverse):
    return inverse * (
        grad_normed
        - jnp.mean(grad_normed, -1, keepdims=True)
        - normed * jnp.mean(grad_normed * normed, -1, keepdims=True)
    )


def rms_parts(values):
    inverse = lax.rsqrt(jnp.mean(values * values, -1, keepdims=True) + eps_norm)
    return (values * inverse, inverse)


def rms_back(grad_normed, normed, inverse):
    return inverse * (grad_normed - normed * jnp.mean(grad_normed * normed, -1, keepdims=True))


def compute_block(tokens, cotangent, slot_mask, modulation, weights, biases):
    f32 = jnp.float32
    bf16 = jnp.bfloat16
    w_qkv, w_out, w_mlp, w_down = weights
    b_qkv, b_out, b_mlp = biases
    slots = slot_mask.shape[0]
    length = GRID * GRID
    rows_all = slots * length
    scale = 1.0 / math.sqrt(HEAD_DIM)
    heads_shape = (slots, length, HEADS, HEAD_DIM)
    cosines, sines = rope_tables()
    mask_f = slot_mask.astype(f32)[:, None, None]
    x_f = tokens.astype(f32).reshape(slots, length, D)
    shift_a, scale_a, gate_a, shift_b, scale_b, gate_b = [
        modulation[:, None, place * D : (place + 1) * D] for place in range(6)
    ]
    normed_a, inv_a = norm_parts(x_f)
    attention_input = (normed_a * (1.0 + scale_a) + shift_a).astype(bf16).reshape(rows_all, D)
    projected_output = (
        jnp.dot(attention_input, w_qkv, preferred_element_type=f32) + b_qkv.astype(f32)
    ).reshape(slots, length, 3 * D)
    q_norm, inv_q = rms_parts(projected_output[..., :D].reshape(heads_shape))
    k_norm, inv_k = rms_parts(projected_output[..., D : 2 * D].reshape(heads_shape))
    queries = (q_norm * cosines + turn_half(q_norm) * sines).astype(bf16)
    keys = (k_norm * cosines + turn_half(k_norm) * sines).astype(bf16)
    values = projected_output[..., 2 * D :].reshape(heads_shape).astype(bf16)
    scores = jnp.einsum("slhe,smhe->shlm", queries, keys, preferred_element_type=f32) * scale
    row_max = jnp.max(scores, -1, keepdims=True)
    log_total = row_max + jnp.log(jnp.sum(jnp.exp(scores - row_max), -1, keepdims=True))
    probs_low = jnp.exp(scores - log_total).astype(bf16)
    attention_output = (
        jnp.einsum("shlm,smhe->slhe", probs_low, values, preferred_element_type=f32)
        .astype(bf16)
        .reshape(rows_all, D)
    )
    attention_branch = (
        jnp.dot(attention_output, w_out, preferred_element_type=f32) + b_out.astype(f32)
    ).reshape(slots, length, D)
    middle = x_f + gate_a * attention_branch
    normed_b, inv_b = norm_parts(middle)
    feedforward_input = (normed_b * (1.0 + scale_b) + shift_b).astype(bf16).reshape(rows_all, D)
    mixed_tokens = jnp.dot(feedforward_input, w_mlp, preferred_element_type=f32) + b_mlp.astype(
        f32
    )
    gate_part = mixed_tokens[:, :FF]
    up_part = mixed_tokens[:, FF:]
    hidden_state = (jax.nn.silu(gate_part) * up_part).astype(bf16)
    feedforward_branch = jnp.dot(hidden_state, w_down, preferred_element_type=f32).reshape(
        slots, length, D
    )
    out = ((middle + gate_b * feedforward_branch) * mask_f).astype(bf16).reshape(rows_all, D)
    g_out = cotangent.astype(f32).reshape(slots, length, D) * mask_f
    g_branch_b = (gate_b * g_out).astype(bf16).reshape(rows_all, D)
    g_gate_b = jnp.sum(g_out * feedforward_branch, axis=1)
    g_hidden = jnp.einsum("rd,fd->rf", g_branch_b, w_down, preferred_element_type=f32)
    sigma_gate = jax.nn.sigmoid(gate_part)
    g_mixed = jnp.concatenate(
        [
            g_hidden * up_part * sigma_gate * (1.0 + gate_part * (1.0 - sigma_gate)),
            g_hidden * (gate_part * sigma_gate),
        ],
        axis=1,
    ).astype(bf16)
    grad_b_mlp = jnp.sum(g_mixed.astype(f32), axis=0)
    g_input_b = jnp.einsum("rf,df->rd", g_mixed, w_mlp, preferred_element_type=f32).reshape(
        slots, length, D
    )
    g_shift_b = jnp.sum(g_input_b, axis=1)
    g_scale_b = jnp.sum(g_input_b * normed_b, axis=1)
    g_middle = g_out + norm_back(g_input_b * (1.0 + scale_b), normed_b, inv_b)
    g_branch_a = (gate_a * g_middle).astype(bf16).reshape(rows_all, D)
    g_gate_a = jnp.sum(g_middle * attention_branch, axis=1)
    grad_b_out = jnp.sum(g_branch_a.astype(f32), axis=0)
    g_attended = (
        jnp.einsum("re,de->rd", g_branch_a, w_out, preferred_element_type=f32)
        .astype(bf16)
        .reshape(heads_shape)
    )
    scores = jnp.einsum("slhe,smhe->shlm", queries, keys, preferred_element_type=f32) * scale
    probs = jnp.exp(scores - log_total)
    probs_low = probs.astype(bf16)
    g_probs = jnp.einsum("slhe,smhe->shlm", g_attended, values, preferred_element_type=f32)
    g_values = jnp.einsum("shlm,slhe->smhe", probs_low, g_attended, preferred_element_type=f32)
    g_scores = (probs * (g_probs - jnp.sum(probs * g_probs, -1, keepdims=True))).astype(bf16)
    g_queries = jnp.einsum("shlm,smhe->slhe", g_scores, keys, preferred_element_type=f32) * scale
    g_keys = jnp.einsum("shlm,slhe->smhe", g_scores, queries, preferred_element_type=f32) * scale
    g_q = rms_back(g_queries * cosines - turn_half(g_queries) * sines, q_norm, inv_q)
    g_k = rms_back(g_keys * cosines - turn_half(g_keys) * sines, k_norm, inv_k)
    g_projected = jnp.concatenate(
        [g_q.reshape(rows_all, D), g_k.reshape(rows_all, D), g_values.reshape(rows_all, D)], axis=1
    ).astype(bf16)
    grad_b_qkv = jnp.sum(g_projected.astype(f32), axis=0)
    g_input_a = jnp.einsum("re,de->rd", g_projected, w_qkv, preferred_element_type=f32).reshape(
        slots, length, D
    )
    g_shift_a = jnp.sum(g_input_a, axis=1)
    g_scale_a = jnp.sum(g_input_a * normed_a, axis=1)
    grad_tokens = g_middle + norm_back(g_input_a * (1.0 + scale_a), normed_a, inv_a)
    g_modulation = jnp.concatenate(
        [g_shift_a, g_scale_a, g_gate_a, g_shift_b, g_scale_b, g_gate_b], axis=1
    ).astype(bf16)
    pairs = (
        (attention_input, g_projected),
        (attention_output, g_branch_a),
        (feedforward_input, g_mixed),
        (hidden_state, g_branch_b),
    )
    return (
        out,
        grad_tokens.reshape(rows_all, D),
        g_modulation,
        (grad_b_qkv, grad_b_out, grad_b_mlp),
        pairs,
    )


def weight_grad(pair):
    return jnp.einsum("rd,re->de", pair[0], pair[1], preferred_element_type=jnp.float32)


def on_device_plain(tokens, conditions, cotangent, slot_mask, weight_flat, bias_flat):
    f32 = jnp.float32
    bf16 = jnp.bfloat16
    axes = ("fsdp", "dp")
    weight_all = lax.all_gather(weight_flat, axes, axis=0, tiled=True)
    bias_all = lax.all_gather(bias_flat, axes, axis=0, tiled=True)
    w_qkv, w_out, w_mlp, w_ada, w_down, b_qkv, b_out, b_mlp, b_ada = unpack_weights(
        weight_all, bias_all
    )
    cond_f = conditions.astype(f32)
    cond_act = jax.nn.silu(cond_f).astype(bf16)
    modulation = jnp.dot(cond_act, w_ada, preferred_element_type=f32) + b_ada.astype(f32)
    out, grad_tokens, g_modulation, bias_sums, pairs = compute_block(
        tokens,
        cotangent,
        slot_mask,
        modulation,
        (w_qkv, w_out, w_mlp, w_down),
        (b_qkv, b_out, b_mlp),
    )
    grad_b_ada = jnp.sum(g_modulation.astype(f32), axis=0)
    g_cond = jnp.einsum("se,de->sd", g_modulation, w_ada, preferred_element_type=f32)
    sigma_cond = jax.nn.sigmoid(cond_f)
    grad_conditions = g_cond * sigma_cond * (1.0 + cond_f * (1.0 - sigma_cond))
    grad_qkv, grad_out, grad_mlp, grad_down = [weight_grad(pair) for pair in pairs]
    grad_ada = weight_grad((cond_act, g_modulation))
    grads_big = jnp.concatenate(
        [
            grad.astype(bf16).reshape(-1)
            for grad in (grad_qkv, grad_out, grad_mlp, grad_ada, grad_down)
        ]
    ).reshape(-1, 128)
    grads_small = jnp.concatenate([*bias_sums, grad_b_ada])
    part_weights = lax.psum_scatter(grads_big, axes, scatter_dimension=0, tiled=True)
    part_biases = lax.psum_scatter(grads_small, axes, scatter_dimension=0, tiled=True)
    return (out, grad_tokens, grad_conditions, part_weights.astype(f32), part_biases)


ROWS_QKV = 3 * D * D // 128
ROWS_OUT = D * D // 128
ROWS_MLP = 2 * D * FF // 128
ROWS_ADA = 6 * D * D // 128
ROWS_DOWN = D * FF // 128
FIRST_MLP = ROWS_QKV + ROWS_OUT
FIRST_ADA = FIRST_MLP + ROWS_MLP
FIRST_DOWN = FIRST_ADA + ROWS_ADA
DEVICES = 32
SHARD = 5832
BLOCK_A = 1296
BLOCK_B = 2688
USED_DOWN = 2592
MLP_BLOCKS = 21
QKV_BLOCKS = 24
ADA_ROWS = SHARD * 128 // (6 * D)


def block_a_range(block):
    return (BLOCK_A * block, BLOCK_A * (block + 1))


def block_b_range(block):
    if block < MLP_BLOCKS:
        first = FIRST_MLP + BLOCK_B * block
        return (first, min(first + BLOCK_B, FIRST_ADA))
    first = FIRST_DOWN + USED_DOWN * (block - MLP_BLOCKS)
    return (first, min(first + USED_DOWN, FIRST_DOWN + ROWS_DOWN))


def colour_edges(edges):
    degree = {}
    for left, right in edges:
        degree["l", left] = degree.get(("l", left), 0) + 1
        degree["r", right] = degree.get(("r", right), 0) + 1
    count = max(degree.values())
    at = {}
    for left, right in edges:
        a, b = ("l", left), ("r", right)
        free_a = next(c for c in range(count) if (a, c) not in at)
        free_b = next(c for c in range(count) if (b, c) not in at)
        if free_a != free_b:
            path, node, colour = [], b, free_a
            while (node, colour) in at:
                other = at[node, colour]
                path.append((node, other, colour))
                node, colour = other, free_a + free_b - colour
            for one, two, old in path:
                del at[one, old], at[two, old]
            for one, two, old in path:
                new = free_a + free_b - old
                at[one, new], at[two, new] = two, one
        at[a, free_a], at[b, free_a] = b, a
    rounds = [[] for _ in range(count)]
    for (node, colour), other in at.items():
        if node[0] == "l":
            rounds[colour].append((node[1], other[1]))
    return [sorted(group) for group in rounds]


def plan_rounds(block_range, device_of_block):
    edges, first_row = [], {}
    for block in range(DEVICES):
        first, last = block_range(block)
        for owner in range(first // SHARD, (last - 1) // SHARD + 1):
            edges.append((owner, device_of_block(block)))
            first_row[owner, device_of_block(block)] = first - owner * SHARD
    rounds = colour_edges(edges)
    return rounds, first_row


def device_index():
    return lax.axis_index("fsdp") * lax.axis_size("dp") + lax.axis_index("dp")


def spread(shard, block_rows, block_range):
    me = device_index()
    rounds, first_row = plan_rounds(block_range, lambda block: block)
    padded = jnp.pad(shard, ((block_rows, block_rows), (0, 0)))
    total = None
    for pairs in rounds:
        starts = np.zeros(DEVICES, np.int32)
        for owner, device in pairs:
            starts[owner] = block_rows + first_row[owner, device]
        piece = lax.dynamic_slice_in_dim(padded, jnp.asarray(starts)[me], block_rows, 0)
        got = lax.ppermute(piece, ("fsdp", "dp"), pairs)
        total = got if total is None else total + got
    return total


def collect(buffer, block, block_rows, block_range, places):
    me = device_index()
    rounds, first_row = plan_rounds(block_range, lambda block: device_of(places, block))
    for pairs in rounds:
        starts = np.zeros(DEVICES, np.int32)
        for owner, device in pairs:
            starts[owner] = BLOCK_B + first_row[owner, device]
        got = lax.ppermute(block, ("fsdp", "dp"), [(device, owner) for owner, device in pairs])
        start = jnp.asarray(starts)[me]
        held = lax.dynamic_slice_in_dim(buffer, start, block_rows, 0)
        buffer = lax.dynamic_update_slice_in_dim(
            buffer, held + got.astype(buffer.dtype), start, 0
        )
    return buffer


def to_tiles(rows, chunks):
    return (
        rows.reshape(-1, 8, chunks, 128).transpose(0, 2, 1, 3).reshape(-1, 128)
    )


def from_tiles(rows, chunks):
    return (
        rows.reshape(-1, chunks, 8, 128).transpose(0, 2, 1, 3).reshape(-1, 128)
    )


def matrix_of_tiles(rows, height, width):
    return (
        rows.reshape(height // 8, width // 128, 8, 128)
        .transpose(0, 2, 1, 3)
        .reshape(height, width)
    )


def tiles_of_matrix(matrix):
    height, width = matrix.shape
    return (
        matrix.reshape(height // 8, 8, width // 128, 128)
        .transpose(0, 2, 1, 3)
        .reshape(-1, 128)
    )


SWAP_X = [(0, 1), (1, 0), (2, 3), (3, 2)]
SWAP_Y = [(0, 2), (2, 0), (1, 3), (3, 1)]
SWAP_CORE = [(d, d ^ 1) for d in range(8)]


def along_z(pairs):
    return [(2 * a + e, 2 * b + e) for a, b in pairs for e in range(2)]


def chips_of(*lines):
    place = {}
    for z, line in enumerate(lines):
        for f, block in enumerate(line):
            place[block] = 4 * f + z
    return place


PLACE_A = (
    chips_of((0, 1, 2, 3), (4, 5, 6, 7), (18, 19, 20, 21), (22, 23, 16, 17)),
    chips_of((8, 9, 10, 11), (12, 13, 14, 15), (24, 25, 26, 27), (28, 29, 30, 31)),
)
PLACE_B = (
    chips_of((2, 3, 4, 5), (6, 7, 8, 9), (10, 11, 12, 13), (14, 0, 15, 1)),
    chips_of((20, 16, 17, 18), (21, 22, 23, 24), (25, 26, 27, 28), (29, 19, 30, 31)),
)


def device_of(places, block):
    core = 0 if block in places[0] else 1
    return 2 * places[core][block] + core


def kind_table(places, first_of_second):
    table = np.zeros(DEVICES, np.int32)
    for block in range(DEVICES):
        table[device_of(places, block)] = int(block >= first_of_second)
    return table


def add_low(a, b):
    return (a.astype(jnp.float32) + b.astype(jnp.float32)).astype(jnp.bfloat16)


def pick(array, index, axis):
    return lax.dynamic_index_in_dim(array, index, axis, keepdims=False)


def first_sends(grads, block_rows):
    f = lax.axis_index("fsdp")
    y, x = f // 2, f % 2
    a, b = [part.reshape(2, 2, 4, block_rows // 2, 128) for part in grads]
    return pick(a, 1 - y, 0), pick(b, 1 - x, 1)


def reduce_planes(grads, sends, block_rows):
    f = lax.axis_index("fsdp")
    y, x = f // 2, f % 2
    a, b = [part.reshape(2, 2, 4, block_rows // 2, 128) for part in grads]
    a = add_low(pick(a, y, 0), lax.ppermute(sends[0], "fsdp", SWAP_Y))
    b = add_low(pick(b, x, 1), lax.ppermute(sends[1], "fsdp", SWAP_X))
    a = add_low(pick(a, x, 0), lax.ppermute(pick(a, 1 - x, 0), "fsdp", SWAP_X))
    b = add_low(pick(b, y, 0), lax.ppermute(pick(b, 1 - y, 0), "fsdp", SWAP_Y))
    return jnp.concatenate([a, b], axis=1)


def reduce_line(planes):
    z = lax.axis_index("dp") // 2
    total = pick(planes, z, 0).astype(jnp.float32)
    for k in range(1, 4):
        swap = [(d, d ^ (2 * k)) for d in range(8)]
        total += lax.ppermute(pick(planes, z ^ k, 0), "dp", swap).astype(jnp.float32)
    return total


def gather_column(array):
    parts = [array] + [
        lax.ppermute(array, "dp", [(d, d ^ k) for d in range(8)]) for k in range(1, 8)
    ]
    return jnp.stack(parts)


def gather_columns(part):
    parts = [part] + [
        lax.ppermute(part, "fsdp", [(f, f ^ k) for f in range(4)]) for k in range(1, 4)
    ]
    return jnp.stack(parts).reshape(DEVICES, *part.shape[1:])


ADA_GROUPS = range(FIRST_ADA // (8 * SHARD), (FIRST_DOWN - 1) // (8 * SHARD) + 1)


def sum_to_owners(terms):
    def send(array, change, groups):
        pairs = [(8 * f + d, (8 * f + d) ^ change) for f in groups for d in range(8)]
        return lax.ppermute(array, ("fsdp", "dp"), pairs)

    terms = terms.reshape(4, 4, 2, *terms.shape[1:])
    terms = terms[:, :, 0] + send(terms[:, :, 1], 1, ADA_GROUPS)
    terms = terms[0] + sum(send(terms[k], 8 * k, ADA_GROUPS) for k in range(1, 4))
    return terms[0] + sum(send(terms[k], 2 * k, range(4)) for k in range(1, 4))


def exchange_relative(pieces):
    pieces = pieces.reshape(4, 8, *pieces.shape[1:])
    parts = [pieces[:, 0]] + [
        lax.ppermute(pieces[:, k], "dp", [(d, d ^ k) for d in range(8)]) for k in range(1, 8)
    ]
    part = jnp.stack(parts, axis=1)
    parts = [part[0]] + [
        lax.ppermute(part[k], "fsdp", [(f, f ^ k) for f in range(4)]) for k in range(1, 4)
    ]
    return jnp.stack(parts).reshape(DEVICES, *pieces.shape[2:])


def mlp_kernel(flat_first, blocks, used_tiles, block_tiles):
    def body(x_ref, g_ref, bias_g_ref, bias_u_ref, gate_w, up_w, flat_ref, *rest):
        hid_ref, gg_ref, gu_ref, branch_ref, gin_ref, sum_g_ref, sum_u_ref, down_ref, sem = rest
        f32, bf16 = jnp.float32, jnp.bfloat16
        step = pl.program_id(0)

        def copies():
            return [
                pltpu.make_async_copy(
                    flat_ref.at[pl.ds(flat_first + block_tiles * i, used_tiles)],
                    down_ref.at[pl.ds(used_tiles * i, used_tiles)],
                    sem.at[i],
                )
                for i in range(blocks)
            ]

        @pl.when(step == 0)
        def _():
            for copy in copies():
                copy.start()

        def columns(ref):
            return jnp.concatenate([ref[:, i].reshape(D, 128) for i in range(2)], axis=1)

        x = x_ref[...]
        w_gate, w_up = columns(gate_w), columns(up_w)
        gate = jnp.dot(x, w_gate, preferred_element_type=f32) + bias_g_ref[...]
        up = jnp.dot(x, w_up, preferred_element_type=f32) + bias_u_ref[...]
        sigma = jax.nn.sigmoid(gate)
        silu = gate * sigma
        hid = (silu * up).astype(bf16)
        hid_ref[...] = hid

        @pl.when(step == 0)
        def _():
            for copy in copies():
                copy.wait()
            branch_ref[...] = jnp.zeros_like(branch_ref)
            gin_ref[...] = jnp.zeros_like(gin_ref)

        chunks = D // 128
        rows = down_ref[pl.ds(step * 32 * chunks, 32 * chunks)].reshape(32, chunks, 8, 128)
        w_down = jnp.concatenate([rows[:, j].reshape(256, 128) for j in range(chunks)], axis=1)
        branch_ref[...] += jnp.dot(hid, w_down, preferred_element_type=f32)
        across = (((1,), (1,)), ((), ()))
        g_hid = lax.dot_general(g_ref[...], w_down, across, preferred_element_type=f32)
        g_gate = (g_hid * up * sigma * (1.0 + gate * (1.0 - sigma))).astype(bf16)
        g_up = (g_hid * silu).astype(bf16)
        gg_ref[...] = g_gate
        gu_ref[...] = g_up
        sum_g_ref[...] = jnp.sum(g_gate.astype(f32), axis=0, keepdims=True)
        sum_u_ref[...] = jnp.sum(g_up.astype(f32), axis=0, keepdims=True)
        gin_ref[...] += lax.dot_general(
            g_gate, w_gate, across, preferred_element_type=f32
        ) + lax.dot_general(g_up, w_up, across, preferred_element_type=f32)

    return body


def mlp_both_ways(x, g, bias, all_b):
    f32, bf16 = jnp.float32, jnp.bfloat16
    rows = x.shape[0]
    blocks = DEVICES - MLP_BLOCKS
    used = USED_DOWN // 8
    steps = FF // 256
    tiles = all_b.reshape(-1, 2 * FF // 128, 8, 128)
    whole = pl.BlockSpec((rows, D), lambda t: (0, 0))
    part = pl.BlockSpec((rows, 256), lambda t: (0, t))
    line = pl.BlockSpec((1, 256), lambda t: (0, t))
    return pl.pallas_call(
        mlp_kernel(MLP_BLOCKS * BLOCK_B // 8, blocks, used, BLOCK_B // 8),
        grid=(steps,),
        in_specs=[
            whole,
            whole,
            line,
            pl.BlockSpec((1, 256), lambda t: (0, steps + t)),
            pl.BlockSpec((D // 8, 2, 8, 128), lambda t: (0, t, 0, 0)),
            pl.BlockSpec((D // 8, 2, 8, 128), lambda t: (0, steps + t, 0, 0)),
            pl.BlockSpec(memory_space=pl.ANY),
        ],
        out_specs=[part, part, part, whole, whole, line, line],
        out_shape=[jax.ShapeDtypeStruct((rows, FF), bf16)] * 3
        + [jax.ShapeDtypeStruct((rows, D), f32)] * 2
        + [jax.ShapeDtypeStruct((1, FF), f32)] * 2,
        scratch_shapes=[
            pltpu.VMEM((blocks * used, 8, 128), bf16),
            pltpu.SemaphoreType.DMA((blocks,)),
        ],
        cost_estimate=pl.CostEstimate(
            flops=12 * rows * D * FF, bytes_accessed=30_000_000, transcendentals=rows * FF
        ),
        compiler_params=pltpu.CompilerParams(vmem_limit_bytes=56 << 20),
        name="mlp_both_ways",
    )(x, g, bias, bias, tiles, tiles, all_b.reshape(-1, 8, 128))


def pair_product(xo, xp, go, gp):
    down = (((0,), (0,)), ((), ()))
    total = lax.dot_general(xo[...], go[...], down, preferred_element_type=jnp.float32)
    total += lax.dot_general(xp[...], gp[...], down, preferred_element_type=jnp.float32)
    return total.astype(jnp.bfloat16)


def store_tiles(out_ref, lead, first, value):
    for j in range(value.shape[1] // 128):
        out_ref[(*lead, first + j)] = value[:, 128 * j : 128 * (j + 1)]


def grads_b_core_0(in_b, g_gate, g_up):
    def body(xo, xp, gog, gpg, gou, gpu, out_ref):
        for half, go, gp in ((0, gog, gpg), (1, gou, gpu)):
            value = pair_product(xo, xp, go, gp)
            for j in range(4):
                part = value[:, 128 * j : 128 * (j + 1)].reshape(16, 7, 8, 128)
                for block in range(16):
                    out_ref[half, PLACE_B[0][block], :, j] = part[block]

    rows = in_b[0].shape[0]
    high = 16 * 56
    x_spec = pl.BlockSpec((rows, high), lambda t: (0, 0))
    g_spec = pl.BlockSpec((rows, 512), lambda t: (0, t))
    out = pl.pallas_call(
        body,
        grid=(FF // 512,),
        in_specs=[x_spec] * 2 + [g_spec] * 4,
        out_specs=pl.BlockSpec((2, 16, 7, 4, 8, 128), lambda t: (0, 0, 0, t, 0, 0)),
        out_shape=jax.ShapeDtypeStruct((2, 16, 7, FF // 128, 8, 128), jnp.bfloat16),
        compiler_params=pltpu.CompilerParams(vmem_limit_bytes=56 << 20),
        name="grads_b_core_0",
    )(*in_b, *g_gate, *g_up)
    return out.reshape(2, -1, 128)


def grads_b_core_1(in_b, g_gate, g_up, hidden, g_branch):
    bf16 = jnp.bfloat16
    rows = in_b[0].shape[0]
    mlp_steps = FF // 512
    wide = 384
    down_steps = FF // wide
    half_tiles = BLOCK_B // 16
    mlp_groups = (D - 16 * 56) // 8
    groups = (MLP_BLOCKS - 16) * 7
    half_groups = USED_DOWN // 9 // 16
    down_blocks = DEVICES - MLP_BLOCKS

    place = PLACE_B[1]

    def body(place_ref, xo, xp, gog, gpg, gou, gpu, ho, hp, go, gp, out_ref):
        step = pl.program_id(0)

        @pl.when(step == 0)
        def _():
            for group in range(mlp_groups, groups):
                first = place[16 + group // 7] * half_tiles + group % 7 * (FF // 128)
                for half in range(2):
                    out_ref[half, pl.ds(first, FF // 128)] = jnp.zeros((FF // 128, 8, 128), bf16)
            for block in range(down_blocks):
                for half in range(2):
                    used = min(half_groups, FF // 8 - (2 * block + half) * half_groups) * 9
                    first = place[MLP_BLOCKS + block] * half_tiles + used
                    rest = half_tiles - used
                    out_ref[half, pl.ds(first, rest)] = jnp.zeros((rest, 8, 128), bf16)

        @pl.when(step < mlp_steps)
        def _():
            for half, g_own, g_par in ((0, gog, gpg), (1, gou, gpu)):
                value = pair_product(xo, xp, g_own, g_par)
                skip = value.shape[0] - mlp_groups * 8
                for group in range(mlp_groups):
                    first = place[16 + group // 7] * half_tiles + group % 7 * (FF // 128)
                    store_tiles(
                        out_ref,
                        (half,),
                        first + step * 4,
                        value[skip + 8 * group : skip + 8 * group + 8],
                    )

        @pl.when(step >= mlp_steps)
        def _():
            value = pair_product(ho, hp, go, gp)
            for group in range(wide // 8):
                at = (step - mlp_steps) * (wide // 8) + group
                part = at // half_groups
                first = place_ref[part // 2] * half_tiles + (at % half_groups) * 9
                store_tiles(out_ref, (part % 2,), first, value[8 * group : 8 * group + 8])

    x_spec = pl.BlockSpec((rows, 384), lambda t: (0, 2))
    g_spec = pl.BlockSpec((rows, 512), lambda t: (0, jnp.minimum(t, mlp_steps - 1)))
    h_spec = pl.BlockSpec((rows, wide), lambda t: (0, jnp.maximum(t - mlp_steps, 0)))
    b_spec = pl.BlockSpec((rows, D), lambda t: (0, 0))
    shape = (2, 16 * half_tiles, 8, 128)
    down_place = jnp.asarray([place[MLP_BLOCKS + i] for i in range(down_blocks)], jnp.int32)
    out = pl.pallas_call(
        body,
        grid=(mlp_steps + down_steps,),
        in_specs=[pl.BlockSpec(memory_space=pltpu.SMEM)]
        + [x_spec] * 2
        + [g_spec] * 4
        + [h_spec] * 2
        + [b_spec] * 2,
        out_specs=pl.BlockSpec(shape, lambda t: (0, 0, 0, 0)),
        out_shape=jax.ShapeDtypeStruct(shape, bf16),
        compiler_params=pltpu.CompilerParams(vmem_limit_bytes=56 << 20),
        name="grads_b_core_1",
    )(down_place, *in_b, *g_gate, *g_up, *hidden, *g_branch)
    return out.reshape(2, -1, 128)


def grads_a(core, in_a, g_proj, att, g_branch):
    rows = in_a[0].shape[0]
    steps = 3 * D // 384
    place = PLACE_A[core]

    def store_qkv(value, first_block, step, out_ref):
        for group in range(48):
            block, half, low = first_block + group // 6, group // 3 % 2, group % 3
            store_tiles(
                out_ref,
                (half, place[block]),
                low * 27 + step * 3,
                value[8 * group : 8 * group + 8],
            )

    def body(xo, xp, go, gp, zo, zp, bo, bp, out_ref):
        step = pl.program_id(0)

        @pl.when(step < steps)
        def _():
            store_qkv(pair_product(xo, xp, go, gp), 8 * core, step, out_ref)
            if core == 0:
                store_qkv(pair_product(zo, zp, go, gp), 16, step, out_ref)

        if core == 1:

            @pl.when(step >= steps)
            def _():
                value = pair_product(zo, zp, bo, bp)
                for group in range(144):
                    block, half, low = QKV_BLOCKS + group // 18, group // 9 % 2, group % 9
                    store_tiles(
                        out_ref,
                        (half, place[block]),
                        low * 9 + (step - steps) * 3,
                        value[8 * group : 8 * group + 8],
                    )

    x_spec = pl.BlockSpec((rows, 384), lambda t: (0, core))
    g_spec = pl.BlockSpec((rows, 384), lambda t: (0, jnp.minimum(t, steps - 1)))
    if core == 0:
        z_spec, z = pl.BlockSpec((rows, 384), lambda t: (0, 2)), in_a
        b_spec, count = pl.BlockSpec((rows, 384), lambda t: (0, 0)), steps
    else:
        z_spec, z = pl.BlockSpec((rows, D), lambda t: (0, 0)), att
        b_spec = pl.BlockSpec((rows, 384), lambda t: (0, jnp.maximum(t - steps, 0)))
        count = steps + D // 384
    shape = (2, 16, 81, 8, 128)
    out = pl.pallas_call(
        body,
        grid=(count,),
        in_specs=[x_spec] * 2 + [g_spec] * 2 + [z_spec] * 2 + [b_spec] * 2,
        out_specs=pl.BlockSpec(shape, lambda t: (0, 0, 0, 0, 0)),
        out_shape=jax.ShapeDtypeStruct(shape, jnp.bfloat16),
        compiler_params=pltpu.CompilerParams(vmem_limit_bytes=56 << 20),
        name=f"grads_a_core_{core}",
    )(*in_a, *g_proj, *z, *g_branch)
    return out.reshape(2, -1, 128)


def gathered_weights(flat_a, flat_b):
    axes = ("fsdp", "dp")
    me = device_index()
    block_a = spread(flat_a, BLOCK_A, block_a_range)
    block_a = jnp.where(me < QKV_BLOCKS, to_tiles(block_a, 27), to_tiles(block_a, 9))
    all_a = lax.all_gather(block_a, axes, axis=0, tiled=True)
    block_b = spread(flat_b, BLOCK_B, block_b_range)
    block_b = jnp.where(
        me < MLP_BLOCKS,
        to_tiles(block_b, 48),
        jnp.pad(to_tiles(block_b[:USED_DOWN], 9), ((0, BLOCK_B - USED_DOWN), (0, 0))),
    )
    all_b = lax.all_gather(block_b, axes, axis=0, tiled=True)
    return all_a, all_b


def on_device_32(tokens, conditions, cotangent, slot_mask, weight_flat, bias_flat):
    f32 = jnp.float32
    bf16 = jnp.bfloat16
    axes = ("fsdp", "dp")
    me = device_index()
    core = lax.axis_index("dp") % 2
    slots = conditions.shape[0]
    images = slots * DEVICES
    length = GRID * GRID
    rows_all = slots * length
    scale = 1.0 / math.sqrt(HEAD_DIM)
    heads_shape = (slots, length, HEADS, HEAD_DIM)
    cond_count = slots * D
    bias_count = bias_flat.shape[0]
    packed_rows = -(-(cond_count + bias_count) // 128)
    packed = jnp.concatenate(
        [
            conditions.reshape(-1),
            bias_flat,
            jnp.zeros(packed_rows * 128 - cond_count - bias_count, bf16),
        ]
    ).reshape(packed_rows, 128)
    column, flat_a = lax.optimization_barrier((gather_column(packed), weight_flat))
    packed_all = gather_columns(column).reshape(DEVICES, -1)
    cond_all = packed_all[:, :cond_count].reshape(images, D).astype(f32)
    places = lax.broadcasted_iota(jnp.int32, (DEVICES, DEVICES), 0)
    others = lax.broadcasted_iota(jnp.int32, (DEVICES, DEVICES), 1)
    chosen = ((places ^ me) == others).astype(bf16)
    bias_all = jnp.dot(
        chosen, packed_all[:, cond_count : cond_count + bias_count], preferred_element_type=f32
    ).reshape(-1)
    b_qkv = bias_all[: 3 * D]
    b_out = bias_all[3 * D : 4 * D]
    b_mlp = bias_all[4 * D : 4 * D + 2 * FF]
    b_ada = bias_all[4 * D + 2 * FF :]
    ada_local = weight_flat.reshape(ADA_ROWS, 6 * D)
    ada_start = jnp.clip(
        me * ADA_ROWS - FIRST_ADA * 128 // (6 * D) + ADA_ROWS, 0, D + ADA_ROWS
    )
    cond_act = jax.nn.silu(cond_all).astype(bf16)
    cond_rows = lax.dynamic_slice_in_dim(
        jnp.pad(cond_act.T, ((ADA_ROWS, ADA_ROWS), (0, 0))), ada_start, ADA_ROWS, 0
    )
    terms = jnp.einsum("km,kn->mn", cond_rows, ada_local, preferred_element_type=f32)
    modulation = sum_to_owners(terms.reshape(DEVICES, slots, 6 * D)) + b_ada
    all_a, all_b = gathered_weights(flat_a, flat_a)
    w_qkv = matrix_of_tiles(all_a[:ROWS_QKV], D, 3 * D)
    w_out = matrix_of_tiles(all_a[ROWS_QKV:], D, D)

    def share(array):
        return (array, lax.ppermute(array, "dp", SWAP_CORE))

    cosines, sines = rope_tables()
    mask_f = slot_mask.astype(f32)[:, None, None]
    x_f = tokens.astype(f32).reshape(slots, length, D)
    shift_a, scale_a, gate_a, shift_b, scale_b, gate_b = [
        modulation[:, None, place * D : (place + 1) * D] for place in range(6)
    ]
    g_out = cotangent.astype(f32).reshape(slots, length, D) * mask_f
    g_branch_b = (gate_b * g_out).astype(bf16).reshape(rows_all, D)
    normed_a, inv_a = norm_parts(x_f)
    input_a = (normed_a * (1.0 + scale_a) + shift_a).astype(bf16).reshape(rows_all, D)
    projected = (jnp.dot(input_a, w_qkv, preferred_element_type=f32) + b_qkv).reshape(
        slots, length, 3 * D
    )
    q_norm, inv_q = rms_parts(projected[..., :D].reshape(heads_shape))
    k_norm, inv_k = rms_parts(projected[..., D : 2 * D].reshape(heads_shape))
    queries = (q_norm * cosines + turn_half(q_norm) * sines).astype(bf16)
    keys = (k_norm * cosines + turn_half(k_norm) * sines).astype(bf16)
    values = projected[..., 2 * D :].reshape(heads_shape).astype(bf16)
    scores = jnp.einsum("slhe,smhe->shlm", queries, keys, preferred_element_type=f32) * scale
    row_max = jnp.max(scores, -1, keepdims=True)
    log_total = row_max + jnp.log(jnp.sum(jnp.exp(scores - row_max), -1, keepdims=True))
    probs_low = jnp.exp(scores - log_total).astype(bf16)
    attended = (
        jnp.einsum("shlm,smhe->slhe", probs_low, values, preferred_element_type=f32)
        .astype(bf16)
        .reshape(rows_all, D)
    )
    branch_a = (jnp.dot(attended, w_out, preferred_element_type=f32) + b_out).reshape(
        slots, length, D
    )
    middle = x_f + gate_a * branch_a
    normed_b, inv_b = norm_parts(middle)
    input_b = (normed_b * (1.0 + scale_b) + shift_b).astype(bf16).reshape(rows_all, D)
    early = [share(array) for array in (input_a, attended, input_b, g_branch_b)]
    hidden, g_gate, g_up, branch_b, g_input_b, sum_gate, sum_up = mlp_both_ways(
        input_b, g_branch_b, b_mlp.reshape(1, 2 * FF), all_b
    )
    shared_mlp = [share(array) for array in (g_gate, g_up, hidden)]
    grads_b = lax.cond(
        core == 0,
        lambda: grads_b_core_0(early[2], shared_mlp[0], shared_mlp[1]),
        lambda: grads_b_core_1(early[2], *shared_mlp, early[3]),
    )
    branch_b = branch_b.reshape(slots, length, D)
    g_input_b = g_input_b.reshape(slots, length, D)
    sends_b = first_sends(grads_b, BLOCK_B)
    out = ((middle + gate_b * branch_b) * mask_f).astype(bf16).reshape(rows_all, D)
    g_gate_b = jnp.sum(g_out * branch_b, axis=1)
    g_shift_b = jnp.sum(g_input_b, axis=1)
    g_scale_b = jnp.sum(g_input_b * normed_b, axis=1)
    g_middle = g_out + norm_back(g_input_b * (1.0 + scale_b), normed_b, inv_b)
    g_branch_a = (gate_a * g_middle).astype(bf16).reshape(rows_all, D)
    g_gate_a = jnp.sum(g_middle * branch_a, axis=1)
    grad_b_out = jnp.sum(g_branch_a.astype(f32), axis=0)
    shared_branch_a = share(g_branch_a)
    g_attended = (
        jnp.einsum("re,de->rd", g_branch_a, w_out, preferred_element_type=f32)
        .astype(bf16)
        .reshape(heads_shape)
    )
    g_attended, sends_b = lax.optimization_barrier((g_attended, sends_b))
    planes_b = reduce_planes(grads_b, sends_b, BLOCK_B)
    scores = jnp.einsum("slhe,smhe->shlm", queries, keys, preferred_element_type=f32) * scale
    probs = jnp.exp(scores - log_total)
    probs_low = probs.astype(bf16)
    g_probs = jnp.einsum("slhe,smhe->shlm", g_attended, values, preferred_element_type=f32)
    g_values = jnp.einsum("shlm,slhe->smhe", probs_low, g_attended, preferred_element_type=f32)
    g_scores = (probs * (g_probs - jnp.sum(probs * g_probs, -1, keepdims=True))).astype(bf16)
    g_queries = jnp.einsum("shlm,smhe->slhe", g_scores, keys, preferred_element_type=f32) * scale
    g_keys = jnp.einsum("shlm,slhe->smhe", g_scores, queries, preferred_element_type=f32) * scale
    g_q = rms_back(g_queries * cosines - turn_half(g_queries) * sines, q_norm, inv_q)
    g_k = rms_back(g_keys * cosines - turn_half(g_keys) * sines, k_norm, inv_k)
    g_projected = jnp.concatenate(
        [g_q.reshape(rows_all, D), g_k.reshape(rows_all, D), g_values.reshape(rows_all, D)], axis=1
    ).astype(bf16)
    grad_b_qkv = jnp.sum(g_projected.astype(f32), axis=0)
    shared_proj = share(g_projected)
    g_input_a = jnp.einsum("re,de->rd", g_projected, w_qkv, preferred_element_type=f32).reshape(
        slots, length, D
    )
    made_a = lax.cond(
        core == 0,
        lambda: grads_a(0, early[0], shared_proj, early[1], shared_branch_a),
        lambda: grads_a(1, early[0], shared_proj, early[1], shared_branch_a),
    )
    sends_a = first_sends(made_a, BLOCK_A)
    g_input_a, sends_a = lax.optimization_barrier((g_input_a, sends_a))
    g_shift_a = jnp.sum(g_input_a, axis=1)
    g_scale_a = jnp.sum(g_input_a * normed_a, axis=1)
    planes_a = reduce_planes(made_a, sends_a, BLOCK_A)
    grad_tokens = g_middle + norm_back(g_input_a * (1.0 + scale_a), normed_a, inv_a)
    g_modulation = jnp.concatenate(
        [g_shift_a, g_scale_a, g_gate_a, g_shift_b, g_scale_b, g_gate_b], axis=1
    ).astype(bf16)
    bias_sums = [grad_b_qkv, grad_b_out, sum_gate.reshape(-1), sum_up.reshape(-1)]
    small = jnp.concatenate([g_modulation.reshape(-1)] + [b.astype(bf16) for b in bias_sums])
    small_all = lax.all_gather(small.reshape(-1, 128), axes, axis=0, tiled=False).reshape(
        DEVICES, -1
    )
    sum_b = reduce_line(planes_b).astype(bf16)
    planes_a, small_all = lax.optimization_barrier((planes_a, small_all))
    sum_a = reduce_line(planes_a).astype(bf16)
    is_down = jnp.asarray(kind_table(PLACE_B, MLP_BLOCKS))[me]
    is_out = jnp.asarray(kind_table(PLACE_A, QKV_BLOCKS))[me]
    halves = sum_b.reshape(2, BLOCK_B // 2, 128)
    sum_b = jnp.where(
        is_down == 0,
        jnp.concatenate(
            [from_tiles(half, 24).reshape(-1, 24, 128) for half in halves], axis=1
        ).reshape(-1, 128),
        jnp.pad(
            from_tiles(halves[:, : USED_DOWN // 2].reshape(-1, 128), 9),
            ((0, BLOCK_B - USED_DOWN), (0, 0)),
        ),
    )
    sum_a = jnp.where(is_out == 0, from_tiles(sum_a, 27), from_tiles(sum_a, 9))
    buffer = jnp.zeros((SHARD + 2 * BLOCK_B, 128), f32)
    buffer = collect(buffer, sum_b, BLOCK_B, block_b_range, PLACE_B)
    buffer = collect(buffer, sum_a, BLOCK_A, block_a_range, PLACE_A)
    main = buffer[BLOCK_B : BLOCK_B + SHARD]
    g_mod_all = (
        jnp.dot(chosen, small_all[:, : slots * 6 * D], preferred_element_type=f32)
        .astype(bf16)
        .reshape(images, 6 * D)
    )
    grad_biases = jnp.concatenate(
        [
            jnp.sum(small_all[:, slots * 6 * D :].astype(f32), axis=0),
            jnp.sum(g_mod_all.astype(f32), axis=0),
        ]
    )
    part_biases = lax.dynamic_slice_in_dim(grad_biases, me * bias_count, bias_count, 0)
    grad_ada = jnp.einsum("km,mn->kn", cond_rows, g_mod_all, preferred_element_type=f32)
    g_cond_rows = jnp.einsum("mn,kn->mk", g_mod_all, ada_local, preferred_element_type=f32)
    came = exchange_relative(g_cond_rows.reshape(DEVICES, slots, ADA_ROWS))
    came = jnp.take(came, jnp.arange(DEVICES) ^ me, axis=0)
    first = FIRST_ADA * 128 // (6 * D)
    g_cond = came.transpose(1, 0, 2).reshape(slots, DEVICES * ADA_ROWS)[:, first : first + D]
    cond_f = conditions.astype(f32)
    sigma_cond = jax.nn.sigmoid(cond_f)
    grad_conditions = g_cond * sigma_cond * (1.0 + cond_f * (1.0 - sigma_cond))
    row = me * SHARD + lax.broadcasted_iota(jnp.int32, (SHARD, 128), 0)
    part_weights = jnp.where(
        (row >= FIRST_ADA) & (row < FIRST_DOWN), grad_ada.reshape(SHARD, 128), main
    )
    return (out, grad_tokens.reshape(rows_all, D), grad_conditions, part_weights, part_biases)


def solution(mesh):
    chosen = on_device_32 if dict(mesh.shape) == {"fsdp": 4, "dp": 8} else on_device_plain
    return jax.shard_map(
        chosen,
        mesh=mesh,
        in_specs=(
            P(("fsdp", "dp"), None),
            P(("fsdp", "dp"), None),
            P(("fsdp", "dp"), None),
            P(("fsdp", "dp")),
            P(("fsdp", "dp"), None),
            P(("fsdp", "dp")),
        ),
        out_specs=(
            P(("fsdp", "dp"), None),
            P(("fsdp", "dp"), None),
            P(("fsdp", "dp"), None),
            P(("fsdp", "dp"), None),
            P(("fsdp", "dp")),
        ),
        check_vma=False,
    )
```

```python
import math

import jax
import jax.numpy as jnp
from jax import lax
from jax.experimental import pallas as pl
from jax.experimental.pallas import tpu as pltpu
import numpy as np
from jax.sharding import PartitionSpec as P

D = 1152
HEADS = 16
HEAD_DIM = 72
FF = 3072
GRID = 16


eps_norm = 1e-06


def unpack_weights(weight_all, bias_all):
    flat = weight_all.reshape(-1)
    layouts = ((D, 3 * D), (D, D), (D, 2 * FF), (D, 6 * D), (FF, D))
    pieces = []
    offset = 0
    for layout in layouts:
        amount = layout[0] * layout[1]
        pieces.append(flat[offset : offset + amount].reshape(layout))
        offset = offset + amount
    offset = 0
    for amount in (3 * D, D, 2 * FF, 6 * D):
        pieces.append(bias_all[offset : offset + amount])
        offset = offset + amount
    return tuple(pieces)


def rope_tables():
    quarter = HEAD_DIM // 4
    places = jnp.arange(GRID * GRID, dtype=jnp.int32)
    rows_at = (places // GRID).astype(jnp.float32)
    cols_at = (places % GRID).astype(jnp.float32)
    freqs = 10000.0 ** (-jnp.arange(quarter, dtype=jnp.float32) / quarter)
    along_rows = rows_at[:, None] * freqs[None, :]
    along_cols = cols_at[:, None] * freqs[None, :]
    angles = jnp.concatenate([along_rows, along_rows, along_cols, along_cols], axis=1)
    return (jnp.cos(angles)[:, None, :], jnp.sin(angles)[:, None, :])


def turn_half(values):
    quarter = values.shape[-1] // 4
    first = values[..., :quarter]
    second = values[..., quarter : 2 * quarter]
    third = values[..., 2 * quarter : 3 * quarter]
    fourth = values[..., 3 * quarter :]
    return jnp.concatenate([-second, first, -fourth, third], axis=-1)


def norm_parts(values):
    centred = values - jnp.mean(values, -1, keepdims=True)
    inverse = lax.rsqrt(jnp.mean(centred * centred, -1, keepdims=True) + eps_norm)
    return (centred * inverse, inverse)


def norm_back(grad_normed, normed, inverse):
    return inverse * (
        grad_normed
        - jnp.mean(grad_normed, -1, keepdims=True)
        - normed * jnp.mean(grad_normed * normed, -1, keepdims=True)
    )


def rms_parts(values):
    inverse = lax.rsqrt(jnp.mean(values * values, -1, keepdims=True) + eps_norm)
    return (values * inverse, inverse)


def rms_back(grad_normed, normed, inverse):
    return inverse * (grad_normed - normed * jnp.mean(grad_normed * normed, -1, keepdims=True))


def compute_block(tokens, cotangent, slot_mask, modulation, weights, biases):
    f32 = jnp.float32
    bf16 = jnp.bfloat16
    w_qkv, w_out, w_mlp, w_down = weights
    b_qkv, b_out, b_mlp = biases
    slots = slot_mask.shape[0]
    length = GRID * GRID
    rows_all = slots * length
    scale = 1.0 / math.sqrt(HEAD_DIM)
    heads_shape = (slots, length, HEADS, HEAD_DIM)
    cosines, sines = rope_tables()
    mask_f = slot_mask.astype(f32)[:, None, None]
    x_f = tokens.astype(f32).reshape(slots, length, D)
    shift_a, scale_a, gate_a, shift_b, scale_b, gate_b = [
        modulation[:, None, place * D : (place + 1) * D] for place in range(6)
    ]
    normed_a, inv_a = norm_parts(x_f)
    attention_input = (normed_a * (1.0 + scale_a) + shift_a).astype(bf16).reshape(rows_all, D)
    projected_output = (
        jnp.dot(attention_input, w_qkv, preferred_element_type=f32) + b_qkv.astype(f32)
    ).reshape(slots, length, 3 * D)
    q_norm, inv_q = rms_parts(projected_output[..., :D].reshape(heads_shape))
    k_norm, inv_k = rms_parts(projected_output[..., D : 2 * D].reshape(heads_shape))
    queries = (q_norm * cosines + turn_half(q_norm) * sines).astype(bf16)
    keys = (k_norm * cosines + turn_half(k_norm) * sines).astype(bf16)
    values = projected_output[..., 2 * D :].reshape(heads_shape).astype(bf16)
    scores = jnp.einsum("slhe,smhe->shlm", queries, keys, preferred_element_type=f32) * scale
    row_max = jnp.max(scores, -1, keepdims=True)
    log_total = row_max + jnp.log(jnp.sum(jnp.exp(scores - row_max), -1, keepdims=True))
    probs_low = jnp.exp(scores - log_total).astype(bf16)
    attention_output = (
        jnp.einsum("shlm,smhe->slhe", probs_low, values, preferred_element_type=f32)
        .astype(bf16)
        .reshape(rows_all, D)
    )
    attention_branch = (
        jnp.dot(attention_output, w_out, preferred_element_type=f32) + b_out.astype(f32)
    ).reshape(slots, length, D)
    middle = x_f + gate_a * attention_branch
    normed_b, inv_b = norm_parts(middle)
    feedforward_input = (normed_b * (1.0 + scale_b) + shift_b).astype(bf16).reshape(rows_all, D)
    mixed_tokens = jnp.dot(feedforward_input, w_mlp, preferred_element_type=f32) + b_mlp.astype(
        f32
    )
    gate_part = mixed_tokens[:, :FF]
    up_part = mixed_tokens[:, FF:]
    hidden_state = (jax.nn.silu(gate_part) * up_part).astype(bf16)
    feedforward_branch = jnp.dot(hidden_state, w_down, preferred_element_type=f32).reshape(
        slots, length, D
    )
    out = ((middle + gate_b * feedforward_branch) * mask_f).astype(bf16).reshape(rows_all, D)
    g_out = cotangent.astype(f32).reshape(slots, length, D) * mask_f
    g_branch_b = (gate_b * g_out).astype(bf16).reshape(rows_all, D)
    g_gate_b = jnp.sum(g_out * feedforward_branch, axis=1)
    g_hidden = jnp.einsum("rd,fd->rf", g_branch_b, w_down, preferred_element_type=f32)
    sigma_gate = jax.nn.sigmoid(gate_part)
    g_mixed = jnp.concatenate(
        [
            g_hidden * up_part * sigma_gate * (1.0 + gate_part * (1.0 - sigma_gate)),
            g_hidden * (gate_part * sigma_gate),
        ],
        axis=1,
    ).astype(bf16)
    grad_b_mlp = jnp.sum(g_mixed.astype(f32), axis=0)
    g_input_b = jnp.einsum("rf,df->rd", g_mixed, w_mlp, preferred_element_type=f32).reshape(
        slots, length, D
    )
    g_shift_b = jnp.sum(g_input_b, axis=1)
    g_scale_b = jnp.sum(g_input_b * normed_b, axis=1)
    g_middle = g_out + norm_back(g_input_b * (1.0 + scale_b), normed_b, inv_b)
    g_branch_a = (gate_a * g_middle).astype(bf16).reshape(rows_all, D)
    g_gate_a = jnp.sum(g_middle * attention_branch, axis=1)
    grad_b_out = jnp.sum(g_branch_a.astype(f32), axis=0)
    g_attended = (
        jnp.einsum("re,de->rd", g_branch_a, w_out, preferred_element_type=f32)
        .astype(bf16)
        .reshape(heads_shape)
    )
    scores = jnp.einsum("slhe,smhe->shlm", queries, keys, preferred_element_type=f32) * scale
    probs = jnp.exp(scores - log_total)
    probs_low = probs.astype(bf16)
    g_probs = jnp.einsum("slhe,smhe->shlm", g_attended, values, preferred_element_type=f32)
    g_values = jnp.einsum("shlm,slhe->smhe", probs_low, g_attended, preferred_element_type=f32)
    g_scores = (probs * (g_probs - jnp.sum(probs * g_probs, -1, keepdims=True))).astype(bf16)
    g_queries = jnp.einsum("shlm,smhe->slhe", g_scores, keys, preferred_element_type=f32) * scale
    g_keys = jnp.einsum("shlm,slhe->smhe", g_scores, queries, preferred_element_type=f32) * scale
    g_q = rms_back(g_queries * cosines - turn_half(g_queries) * sines, q_norm, inv_q)
    g_k = rms_back(g_keys * cosines - turn_half(g_keys) * sines, k_norm, inv_k)
    g_projected = jnp.concatenate(
        [g_q.reshape(rows_all, D), g_k.reshape(rows_all, D), g_values.reshape(rows_all, D)], axis=1
    ).astype(bf16)
    grad_b_qkv = jnp.sum(g_projected.astype(f32), axis=0)
    g_input_a = jnp.einsum("re,de->rd", g_projected, w_qkv, preferred_element_type=f32).reshape(
        slots, length, D
    )
    g_shift_a = jnp.sum(g_input_a, axis=1)
    g_scale_a = jnp.sum(g_input_a * normed_a, axis=1)
    grad_tokens = g_middle + norm_back(g_input_a * (1.0 + scale_a), normed_a, inv_a)
    g_modulation = jnp.concatenate(
        [g_shift_a, g_scale_a, g_gate_a, g_shift_b, g_scale_b, g_gate_b], axis=1
    ).astype(bf16)
    pairs = (
        (attention_input, g_projected),
        (attention_output, g_branch_a),
        (feedforward_input, g_mixed),
        (hidden_state, g_branch_b),
    )
    return (
        out,
        grad_tokens.reshape(rows_all, D),
        g_modulation,
        (grad_b_qkv, grad_b_out, grad_b_mlp),
        pairs,
    )


def weight_grad(pair):
    return jnp.einsum("rd,re->de", pair[0], pair[1], preferred_element_type=jnp.float32)


def on_device_plain(tokens, conditions, cotangent, slot_mask, weight_flat, bias_flat):
    f32 = jnp.float32
    bf16 = jnp.bfloat16
    axes = ("fsdp", "dp")
    weight_all = lax.all_gather(weight_flat, axes, axis=0, tiled=True)
    bias_all = lax.all_gather(bias_flat, axes, axis=0, tiled=True)
    w_qkv, w_out, w_mlp, w_ada, w_down, b_qkv, b_out, b_mlp, b_ada = unpack_weights(
        weight_all, bias_all
    )
    cond_f = conditions.astype(f32)
    cond_act = jax.nn.silu(cond_f).astype(bf16)
    modulation = jnp.dot(cond_act, w_ada, preferred_element_type=f32) + b_ada.astype(f32)
    out, grad_tokens, g_modulation, bias_sums, pairs = compute_block(
        tokens,
        cotangent,
        slot_mask,
        modulation,
        (w_qkv, w_out, w_mlp, w_down),
        (b_qkv, b_out, b_mlp),
    )
    grad_b_ada = jnp.sum(g_modulation.astype(f32), axis=0)
    g_cond = jnp.einsum("se,de->sd", g_modulation, w_ada, preferred_element_type=f32)
    sigma_cond = jax.nn.sigmoid(cond_f)
    grad_conditions = g_cond * sigma_cond * (1.0 + cond_f * (1.0 - sigma_cond))
    grad_qkv, grad_out, grad_mlp, grad_down = [weight_grad(pair) for pair in pairs]
    grad_ada = weight_grad((cond_act, g_modulation))
    grads_big = jnp.concatenate(
        [
            grad.astype(bf16).reshape(-1)
            for grad in (grad_qkv, grad_out, grad_mlp, grad_ada, grad_down)
        ]
    ).reshape(-1, 128)
    grads_small = jnp.concatenate([*bias_sums, grad_b_ada])
    part_weights = lax.psum_scatter(grads_big, axes, scatter_dimension=0, tiled=True)
    part_biases = lax.psum_scatter(grads_small, axes, scatter_dimension=0, tiled=True)
    return (out, grad_tokens, grad_conditions, part_weights.astype(f32), part_biases)


ROWS_QKV = 3 * D * D // 128
ROWS_OUT = D * D // 128
ROWS_MLP = 2 * D * FF // 128
ROWS_ADA = 6 * D * D // 128
ROWS_DOWN = D * FF // 128
FIRST_MLP = ROWS_QKV + ROWS_OUT
FIRST_ADA = FIRST_MLP + ROWS_MLP
FIRST_DOWN = FIRST_ADA + ROWS_ADA
DEVICES = 32
SHARD = 5832
BLOCK_A = 1296
BLOCK_B = 2688
USED_DOWN = 2592
MLP_BLOCKS = 21
QKV_BLOCKS = 24
ADA_ROWS = SHARD * 128 // (6 * D)


def block_a_range(block):
    return (BLOCK_A * block, BLOCK_A * (block + 1))


def block_b_range(block):
    if block < MLP_BLOCKS:
        first = FIRST_MLP + BLOCK_B * block
        return (first, min(first + BLOCK_B, FIRST_ADA))
    first = FIRST_DOWN + USED_DOWN * (block - MLP_BLOCKS)
    return (first, min(first + USED_DOWN, FIRST_DOWN + ROWS_DOWN))


def plan_rounds(block_range, first_block, count, device_of_block):
    rounds = []
    for k in range(count):
        pairs = []
        for owner in range(DEVICES):
            block = first_block(owner) + k
            if 0 <= block < DEVICES:
                first, last = block_range(block)
                if first < (owner + 1) * SHARD and last > owner * SHARD:
                    pairs.append((owner, device_of_block(block)))
        rounds.append(pairs)
    return rounds


DOWN_OWNER = FIRST_DOWN // SHARD


def first_block_a(owner):
    return owner * SHARD // BLOCK_A


def first_block_b(owner):
    if owner < DOWN_OWNER:
        return (owner * SHARD - FIRST_MLP) // BLOCK_B
    return MLP_BLOCKS + max((owner * SHARD - FIRST_DOWN) // USED_DOWN, -1)


def starts_a():
    return -(device_index() * SHARD % BLOCK_A), BLOCK_A


def starts_b():
    me = device_index()
    low = me >= DOWN_OWNER
    first = jnp.where(low, FIRST_DOWN, FIRST_MLP)
    step = jnp.where(low, USED_DOWN, BLOCK_B)
    return -((me * SHARD - first) % step), step


PLAN_A = (BLOCK_A, block_a_range, first_block_a, 5, starts_a)
PLAN_B = (BLOCK_B, block_b_range, first_block_b, 4, starts_b)


def device_index():
    return lax.axis_index("fsdp") * lax.axis_size("dp") + lax.axis_index("dp")


def cut_pieces(shard, plan):
    block_rows, _, _, count, starts = plan
    padded = jnp.pad(shard, ((block_rows, block_rows), (0, 0)))
    first, step = starts()
    return [
        lax.dynamic_slice_in_dim(padded, block_rows + first + k * step, block_rows, 0)
        for k in range(count)
    ]


def spread(pieces, plan):
    _, block_range, first_block, count, _ = plan
    rounds = plan_rounds(block_range, first_block, count, lambda block: block)
    total = None
    for piece, pairs in zip(pieces, rounds, strict=True):
        got = lax.ppermute(piece, ("fsdp", "dp"), pairs)
        total = got if total is None else total + got
    return total


def send_back(block, plan, places):
    _, block_range, first_block, count, _ = plan
    rounds = plan_rounds(block_range, first_block, count, lambda block: device_of(places, block))
    return [
        lax.ppermute(block, ("fsdp", "dp"), [(device, owner) for owner, device in pairs])
        for pairs in rounds
    ]


def to_tiles(rows, chunks):
    return (
        rows.reshape(-1, 8, chunks, 128).transpose(0, 2, 1, 3).reshape(-1, 128)
    )


def from_tiles(rows, chunks):
    return (
        rows.reshape(-1, chunks, 8, 128).transpose(0, 2, 1, 3).reshape(-1, 128)
    )


def matrix_of_tiles(rows, height, width):
    return (
        rows.reshape(height // 8, width // 128, 8, 128)
        .transpose(0, 2, 1, 3)
        .reshape(height, width)
    )


def tiles_of_matrix(matrix):
    height, width = matrix.shape
    return (
        matrix.reshape(height // 8, 8, width // 128, 128)
        .transpose(0, 2, 1, 3)
        .reshape(-1, 128)
    )


SWAP_X = [(0, 1), (1, 0), (2, 3), (3, 2)]
SWAP_Y = [(0, 2), (2, 0), (1, 3), (3, 1)]
SWAP_CORE = [(d, d ^ 1) for d in range(8)]


def along_z(pairs):
    return [(2 * a + e, 2 * b + e) for a, b in pairs for e in range(2)]


def chips_of(*lines):
    place = {}
    for z, line in enumerate(lines):
        for f, block in enumerate(line):
            place[block] = 4 * f + z
    return place


PLACE_A = (
    chips_of((0, 1, 2, 3), (4, 5, 6, 7), (18, 19, 20, 21), (22, 23, 16, 17)),
    chips_of((8, 9, 10, 11), (12, 13, 14, 15), (24, 25, 26, 27), (28, 29, 30, 31)),
)
PLACE_B = (
    chips_of((2, 3, 4, 5), (6, 7, 8, 9), (10, 11, 12, 13), (14, 0, 15, 1)),
    chips_of((20, 16, 17, 18), (21, 22, 23, 24), (25, 26, 27, 28), (29, 19, 30, 31)),
)


def device_of(places, block):
    core = 0 if block in places[0] else 1
    return 2 * places[core][block] + core


def is_kind(places, first_of_second):
    mask = sum(1 << device_of(places, block) for block in range(first_of_second, DEVICES))
    bits = jnp.uint32(mask) >> device_index().astype(jnp.uint32)
    return bits % 2 == 1


def add_low(a, b):
    return (a.astype(jnp.float32) + b.astype(jnp.float32)).astype(jnp.bfloat16)


def pick(array, index, axis):
    return lax.dynamic_index_in_dim(array, index, axis, keepdims=False)


def first_sends(grads, block_rows):
    f = lax.axis_index("fsdp")
    y, x = f // 2, f % 2
    a, b = [part.reshape(2, 2, 4, block_rows // 2, 128) for part in grads]
    return pick(a, 1 - y, 0), pick(b, 1 - x, 1)


def over_planes(sends, axes):
    return [lax.ppermute(send, "fsdp", axis) for send, axis in zip(sends, axes, strict=True)]


def second_sends(grads, arrived, block_rows):
    f = lax.axis_index("fsdp")
    y, x = f // 2, f % 2
    a, b = [part.reshape(2, 2, 4, block_rows // 2, 128) for part in grads]
    a = add_low(pick(a, y, 0), arrived[0])
    b = add_low(pick(b, x, 1), arrived[1])
    return (pick(a, x, 0), pick(b, y, 0)), (pick(a, 1 - x, 0), pick(b, 1 - y, 0))


def plane_sums(kept, arrived):
    return jnp.concatenate([add_low(k, a) for k, a in zip(kept, arrived, strict=True)], axis=1)


def after(value, *others):
    return lax.optimization_barrier((value, others))[0]


def line_sends(planes):
    z = lax.axis_index("dp") // 2
    return [pick(planes, z ^ k, 0) for k in range(4)]


def from_line(sends):
    return [
        lax.ppermute(sends[k], "dp", [(d, d ^ (2 * k)) for d in range(8)]) for k in range(1, 4)
    ]


def sum_line(own, others):
    total = own.astype(jnp.float32)
    for other in others:
        total += other.astype(jnp.float32)
    return total


def gather_column(array):
    parts = [array] + [
        lax.ppermute(array, "dp", [(d, d ^ k) for d in range(8)]) for k in range(1, 8)
    ]
    return jnp.stack(parts)


def gather_columns(part):
    parts = [part] + [
        lax.ppermute(part, "fsdp", [(f, f ^ k) for f in range(4)]) for k in range(1, 4)
    ]
    return jnp.stack(parts).reshape(DEVICES, *part.shape[1:])


ADA_GROUPS = range(FIRST_ADA // (8 * SHARD), (FIRST_DOWN - 1) // (8 * SHARD) + 1)


def sum_to_owners(terms):
    def send(array, change, groups):
        pairs = [(8 * f + d, (8 * f + d) ^ change) for f in groups for d in range(8)]
        return lax.ppermute(array, ("fsdp", "dp"), pairs)

    terms = terms.reshape(4, 4, 2, *terms.shape[1:])
    terms = terms[:, :, 0] + send(terms[:, :, 1], 1, ADA_GROUPS)
    terms = terms[0] + sum(send(terms[k], 8 * k, ADA_GROUPS) for k in range(1, 4))
    return terms[0] + sum(send(terms[k], 2 * k, range(4)) for k in range(1, 4))


def mlp_both_ways(x, g, bias, gathered):
    f32, bf16 = jnp.float32, jnp.bfloat16
    rows = x.shape[0]
    steps = FF // 256
    full = BLOCK_B // 8
    used = USED_DOWN // 8
    wide = 2 * FF // 128
    chunks = D // 128
    across = (((1,), (1,)), ((), ()))

    def body(x_ref, g_ref, bias_g_ref, bias_u_ref, source, *rest):
        hid_ref, gg_ref, gu_ref, branch_ref, gin_ref, sum_g_ref, sum_u_ref, *rest = rest
        mix_ref, down_ref, sem = rest
        step = pl.program_id(0)

        def each(act):
            stride = (BLOCK_A + BLOCK_B) // 8
            for i in range(DEVICES):
                first = i * stride + BLOCK_A // 8
                if i < MLP_BLOCKS:
                    piece = source.at[pl.ds(first, full)]
                    flat = mix_ref.reshape(MLP_BLOCKS * full, 8, 128)
                    target = flat.at[pl.ds(i * full, full)]
                else:
                    piece = source.at[pl.ds(first, used)]
                    target = down_ref.at[pl.ds((i - MLP_BLOCKS) * used, used)]
                act(pltpu.make_async_copy(piece, target, sem.at[i]))

        @pl.when(step == 0)
        def _():
            each(lambda copy: copy.start())
            branch_ref[...] = jnp.zeros_like(branch_ref)
            gin_ref[...] = jnp.zeros_like(gin_ref)
            each(lambda copy: copy.wait())

        def columns(first):
            return jnp.concatenate(
                [
                    mix_ref[: D // 8, first + i].reshape(D, 128)
                    for i in range(2)
                ],
                axis=1,
            )

        x = x_ref[...]
        w_gate, w_up = columns(2 * step), columns(wide // 2 + 2 * step)
        gate = jnp.dot(x, w_gate, preferred_element_type=f32) + bias_g_ref[...]
        up = jnp.dot(x, w_up, preferred_element_type=f32) + bias_u_ref[...]
        sigma = jax.nn.sigmoid(gate)
        silu = gate * sigma
        hid = (silu * up).astype(bf16)
        hid_ref[...] = hid
        low_rows = down_ref[pl.ds(step * 32 * chunks, 32 * chunks)].reshape(32, chunks, 8, 128)
        w_down = jnp.concatenate([low_rows[:, j].reshape(256, 128) for j in range(chunks)], axis=1)
        branch_ref[...] += jnp.dot(hid, w_down, preferred_element_type=f32)
        g_hid = lax.dot_general(g_ref[...], w_down, across, preferred_element_type=f32)
        g_gate = (g_hid * up * sigma * (1.0 + gate * (1.0 - sigma))).astype(bf16)
        g_up = (g_hid * silu).astype(bf16)
        gg_ref[...] = g_gate
        gu_ref[...] = g_up
        sum_g_ref[...] = jnp.sum(g_gate.astype(f32), axis=0, keepdims=True)
        sum_u_ref[...] = jnp.sum(g_up.astype(f32), axis=0, keepdims=True)
        gin_ref[...] += lax.dot_general(
            g_gate, w_gate, across, preferred_element_type=f32
        ) + lax.dot_general(g_up, w_up, across, preferred_element_type=f32)

    whole = pl.BlockSpec((rows, D), lambda t: (0, 0))
    part = pl.BlockSpec((rows, 256), lambda t: (0, t))
    line = pl.BlockSpec((1, 256), lambda t: (0, t))
    return pl.pallas_call(
        body,
        grid=(steps,),
        in_specs=[
            whole,
            whole,
            line,
            pl.BlockSpec((1, 256), lambda t: (0, steps + t)),
            pl.BlockSpec(memory_space=pl.ANY),
        ],
        out_specs=[part, part, part, whole, whole, line, line],
        out_shape=[jax.ShapeDtypeStruct((rows, FF), bf16)] * 3
        + [jax.ShapeDtypeStruct((rows, D), f32)] * 2
        + [jax.ShapeDtypeStruct((1, FF), f32)] * 2,
        scratch_shapes=[
            pltpu.VMEM((MLP_BLOCKS * full // wide, wide, 8, 128), bf16),
            pltpu.VMEM(((DEVICES - MLP_BLOCKS) * used, 8, 128), bf16),
            pltpu.SemaphoreType.DMA((DEVICES,)),
        ],
        cost_estimate=pl.CostEstimate(
            flops=12 * rows * D * FF, bytes_accessed=30_000_000, transcendentals=rows * FF
        ),
        compiler_params=pltpu.CompilerParams(vmem_limit_bytes=46 << 20),
        name="mlp_both_ways",
    )(x, g, bias, bias, gathered)


def pair_product(xo, xp, go, gp):
    down = (((0,), (0,)), ((), ()))
    total = lax.dot_general(xo[...], go[...], down, preferred_element_type=jnp.float32)
    total += lax.dot_general(xp[...], gp[...], down, preferred_element_type=jnp.float32)
    return total.astype(jnp.bfloat16)


def store_tiles(out_ref, lead, first, value):
    for j in range(value.shape[1] // 128):
        out_ref[(*lead, first + j)] = value[:, 128 * j : 128 * (j + 1)]


def grads_b_core_0(in_b, g_gate, g_up):
    def body(xo, xp, gog, gpg, gou, gpu, *outs):
        for out_ref, go, gp in ((outs[0], gog, gpg), (outs[1], gou, gpu)):
            value = pair_product(xo, xp, go, gp)
            for j in range(4):
                part = value[:, 128 * j : 128 * (j + 1)].reshape(16, 7, 8, 128)
                for block in range(16):
                    out_ref[PLACE_B[0][block], :, j] = part[block]

    rows = in_b[0].shape[0]
    high = 16 * 56
    x_spec = pl.BlockSpec((rows, high), lambda t: (0, 0))
    g_spec = pl.BlockSpec((rows, 512), lambda t: (0, t))
    out = pl.pallas_call(
        body,
        grid=(FF // 512,),
        in_specs=[x_spec] * 2 + [g_spec] * 4,
        out_specs=[pl.BlockSpec((16, 7, 4, 8, 128), lambda t: (0, 0, t, 0, 0))] * 2,
        out_shape=[jax.ShapeDtypeStruct((16, 7, FF // 128, 8, 128), jnp.bfloat16)] * 2,
        compiler_params=pltpu.CompilerParams(vmem_limit_bytes=44 << 20),
        name="grads_b_core_0",
    )(*in_b, *g_gate, *g_up)
    return [part.reshape(-1, 128) for part in out]


def grads_b_core_1(in_b, g_gate, g_up, hidden, g_branch):
    bf16 = jnp.bfloat16
    rows = in_b[0].shape[0]
    mlp_steps = FF // 512
    wide = 384
    down_steps = FF // wide
    half_tiles = BLOCK_B // 16
    mlp_groups = (D - 16 * 56) // 8
    groups = (MLP_BLOCKS - 16) * 7
    half_groups = USED_DOWN // 9 // 16
    down_blocks = DEVICES - MLP_BLOCKS

    place = PLACE_B[1]

    def body(place_ref, xo, xp, gog, gpg, gou, gpu, ho, hp, go, gp, *outs):
        step = pl.program_id(0)

        @pl.when(step == 0)
        def _():
            for group in range(mlp_groups, groups):
                first = place[16 + group // 7] * half_tiles + group % 7 * (FF // 128)
                for out_ref in outs:
                    out_ref[pl.ds(first, FF // 128)] = jnp.zeros((FF // 128, 8, 128), bf16)
            for block in range(down_blocks):
                for half in range(2):
                    used = min(half_groups, FF // 8 - (2 * block + half) * half_groups) * 9
                    first = place[MLP_BLOCKS + block] * half_tiles + used
                    rest = half_tiles - used
                    outs[half][pl.ds(first, rest)] = jnp.zeros((rest, 8, 128), bf16)

        @pl.when(step < mlp_steps)
        def _():
            for out_ref, g_own, g_par in ((outs[0], gog, gpg), (outs[1], gou, gpu)):
                value = pair_product(xo, xp, g_own, g_par)
                skip = value.shape[0] - mlp_groups * 8
                for group in range(mlp_groups):
                    first = place[16 + group // 7] * half_tiles + group % 7 * (FF // 128)
                    store_tiles(
                        out_ref,
                        (),
                        first + step * 4,
                        value[skip + 8 * group : skip + 8 * group + 8],
                    )

        @pl.when(step >= mlp_steps)
        def _():
            value = pair_product(ho, hp, go, gp)
            for group in range(wide // 8):
                at = (step - mlp_steps) * (wide // 8) + group
                part = at // half_groups
                first = place_ref[part // 2] * half_tiles + (at % half_groups) * 9
                piece = value[8 * group : 8 * group + 8]

                def put(out_ref, first=first, piece=piece):
                    store_tiles(out_ref, (), first, piece)

                pl.when(part % 2 == 0)(lambda put=put: put(outs[0]))
                pl.when(part % 2 == 1)(lambda put=put: put(outs[1]))

    x_spec = pl.BlockSpec((rows, 384), lambda t: (0, 2))
    g_spec = pl.BlockSpec((rows, 512), lambda t: (0, jnp.minimum(t, mlp_steps - 1)))
    h_spec = pl.BlockSpec((rows, wide), lambda t: (0, jnp.maximum(t - mlp_steps, 0)))
    b_spec = pl.BlockSpec((rows, D), lambda t: (0, 0))
    shape = (16 * half_tiles, 8, 128)
    down_place = jnp.asarray([place[MLP_BLOCKS + i] for i in range(down_blocks)], jnp.int32)
    out = pl.pallas_call(
        body,
        grid=(mlp_steps + down_steps,),
        in_specs=[pl.BlockSpec(memory_space=pltpu.SMEM)]
        + [x_spec] * 2
        + [g_spec] * 4
        + [h_spec] * 2
        + [b_spec] * 2,
        out_specs=[pl.BlockSpec(shape, lambda t: (0, 0, 0))] * 2,
        out_shape=[jax.ShapeDtypeStruct(shape, bf16)] * 2,
        compiler_params=pltpu.CompilerParams(vmem_limit_bytes=44 << 20),
        name="grads_b_core_1",
    )(down_place, *in_b, *g_gate, *g_up, *hidden, *g_branch)
    return [part.reshape(-1, 128) for part in out]


def grads_a(core, in_a, g_proj, att, g_branch):
    rows = in_a[0].shape[0]
    steps = 3 * D // 384
    place = PLACE_A[core]

    def store_qkv(value, first_block, step, outs):
        for group in range(48):
            block, half, low = first_block + group // 6, group // 3 % 2, group % 3
            store_tiles(
                outs[half],
                (place[block],),
                low * 27 + step * 3,
                value[8 * group : 8 * group + 8],
            )

    def body(xo, xp, go, gp, zo, zp, bo, bp, *outs):
        step = pl.program_id(0)

        @pl.when(step < steps)
        def _():
            store_qkv(pair_product(xo, xp, go, gp), 8 * core, step, outs)
            if core == 0:
                store_qkv(pair_product(zo, zp, go, gp), 16, step, outs)

        if core == 1:

            @pl.when(step >= steps)
            def _():
                value = pair_product(zo, zp, bo, bp)
                for group in range(144):
                    block, half, low = QKV_BLOCKS + group // 18, group // 9 % 2, group % 9
                    store_tiles(
                        outs[half],
                        (place[block],),
                        low * 9 + (step - steps) * 3,
                        value[8 * group : 8 * group + 8],
                    )

    x_spec = pl.BlockSpec((rows, 384), lambda t: (0, core))
    g_spec = pl.BlockSpec((rows, 384), lambda t: (0, jnp.minimum(t, steps - 1)))
    if core == 0:
        z_spec, z = pl.BlockSpec((rows, 384), lambda t: (0, 2)), in_a
        b_spec, count = pl.BlockSpec((rows, 384), lambda t: (0, 0)), steps
    else:
        z_spec, z = pl.BlockSpec((rows, D), lambda t: (0, 0)), att
        b_spec = pl.BlockSpec((rows, 384), lambda t: (0, jnp.maximum(t - steps, 0)))
        count = steps + D // 384
    shape = (16, 81, 8, 128)
    out = pl.pallas_call(
        body,
        grid=(count,),
        in_specs=[x_spec] * 2 + [g_spec] * 2 + [z_spec] * 2 + [b_spec] * 2,
        out_specs=[pl.BlockSpec(shape, lambda t: (0, 0, 0, 0))] * 2,
        out_shape=[jax.ShapeDtypeStruct(shape, jnp.bfloat16)] * 2,
        compiler_params=pltpu.CompilerParams(vmem_limit_bytes=44 << 20),
        name=f"grads_a_core_{core}",
    )(*in_a, *g_proj, *z, *g_branch)
    return [part.reshape(-1, 128) for part in out]


def gathered_weights(pieces_a, pieces_b):
    me = device_index()
    block_a = spread(pieces_a, PLAN_A)
    block_a = jnp.where(me < QKV_BLOCKS, to_tiles(block_a, 27), to_tiles(block_a, 9))
    block_b = spread(pieces_b, PLAN_B)
    block_b = jnp.where(
        me < MLP_BLOCKS,
        to_tiles(block_b, 48),
        jnp.pad(to_tiles(block_b[:USED_DOWN], 9), ((0, BLOCK_B - USED_DOWN), (0, 0))),
    )
    block = jnp.concatenate([block_a, block_b])
    return lax.all_gather(block, ("fsdp", "dp"), axis=0, tiled=True).reshape(-1, 8, 128)


def head_indicator():
    feature = lax.broadcasted_iota(jnp.int32, (D, 128), 0)
    head = lax.broadcasted_iota(jnp.int32, (D, 128), 1)
    return ((feature >= head * HEAD_DIM) & (feature < (head + 1) * HEAD_DIM)).astype(jnp.bfloat16)


def two_parts(value):
    high = value.astype(jnp.bfloat16)
    return high, (value - high.astype(jnp.float32)).astype(jnp.bfloat16)


def head_means(value, indicator):
    high, low = two_parts(value)
    total = jnp.dot(high, indicator, preferred_element_type=jnp.float32)
    total += jnp.dot(low, indicator, preferred_element_type=jnp.float32)
    return total * (1.0 / HEAD_DIM)


def over_heads(value, indicator):
    high, low = two_parts(value)
    across = (((1,), (1,)), ((), ()))
    total = lax.dot_general(high, indicator, across, preferred_element_type=jnp.float32)
    return total + lax.dot_general(low, indicator, across, preferred_element_type=jnp.float32)


def turned(value):
    quarter = HEAD_DIM // 4
    feature = lax.broadcasted_iota(jnp.int32, value.shape, 1) % (2 * quarter)
    ahead = pltpu.roll(value, D - quarter, 1)
    behind = pltpu.roll(value, quarter, 1)
    return jnp.where(feature < quarter, -ahead, behind)


def heads_of(ref):
    return [ref[:, HEAD_DIM * h : HEAD_DIM * (h + 1)] for h in range(HEADS)]


ACROSS = (((1,), (1,)), ((), ()))
DOWN = (((0,), (0,)), ((), ()))


def attention_forward(projected, cosines, sines):
    f32, bf16 = jnp.float32, jnp.bfloat16
    rows = projected.shape[0]
    length = cosines.shape[0]
    scale = 1.0 / math.sqrt(HEAD_DIM)

    def body(proj_ref, cos_ref, sin_ref, ind_ref, q_ref, k_ref, v_ref, att_ref, log_ref):
        indicator = ind_ref[...]
        for part, ref in ((0, q_ref), (1, k_ref)):
            value = proj_ref[:, D * part : D * (part + 1)]
            inverse = lax.rsqrt(head_means(value * value, indicator) + eps_norm)
            norm = value * over_heads(inverse, indicator)
            ref[...] = (norm * cos_ref[...] + turned(norm) * sin_ref[...]).astype(bf16)
        v_ref[...] = proj_ref[:, 2 * D :].astype(bf16)
        logs = []
        for h in range(HEADS):
            at = slice(HEAD_DIM * h, HEAD_DIM * (h + 1))
            scores = (
                lax.dot_general(q_ref[:, at], k_ref[:, at], ACROSS, preferred_element_type=f32)
                * scale
            )
            top = jnp.max(scores, axis=1, keepdims=True)
            log_total = top + jnp.log(jnp.sum(jnp.exp(scores - top), axis=1, keepdims=True))
            probs = jnp.exp(scores - log_total).astype(bf16)
            att_ref[:, at] = jnp.dot(probs, v_ref[:, at], preferred_element_type=f32).astype(bf16)
            log_ref[:, h : h + 1] = log_total

    wide = pl.BlockSpec((length, D), lambda i: (i, 0))
    table = pl.BlockSpec((length, D), lambda i: (0, 0))
    return pl.pallas_call(
        body,
        grid=(rows // length,),
        in_specs=[
            pl.BlockSpec((length, 3 * D), lambda i: (i, 0)),
            table,
            table,
            pl.BlockSpec((D, 128), lambda i: (0, 0)),
        ],
        out_specs=[wide] * 4 + [pl.BlockSpec((length, HEADS), lambda i: (i, 0))],
        out_shape=[jax.ShapeDtypeStruct((rows, D), bf16)] * 4
        + [jax.ShapeDtypeStruct((rows, HEADS), f32)],
        cost_estimate=pl.CostEstimate(
            flops=8 * rows * length * D, bytes_accessed=20_000_000, transcendentals=40_000_000
        ),
        compiler_params=pltpu.CompilerParams(vmem_limit_bytes=44 << 20),
        name="attention_forward",
    )(projected, cosines, sines, head_indicator())


def attention_backward(projected, queries, keys, values, log_total, g_attended, cosines, sines):
    f32, bf16 = jnp.float32, jnp.bfloat16
    rows = projected.shape[0]
    length = cosines.shape[0]
    scale = 1.0 / math.sqrt(HEAD_DIM)

    def body(proj_ref, q_ref, k_ref, v_ref, log_ref, g_ref, cos_ref, sin_ref, ind_ref, *rest):
        out_ref, sum_ref, gq_ref, gk_ref, gv_ref = rest
        for h in range(HEADS):
            at = slice(HEAD_DIM * h, HEAD_DIM * (h + 1))
            q, k, v, g = q_ref[:, at], k_ref[:, at], v_ref[:, at], g_ref[:, at]
            scores = lax.dot_general(q, k, ACROSS, preferred_element_type=f32) * scale
            probs = jnp.exp(scores - log_ref[:, h : h + 1])
            g_probs = lax.dot_general(g, v, ACROSS, preferred_element_type=f32)
            gv_ref[:, at] = lax.dot_general(
                probs.astype(bf16), g, DOWN, preferred_element_type=f32
            )
            inner = jnp.sum(probs * g_probs, axis=1, keepdims=True)
            g_scores = (probs * (g_probs - inner)).astype(bf16)
            gq_ref[:, at] = jnp.dot(g_scores, k, preferred_element_type=f32) * scale
            gk_ref[:, at] = (
                lax.dot_general(g_scores, q, DOWN, preferred_element_type=f32) * scale
            )
        indicator = ind_ref[...]
        for part, ref in ((0, gq_ref), (1, gk_ref)):
            value = proj_ref[:, D * part : D * (part + 1)]
            inverse = over_heads(
                lax.rsqrt(head_means(value * value, indicator) + eps_norm), indicator
            )
            norm = value * inverse
            back = ref[...] * cos_ref[...] - turned(ref[...]) * sin_ref[...]
            mean = over_heads(head_means(back * norm, indicator), indicator)
            out_ref[:, D * part : D * (part + 1)] = (inverse * (back - norm * mean)).astype(bf16)
        out_ref[:, 2 * D :] = gv_ref[...].astype(bf16)
        sum_ref[0] = jnp.sum(out_ref[...].astype(f32), axis=0, keepdims=True)

    wide = pl.BlockSpec((length, D), lambda i: (i, 0))
    table = pl.BlockSpec((length, D), lambda i: (0, 0))
    images = rows // length
    return pl.pallas_call(
        body,
        grid=(images,),
        in_specs=[
            pl.BlockSpec((length, 2 * D), lambda i: (i, 0)),
            wide,
            wide,
            wide,
            pl.BlockSpec((length, HEADS), lambda i: (i, 0)),
            wide,
            table,
            table,
            pl.BlockSpec((D, 128), lambda i: (0, 0)),
        ],
        out_specs=[
            pl.BlockSpec((length, 3 * D), lambda i: (i, 0)),
            pl.BlockSpec((1, 1, 3 * D), lambda i: (i, 0, 0)),
        ],
        out_shape=[
            jax.ShapeDtypeStruct((rows, 3 * D), bf16),
            jax.ShapeDtypeStruct((images, 1, 3 * D), f32),
        ],
        scratch_shapes=[pltpu.VMEM((length, D), f32)] * 3,
        cost_estimate=pl.CostEstimate(flops=1000, bytes_accessed=1000, transcendentals=0),
        compiler_params=pltpu.CompilerParams(vmem_limit_bytes=44 << 20),
        name="attention_backward",
    )(projected, queries, keys, values, log_total, g_attended, cosines, sines, head_indicator())


def split_a(gathered):
    block = BLOCK_A // 8

    def body(all_ref, qkv_ref, out_ref, sem):
        copies = []
        for i in range(DEVICES):
            ref, first = (qkv_ref, 0) if i < QKV_BLOCKS else (out_ref, QKV_BLOCKS)
            copies.append(
                pltpu.make_async_copy(
                    all_ref.at[pl.ds(i * (BLOCK_A + BLOCK_B) // 8, block)],
                    ref.at[pl.ds((i - first) * block, block)],
                    sem.at[i],
                )
            )
        for copy in copies:
            copy.start()
        for copy in copies:
            copy.wait()

    w_qkv, w_out = pl.pallas_call(
        body,
        in_specs=[pl.BlockSpec(memory_space=pl.ANY)],
        out_specs=[pl.BlockSpec(memory_space=pltpu.VMEM)] * 2,
        out_shape=[
            jax.ShapeDtypeStruct((ROWS_QKV // 8, 8, 128), jnp.bfloat16),
            jax.ShapeDtypeStruct((ROWS_OUT // 8, 8, 128), jnp.bfloat16),
        ],
        scratch_shapes=[pltpu.SemaphoreType.DMA((DEVICES,))],
        compiler_params=pltpu.CompilerParams(vmem_limit_bytes=40 << 20),
        name="split_a",
    )(gathered)
    return matrix_of_tiles(w_qkv, D, 3 * D), matrix_of_tiles(w_out, D, D)


def owned_rows(back_a, back_b, grad_ada):
    first_a, step_a = starts_a()
    first_b, step_b = starts_b()
    me = device_index()
    numbers = jnp.stack(
        [jnp.asarray(v, jnp.int32) for v in (first_a, step_a, first_b, step_b, me * SHARD)]
    )
    total = SHARD + 2 * BLOCK_B

    def body(numbers_ref, *refs):
        out_ref, sum_ref = refs[-2:]
        sum_ref[...] = jnp.zeros_like(sum_ref)
        for refs_of, at, rows in (
            (refs[: len(back_b)], 2, BLOCK_B),
            (refs[len(back_b) : len(back_b) + len(back_a)], 0, BLOCK_A),
        ):
            for k, ref in enumerate(refs_of):
                start = BLOCK_B + numbers_ref[at] + k * numbers_ref[at + 1]
                start = pl.multiple_of(jnp.clip(start, 0, total - rows), 8)
                sum_ref[pl.ds(start, rows)] += ref[...].astype(jnp.float32)
        row = numbers_ref[4] + lax.broadcasted_iota(jnp.int32, (SHARD, 128), 0)
        out_ref[...] = jnp.where(
            (row >= FIRST_ADA) & (row < FIRST_DOWN),
            refs[-3][...],
            sum_ref[pl.ds(BLOCK_B, SHARD)],
        )

    return pl.pallas_call(
        body,
        in_specs=[pl.BlockSpec(memory_space=pltpu.SMEM)]
        + [pl.BlockSpec(memory_space=pltpu.VMEM)] * (len(back_a) + len(back_b) + 1),
        out_specs=pl.BlockSpec(memory_space=pltpu.VMEM),
        out_shape=jax.ShapeDtypeStruct((SHARD, 128), jnp.float32),
        scratch_shapes=[pltpu.VMEM((total, 128), jnp.float32)],
        compiler_params=pltpu.CompilerParams(vmem_limit_bytes=40 << 20),
        name="owned_rows",
    )(numbers, *back_b, *back_a, grad_ada)


def on_device_32(tokens, conditions, cotangent, slot_mask, weight_flat, bias_flat):
    f32 = jnp.float32
    bf16 = jnp.bfloat16
    axes = ("fsdp", "dp")
    me = device_index()
    core = lax.axis_index("dp") % 2
    slots = conditions.shape[0]
    images = slots * DEVICES
    length = GRID * GRID
    rows_all = slots * length
    cond_count = slots * D
    bias_count = bias_flat.shape[0]
    packed_rows = -(-(cond_count + bias_count) // 128)
    packed = jnp.concatenate(
        [
            conditions.reshape(-1),
            bias_flat,
            jnp.zeros(packed_rows * 128 - cond_count - bias_count, bf16),
        ]
    ).reshape(packed_rows, 128)
    pieces_a = cut_pieces(weight_flat, PLAN_A)
    packed, pieces_a = lax.optimization_barrier((packed, pieces_a))
    gathered = gathered_weights(pieces_a, cut_pieces(weight_flat, PLAN_B))
    packed_all = gather_columns(gather_column(packed)).reshape(DEVICES, -1)
    cond_all = packed_all[:, :cond_count].reshape(images, D).astype(f32)
    places = lax.broadcasted_iota(jnp.int32, (DEVICES, DEVICES), 0)
    others = lax.broadcasted_iota(jnp.int32, (DEVICES, DEVICES), 1)
    chosen = ((places ^ me) == others).astype(bf16)
    bias_all = jnp.dot(
        chosen, packed_all[:, cond_count : cond_count + bias_count], preferred_element_type=f32
    ).reshape(-1)
    b_qkv = bias_all[: 3 * D]
    b_out = bias_all[3 * D : 4 * D]
    b_mlp = bias_all[4 * D : 4 * D + 2 * FF]
    b_ada = bias_all[4 * D + 2 * FF :]
    ada_local = weight_flat.reshape(ADA_ROWS, 6 * D)
    ada_start = jnp.clip(
        me * ADA_ROWS - FIRST_ADA * 128 // (6 * D) + ADA_ROWS, 0, D + ADA_ROWS
    )
    cond_act = jax.nn.silu(cond_all).astype(bf16)
    cond_rows = lax.dynamic_slice_in_dim(
        jnp.pad(cond_act.T, ((ADA_ROWS, ADA_ROWS), (0, 0))), ada_start, ADA_ROWS, 0
    )
    terms = jnp.einsum("km,kn->mn", cond_rows, ada_local, preferred_element_type=f32)
    modulation = sum_to_owners(terms.reshape(DEVICES, slots, 6 * D)) + b_ada
    w_qkv, w_out = split_a(gathered)

    def share(array):
        return (array, lax.ppermute(array, "dp", SWAP_CORE))

    cosines, sines = [jnp.tile(table[:, 0], (1, HEADS)) for table in rope_tables()]
    mask_f = slot_mask.astype(f32)[:, None, None]
    x_f = tokens.astype(f32).reshape(slots, length, D)
    shift_a, scale_a, gate_a, shift_b, scale_b, gate_b = [
        modulation[:, None, place * D : (place + 1) * D] for place in range(6)
    ]
    g_out = cotangent.astype(f32).reshape(slots, length, D) * mask_f
    g_branch_b = (gate_b * g_out).astype(bf16).reshape(rows_all, D)
    normed_a, inv_a = norm_parts(x_f)
    input_a = (normed_a * (1.0 + scale_a) + shift_a).astype(bf16).reshape(rows_all, D)
    projected = jnp.dot(input_a, w_qkv, preferred_element_type=f32) + b_qkv
    queries, keys, values, attended, log_total = attention_forward(projected, cosines, sines)
    branch_a = (jnp.dot(attended, w_out, preferred_element_type=f32) + b_out).reshape(
        slots, length, D
    )
    middle = x_f + gate_a * branch_a
    normed_b, inv_b = norm_parts(middle)
    input_b = (normed_b * (1.0 + scale_b) + shift_b).astype(bf16).reshape(rows_all, D)
    early = [share(array) for array in (input_a, attended, input_b, g_branch_b)]
    hidden, g_gate, g_up, branch_b, g_input_b, sum_gate, sum_up = mlp_both_ways(
        input_b, g_branch_b, b_mlp.reshape(1, 2 * FF), gathered
    )
    shared_mlp = [share(array) for array in (g_gate, g_up, hidden)]
    branch_b = branch_b.reshape(slots, length, D)
    g_input_b = g_input_b.reshape(slots, length, D)
    out = ((middle + gate_b * branch_b) * mask_f).astype(bf16).reshape(rows_all, D)
    g_gate_b = jnp.sum(g_out * branch_b, axis=1)
    g_shift_b = jnp.sum(g_input_b, axis=1)
    g_scale_b = jnp.sum(g_input_b * normed_b, axis=1)
    g_middle = g_out + norm_back(g_input_b * (1.0 + scale_b), normed_b, inv_b)
    g_branch_a = (gate_a * g_middle).astype(bf16).reshape(rows_all, D)
    g_gate_a = jnp.sum(g_middle * branch_a, axis=1)
    grad_b_out = jnp.sum(g_branch_a.astype(f32), axis=0)
    shared_branch_a = share(g_branch_a)
    grads_b = lax.cond(
        core == 0,
        lambda: grads_b_core_0(early[2], shared_mlp[0], shared_mlp[1]),
        lambda: grads_b_core_1(early[2], *shared_mlp, early[3]),
    )
    orders = (SWAP_Y, SWAP_X), (SWAP_X, SWAP_Y)
    sends_b = first_sends(grads_b, BLOCK_B)
    arrived = over_planes(sends_b, orders[0])
    g_attended = jnp.einsum("re,de->rd", g_branch_a, w_out, preferred_element_type=f32)
    g_attended = after(g_attended.astype(bf16), sends_b)
    g_projected, proj_sums = attention_backward(
        projected, queries, keys, values, log_total, g_attended, cosines, sines
    )
    grad_b_qkv = jnp.sum(proj_sums, axis=(0, 1))
    shared_proj = share(g_projected)
    kept_b, sends_b = second_sends(grads_b, after(arrived, g_projected), BLOCK_B)
    g_projected, shared_proj = after((g_projected, shared_proj), sends_b)
    g_input_a = jnp.einsum("re,de->rd", g_projected, w_qkv, preferred_element_type=f32)
    g_input_a = lax.optimization_barrier(g_input_a).reshape(slots, length, D)
    g_shift_a = jnp.sum(g_input_a, axis=1)
    g_scale_a = jnp.sum(g_input_a * normed_a, axis=1)
    g_modulation = jnp.concatenate(
        [g_shift_a, g_scale_a, g_gate_a, g_shift_b, g_scale_b, g_gate_b], axis=1
    ).astype(bf16)
    bias_sums = [grad_b_qkv, grad_b_out, sum_gate.reshape(-1), sum_up.reshape(-1)]
    small = jnp.concatenate([g_modulation.reshape(-1)] + [b.astype(bf16) for b in bias_sums])
    shared_proj = after(shared_proj, small)
    small_all = lax.all_gather(small.reshape(-1, 128), axes, axis=0, tiled=False).reshape(
        DEVICES, -1
    )
    made_a = lax.cond(
        core == 0,
        lambda: grads_a(0, early[0], shared_proj, early[1], shared_branch_a),
        lambda: grads_a(1, early[0], shared_proj, early[1], shared_branch_a),
    )
    sends_a = first_sends(made_a, BLOCK_A)
    planes_b = plane_sums(kept_b, after(over_planes(sends_b, orders[1]), sends_a))
    sends_b = line_sends(planes_b)
    arrived = after(over_planes(sends_a, orders[0]), sends_b)
    kept_a, sends_a = second_sends(made_a, arrived, BLOCK_A)
    line_b = after(from_line(sends_b), sends_a)
    grad_tokens = g_middle + norm_back(g_input_a * (1.0 + scale_a), normed_a, inv_a)
    sum_b = sum_line(sends_b[0], line_b).astype(bf16)
    halves = sum_b.reshape(2, BLOCK_B // 2, 128)
    sum_b = jnp.where(
        jnp.logical_not(is_kind(PLACE_B, MLP_BLOCKS)),
        jnp.concatenate(
            [from_tiles(half, 24).reshape(-1, 24, 128) for half in halves], axis=1
        ).reshape(-1, 128),
        jnp.pad(
            from_tiles(halves[:, : USED_DOWN // 2].reshape(-1, 128), 9),
            ((0, BLOCK_B - USED_DOWN), (0, 0)),
        ),
    )
    planes_a = plane_sums(kept_a, after(over_planes(sends_a, orders[1]), sum_b))
    sends_a = line_sends(planes_a)
    back_b = send_back(after(sum_b, sends_a), PLAN_B, PLACE_B)
    sum_a = sum_line(sends_a[0], after(from_line(sends_a), back_b)).astype(bf16)
    sum_a = jnp.where(is_kind(PLACE_A, QKV_BLOCKS), from_tiles(sum_a, 9), from_tiles(sum_a, 27))
    back_a = send_back(sum_a, PLAN_A, PLACE_A)
    g_mod_all = (
        jnp.dot(chosen, small_all[:, : slots * 6 * D], preferred_element_type=f32)
        .astype(bf16)
        .reshape(images, 6 * D)
    )
    grad_biases = jnp.concatenate(
        [
            jnp.sum(small_all[:, slots * 6 * D :].astype(f32), axis=0),
            jnp.sum(g_mod_all.astype(f32), axis=0),
        ]
    )
    part_biases = lax.dynamic_slice_in_dim(grad_biases, me * bias_count, bias_count, 0)
    grad_ada = jnp.einsum("km,mn->kn", cond_rows, g_mod_all, preferred_element_type=f32)
    g_cond_rows = jnp.einsum("mn,kn->mk", g_mod_all, ada_local, preferred_element_type=f32)
    rows_of_all = lax.all_gather(
        jnp.pad(g_cond_rows, ((0, 0), (0, 128 - ADA_ROWS))), axes, axis=0, tiled=False
    )
    came = jnp.where(
        (jnp.arange(DEVICES)[:, None] ^ me) == jnp.arange(DEVICES)[None, :], 1.0, 0.0
    )[:, :, None, None] * rows_of_all[:, :, :ADA_ROWS].reshape(DEVICES, DEVICES, slots, ADA_ROWS)
    came = jnp.sum(came, axis=1)
    first = FIRST_ADA * 128 // (6 * D)
    g_cond = came.transpose(1, 0, 2).reshape(slots, DEVICES * ADA_ROWS)[:, first : first + D]
    cond_f = conditions.astype(f32)
    sigma_cond = jax.nn.sigmoid(cond_f)
    grad_conditions = g_cond * sigma_cond * (1.0 + cond_f * (1.0 - sigma_cond))
    part_weights = owned_rows(back_a, back_b, grad_ada.reshape(SHARD, 128))
    return (out, grad_tokens.reshape(rows_all, D), grad_conditions, part_weights, part_biases)


def solution(mesh):
    chosen = on_device_32 if dict(mesh.shape) == {"fsdp": 4, "dp": 8} else on_device_plain
    return jax.shard_map(
        chosen,
        mesh=mesh,
        in_specs=(
            P(("fsdp", "dp"), None),
            P(("fsdp", "dp"), None),
            P(("fsdp", "dp"), None),
            P(("fsdp", "dp")),
            P(("fsdp", "dp"), None),
            P(("fsdp", "dp")),
        ),
        out_specs=(
            P(("fsdp", "dp"), None),
            P(("fsdp", "dp"), None),
            P(("fsdp", "dp"), None),
            P(("fsdp", "dp"), None),
            P(("fsdp", "dp")),
        ),
        check_vma=False,
    )
```

```python
import math

import jax
import jax.numpy as jnp
from jax import lax
from jax.experimental import pallas as pl
from jax.experimental.pallas import tpu as pltpu
import numpy as np
from jax.sharding import PartitionSpec as P

D = 1152
HEADS = 16
HEAD_DIM = 72
FF = 3072
GRID = 16


eps_norm = 1e-06


def unpack_weights(weight_all, bias_all):
    flat = weight_all.reshape(-1)
    layouts = ((D, 3 * D), (D, D), (D, 2 * FF), (D, 6 * D), (FF, D))
    pieces = []
    offset = 0
    for layout in layouts:
        amount = layout[0] * layout[1]
        pieces.append(flat[offset : offset + amount].reshape(layout))
        offset = offset + amount
    offset = 0
    for amount in (3 * D, D, 2 * FF, 6 * D):
        pieces.append(bias_all[offset : offset + amount])
        offset = offset + amount
    return tuple(pieces)


def rope_tables():
    quarter = HEAD_DIM // 4
    places = jnp.arange(GRID * GRID, dtype=jnp.int32)
    rows_at = (places // GRID).astype(jnp.float32)
    cols_at = (places % GRID).astype(jnp.float32)
    freqs = 10000.0 ** (-jnp.arange(quarter, dtype=jnp.float32) / quarter)
    along_rows = rows_at[:, None] * freqs[None, :]
    along_cols = cols_at[:, None] * freqs[None, :]
    angles = jnp.concatenate([along_rows, along_rows, along_cols, along_cols], axis=1)
    return (jnp.cos(angles)[:, None, :], jnp.sin(angles)[:, None, :])


def turn_half(values):
    quarter = values.shape[-1] // 4
    first = values[..., :quarter]
    second = values[..., quarter : 2 * quarter]
    third = values[..., 2 * quarter : 3 * quarter]
    fourth = values[..., 3 * quarter :]
    return jnp.concatenate([-second, first, -fourth, third], axis=-1)


def norm_parts(values):
    centred = values - jnp.mean(values, -1, keepdims=True)
    inverse = lax.rsqrt(jnp.mean(centred * centred, -1, keepdims=True) + eps_norm)
    return (centred * inverse, inverse)


def norm_back(grad_normed, normed, inverse):
    return inverse * (
        grad_normed
        - jnp.mean(grad_normed, -1, keepdims=True)
        - normed * jnp.mean(grad_normed * normed, -1, keepdims=True)
    )


def rms_parts(values):
    inverse = lax.rsqrt(jnp.mean(values * values, -1, keepdims=True) + eps_norm)
    return (values * inverse, inverse)


def rms_back(grad_normed, normed, inverse):
    return inverse * (grad_normed - normed * jnp.mean(grad_normed * normed, -1, keepdims=True))


def compute_block(tokens, cotangent, slot_mask, modulation, weights, biases):
    f32 = jnp.float32
    bf16 = jnp.bfloat16
    w_qkv, w_out, w_mlp, w_down = weights
    b_qkv, b_out, b_mlp = biases
    slots = slot_mask.shape[0]
    length = GRID * GRID
    rows_all = slots * length
    scale = 1.0 / math.sqrt(HEAD_DIM)
    heads_shape = (slots, length, HEADS, HEAD_DIM)
    cosines, sines = rope_tables()
    mask_f = slot_mask.astype(f32)[:, None, None]
    x_f = tokens.astype(f32).reshape(slots, length, D)
    shift_a, scale_a, gate_a, shift_b, scale_b, gate_b = [
        modulation[:, None, place * D : (place + 1) * D] for place in range(6)
    ]
    normed_a, inv_a = norm_parts(x_f)
    attention_input = (normed_a * (1.0 + scale_a) + shift_a).astype(bf16).reshape(rows_all, D)
    projected_output = (
        jnp.dot(attention_input, w_qkv, preferred_element_type=f32) + b_qkv.astype(f32)
    ).reshape(slots, length, 3 * D)
    q_norm, inv_q = rms_parts(projected_output[..., :D].reshape(heads_shape))
    k_norm, inv_k = rms_parts(projected_output[..., D : 2 * D].reshape(heads_shape))
    queries = (q_norm * cosines + turn_half(q_norm) * sines).astype(bf16)
    keys = (k_norm * cosines + turn_half(k_norm) * sines).astype(bf16)
    values = projected_output[..., 2 * D :].reshape(heads_shape).astype(bf16)
    scores = jnp.einsum("slhe,smhe->shlm", queries, keys, preferred_element_type=f32) * scale
    row_max = jnp.max(scores, -1, keepdims=True)
    log_total = row_max + jnp.log(jnp.sum(jnp.exp(scores - row_max), -1, keepdims=True))
    probs_low = jnp.exp(scores - log_total).astype(bf16)
    attention_output = (
        jnp.einsum("shlm,smhe->slhe", probs_low, values, preferred_element_type=f32)
        .astype(bf16)
        .reshape(rows_all, D)
    )
    attention_branch = (
        jnp.dot(attention_output, w_out, preferred_element_type=f32) + b_out.astype(f32)
    ).reshape(slots, length, D)
    middle = x_f + gate_a * attention_branch
    normed_b, inv_b = norm_parts(middle)
    feedforward_input = (normed_b * (1.0 + scale_b) + shift_b).astype(bf16).reshape(rows_all, D)
    mixed_tokens = jnp.dot(feedforward_input, w_mlp, preferred_element_type=f32) + b_mlp.astype(
        f32
    )
    gate_part = mixed_tokens[:, :FF]
    up_part = mixed_tokens[:, FF:]
    hidden_state = (jax.nn.silu(gate_part) * up_part).astype(bf16)
    feedforward_branch = jnp.dot(hidden_state, w_down, preferred_element_type=f32).reshape(
        slots, length, D
    )
    out = ((middle + gate_b * feedforward_branch) * mask_f).astype(bf16).reshape(rows_all, D)
    g_out = cotangent.astype(f32).reshape(slots, length, D) * mask_f
    g_branch_b = (gate_b * g_out).astype(bf16).reshape(rows_all, D)
    g_gate_b = jnp.sum(g_out * feedforward_branch, axis=1)
    g_hidden = jnp.einsum("rd,fd->rf", g_branch_b, w_down, preferred_element_type=f32)
    sigma_gate = jax.nn.sigmoid(gate_part)
    g_mixed = jnp.concatenate(
        [
            g_hidden * up_part * sigma_gate * (1.0 + gate_part * (1.0 - sigma_gate)),
            g_hidden * (gate_part * sigma_gate),
        ],
        axis=1,
    ).astype(bf16)
    grad_b_mlp = jnp.sum(g_mixed.astype(f32), axis=0)
    g_input_b = jnp.einsum("rf,df->rd", g_mixed, w_mlp, preferred_element_type=f32).reshape(
        slots, length, D
    )
    g_shift_b = jnp.sum(g_input_b, axis=1)
    g_scale_b = jnp.sum(g_input_b * normed_b, axis=1)
    g_middle = g_out + norm_back(g_input_b * (1.0 + scale_b), normed_b, inv_b)
    g_branch_a = (gate_a * g_middle).astype(bf16).reshape(rows_all, D)
    g_gate_a = jnp.sum(g_middle * attention_branch, axis=1)
    grad_b_out = jnp.sum(g_branch_a.astype(f32), axis=0)
    g_attended = (
        jnp.einsum("re,de->rd", g_branch_a, w_out, preferred_element_type=f32)
        .astype(bf16)
        .reshape(heads_shape)
    )
    scores = jnp.einsum("slhe,smhe->shlm", queries, keys, preferred_element_type=f32) * scale
    probs = jnp.exp(scores - log_total)
    probs_low = probs.astype(bf16)
    g_probs = jnp.einsum("slhe,smhe->shlm", g_attended, values, preferred_element_type=f32)
    g_values = jnp.einsum("shlm,slhe->smhe", probs_low, g_attended, preferred_element_type=f32)
    g_scores = (probs * (g_probs - jnp.sum(probs * g_probs, -1, keepdims=True))).astype(bf16)
    g_queries = jnp.einsum("shlm,smhe->slhe", g_scores, keys, preferred_element_type=f32) * scale
    g_keys = jnp.einsum("shlm,slhe->smhe", g_scores, queries, preferred_element_type=f32) * scale
    g_q = rms_back(g_queries * cosines - turn_half(g_queries) * sines, q_norm, inv_q)
    g_k = rms_back(g_keys * cosines - turn_half(g_keys) * sines, k_norm, inv_k)
    g_projected = jnp.concatenate(
        [g_q.reshape(rows_all, D), g_k.reshape(rows_all, D), g_values.reshape(rows_all, D)], axis=1
    ).astype(bf16)
    grad_b_qkv = jnp.sum(g_projected.astype(f32), axis=0)
    g_input_a = jnp.einsum("re,de->rd", g_projected, w_qkv, preferred_element_type=f32).reshape(
        slots, length, D
    )
    g_shift_a = jnp.sum(g_input_a, axis=1)
    g_scale_a = jnp.sum(g_input_a * normed_a, axis=1)
    grad_tokens = g_middle + norm_back(g_input_a * (1.0 + scale_a), normed_a, inv_a)
    g_modulation = jnp.concatenate(
        [g_shift_a, g_scale_a, g_gate_a, g_shift_b, g_scale_b, g_gate_b], axis=1
    ).astype(bf16)
    pairs = (
        (attention_input, g_projected),
        (attention_output, g_branch_a),
        (feedforward_input, g_mixed),
        (hidden_state, g_branch_b),
    )
    return (
        out,
        grad_tokens.reshape(rows_all, D),
        g_modulation,
        (grad_b_qkv, grad_b_out, grad_b_mlp),
        pairs,
    )


def weight_grad(pair):
    return jnp.einsum("rd,re->de", pair[0], pair[1], preferred_element_type=jnp.float32)


def on_device_plain(tokens, conditions, cotangent, slot_mask, weight_flat, bias_flat):
    f32 = jnp.float32
    bf16 = jnp.bfloat16
    axes = ("fsdp", "dp")
    weight_all = lax.all_gather(weight_flat, axes, axis=0, tiled=True)
    bias_all = lax.all_gather(bias_flat, axes, axis=0, tiled=True)
    w_qkv, w_out, w_mlp, w_ada, w_down, b_qkv, b_out, b_mlp, b_ada = unpack_weights(
        weight_all, bias_all
    )
    cond_f = conditions.astype(f32)
    cond_act = jax.nn.silu(cond_f).astype(bf16)
    modulation = jnp.dot(cond_act, w_ada, preferred_element_type=f32) + b_ada.astype(f32)
    out, grad_tokens, g_modulation, bias_sums, pairs = compute_block(
        tokens,
        cotangent,
        slot_mask,
        modulation,
        (w_qkv, w_out, w_mlp, w_down),
        (b_qkv, b_out, b_mlp),
    )
    grad_b_ada = jnp.sum(g_modulation.astype(f32), axis=0)
    g_cond = jnp.einsum("se,de->sd", g_modulation, w_ada, preferred_element_type=f32)
    sigma_cond = jax.nn.sigmoid(cond_f)
    grad_conditions = g_cond * sigma_cond * (1.0 + cond_f * (1.0 - sigma_cond))
    grad_qkv, grad_out, grad_mlp, grad_down = [weight_grad(pair) for pair in pairs]
    grad_ada = weight_grad((cond_act, g_modulation))
    grads_big = jnp.concatenate(
        [
            grad.astype(bf16).reshape(-1)
            for grad in (grad_qkv, grad_out, grad_mlp, grad_ada, grad_down)
        ]
    ).reshape(-1, 128)
    grads_small = jnp.concatenate([*bias_sums, grad_b_ada])
    part_weights = lax.psum_scatter(grads_big, axes, scatter_dimension=0, tiled=True)
    part_biases = lax.psum_scatter(grads_small, axes, scatter_dimension=0, tiled=True)
    return (out, grad_tokens, grad_conditions, part_weights.astype(f32), part_biases)


ROWS_QKV = 3 * D * D // 128
ROWS_OUT = D * D // 128
ROWS_MLP = 2 * D * FF // 128
ROWS_ADA = 6 * D * D // 128
ROWS_DOWN = D * FF // 128
FIRST_MLP = ROWS_QKV + ROWS_OUT
FIRST_ADA = FIRST_MLP + ROWS_MLP
FIRST_DOWN = FIRST_ADA + ROWS_ADA
DEVICES = 32
SHARD = 5832
BLOCK_A = 1296
BLOCK_B = 2688
USED_DOWN = 2592
MLP_BLOCKS = 21
QKV_BLOCKS = 24
ADA_ROWS = SHARD * 128 // (6 * D)


def block_a_range(block):
    return (BLOCK_A * block, BLOCK_A * (block + 1))


def block_b_range(block):
    if block < MLP_BLOCKS:
        first = FIRST_MLP + BLOCK_B * block
        return (first, min(first + BLOCK_B, FIRST_ADA))
    first = FIRST_DOWN + USED_DOWN * (block - MLP_BLOCKS)
    return (first, min(first + USED_DOWN, FIRST_DOWN + ROWS_DOWN))


def plan_rounds(block_range, first_block, count, device_of_block):
    rounds = []
    for k in range(count):
        pairs = []
        for owner in range(DEVICES):
            block = first_block(owner) + k
            if 0 <= block < DEVICES:
                first, last = block_range(block)
                if first < (owner + 1) * SHARD and last > owner * SHARD:
                    pairs.append((owner, device_of_block(block)))
        rounds.append(pairs)
    return rounds


DOWN_OWNER = FIRST_DOWN // SHARD


def first_block_a(owner):
    return owner * SHARD // BLOCK_A


def first_block_b(owner):
    if owner < DOWN_OWNER:
        return (owner * SHARD - FIRST_MLP) // BLOCK_B
    return MLP_BLOCKS + max((owner * SHARD - FIRST_DOWN) // USED_DOWN, -1)


def starts_a():
    return -(device_index() * SHARD % BLOCK_A), BLOCK_A


def starts_b():
    me = device_index()
    low = me >= DOWN_OWNER
    first = jnp.where(low, FIRST_DOWN, FIRST_MLP)
    step = jnp.where(low, USED_DOWN, BLOCK_B)
    return -((me * SHARD - first) % step), step


PLAN_A = (BLOCK_A, block_a_range, first_block_a, 5, starts_a)
PLAN_B = (BLOCK_B, block_b_range, first_block_b, 4, starts_b)


def device_index():
    return lax.axis_index("fsdp") * lax.axis_size("dp") + lax.axis_index("dp")


def cut_pieces(shard, plan):
    block_rows, _, _, count, starts = plan
    padded = jnp.pad(shard, ((block_rows, block_rows), (0, 0)))
    first, step = starts()
    return [
        lax.dynamic_slice_in_dim(padded, block_rows + first + k * step, block_rows, 0)
        for k in range(count)
    ]


def spread(pieces, plan):
    _, block_range, first_block, count, _ = plan
    rounds = plan_rounds(block_range, first_block, count, lambda block: block)
    total = None
    for piece, pairs in zip(pieces, rounds, strict=True):
        got = lax.ppermute(piece, ("fsdp", "dp"), pairs)
        total = got if total is None else total + got
    return total


def send_back(block, plan, places):
    _, block_range, first_block, count, _ = plan
    rounds = plan_rounds(block_range, first_block, count, lambda block: device_of(places, block))
    return [
        lax.ppermute(block, ("fsdp", "dp"), [(device, owner) for owner, device in pairs])
        for pairs in rounds
    ]


def to_tiles(rows, chunks):
    return (
        rows.reshape(-1, 8, chunks, 128).transpose(0, 2, 1, 3).reshape(-1, 128)
    )


def from_tiles(rows, chunks):
    return (
        rows.reshape(-1, chunks, 8, 128).transpose(0, 2, 1, 3).reshape(-1, 128)
    )


def matrix_of_tiles(rows, height, width):
    return (
        rows.reshape(height // 8, width // 128, 8, 128)
        .transpose(0, 2, 1, 3)
        .reshape(height, width)
    )


def tiles_of_matrix(matrix):
    height, width = matrix.shape
    return (
        matrix.reshape(height // 8, 8, width // 128, 128)
        .transpose(0, 2, 1, 3)
        .reshape(-1, 128)
    )


SWAP_X = [(0, 1), (1, 0), (2, 3), (3, 2)]
SWAP_Y = [(0, 2), (2, 0), (1, 3), (3, 1)]
SWAP_CORE = [(d, d ^ 1) for d in range(8)]


def along_z(pairs):
    return [(2 * a + e, 2 * b + e) for a, b in pairs for e in range(2)]


def chips_of(*lines):
    place = {}
    for z, line in enumerate(lines):
        for f, block in enumerate(line):
            place[block] = 4 * f + z
    return place


PLACE_A = (
    chips_of((0, 1, 2, 3), (4, 5, 6, 7), (18, 19, 20, 21), (22, 23, 16, 17)),
    chips_of((8, 9, 10, 11), (12, 13, 14, 15), (24, 25, 26, 27), (28, 29, 30, 31)),
)
PLACE_B = (
    chips_of((2, 3, 4, 5), (6, 7, 8, 9), (10, 11, 12, 13), (14, 0, 15, 1)),
    chips_of((20, 16, 17, 18), (21, 22, 23, 24), (25, 26, 27, 28), (29, 19, 30, 31)),
)


def device_of(places, block):
    core = 0 if block in places[0] else 1
    return 2 * places[core][block] + core


def is_kind(places, first_of_second):
    mask = sum(1 << device_of(places, block) for block in range(first_of_second, DEVICES))
    bits = jnp.uint32(mask) >> device_index().astype(jnp.uint32)
    return bits % 2 == 1


def add_low(a, b):
    return (a.astype(jnp.float32) + b.astype(jnp.float32)).astype(jnp.bfloat16)


def pick(array, index, axis):
    return lax.dynamic_index_in_dim(array, index, axis, keepdims=False)


def first_sends(grads, block_rows):
    f = lax.axis_index("fsdp")
    y, x = f // 2, f % 2
    a, b = [part.reshape(2, 2, 4, block_rows // 2, 128) for part in grads]
    return pick(a, 1 - y, 0), pick(b, 1 - x, 1)


def over_planes(sends, axes):
    return [lax.ppermute(send, "fsdp", axis) for send, axis in zip(sends, axes, strict=True)]


def second_sends(grads, arrived, block_rows):
    f = lax.axis_index("fsdp")
    y, x = f // 2, f % 2
    a, b = [part.reshape(2, 2, 4, block_rows // 2, 128) for part in grads]
    a = add_low(pick(a, y, 0), arrived[0])
    b = add_low(pick(b, x, 1), arrived[1])
    return (pick(a, x, 0), pick(b, y, 0)), (pick(a, 1 - x, 0), pick(b, 1 - y, 0))


def plane_sums(kept, arrived):
    return jnp.concatenate([add_low(k, a) for k, a in zip(kept, arrived, strict=True)], axis=1)


def after(value, *others):
    return lax.optimization_barrier((value, others))[0]


def line_sends(planes):
    z = lax.axis_index("dp") // 2
    return [pick(planes, z ^ k, 0) for k in range(4)]


def from_line(sends):
    return [
        lax.ppermute(sends[k], "dp", [(d, d ^ (2 * k)) for d in range(8)]) for k in range(1, 4)
    ]


def sum_line(own, others):
    total = own.astype(jnp.float32)
    for other in others:
        total += other.astype(jnp.float32)
    return total


def gather_column(array):
    parts = [array] + [
        lax.ppermute(array, "dp", [(d, d ^ k) for d in range(8)]) for k in range(1, 8)
    ]
    return jnp.stack(parts)


def gather_columns(part):
    parts = [part] + [
        lax.ppermute(part, "fsdp", [(f, f ^ k) for f in range(4)]) for k in range(1, 4)
    ]
    return jnp.stack(parts).reshape(DEVICES, *part.shape[1:])


ADA_GROUPS = range(FIRST_ADA // (8 * SHARD), (FIRST_DOWN - 1) // (8 * SHARD) + 1)


def sum_to_owners(terms):
    def send(array, change, groups):
        pairs = [(8 * f + d, (8 * f + d) ^ change) for f in groups for d in range(8)]
        return lax.ppermute(array, ("fsdp", "dp"), pairs)

    terms = terms.reshape(4, 4, 2, *terms.shape[1:])
    terms = terms[:, :, 0] + send(terms[:, :, 1], 1, ADA_GROUPS)
    terms = terms[0] + sum(send(terms[k], 8 * k, ADA_GROUPS) for k in range(1, 4))
    return terms[0] + sum(send(terms[k], 2 * k, range(4)) for k in range(1, 4))


def mlp_both_ways(x, g, bias, gathered):
    f32, bf16 = jnp.float32, jnp.bfloat16
    rows = x.shape[0]
    tile = 512
    steps = FF // tile
    full = BLOCK_B // 8
    used = USED_DOWN // 8
    wide = 2 * FF // 128
    chunks = D // 128
    across = (((1,), (1,)), ((), ()))

    def body(x_ref, g_ref, bias_g_ref, bias_u_ref, source, *rest):
        hid_ref, gg_ref, gu_ref, branch_ref, gin_ref, sum_g_ref, sum_u_ref, *rest = rest
        mix_ref, down_ref, sem = rest
        step = pl.program_id(0)

        def each(act):
            stride = (BLOCK_A + BLOCK_B) // 8
            for i in range(DEVICES):
                first = i * stride + BLOCK_A // 8
                if i < MLP_BLOCKS:
                    piece = source.at[pl.ds(first, full)]
                    flat = mix_ref.reshape(MLP_BLOCKS * full, 8, 128)
                    target = flat.at[pl.ds(i * full, full)]
                else:
                    piece = source.at[pl.ds(first, used)]
                    target = down_ref.at[pl.ds((i - MLP_BLOCKS) * used, used)]
                act(pltpu.make_async_copy(piece, target, sem.at[i]))

        @pl.when(step == 0)
        def _():
            each(lambda copy: copy.start())
            branch_ref[...] = jnp.zeros_like(branch_ref)
            gin_ref[...] = jnp.zeros_like(gin_ref)
            each(lambda copy: copy.wait())

        def columns(first):
            return jnp.concatenate(
                [
                    mix_ref[: D // 8, first + i].reshape(D, 128)
                    for i in range(tile // 128)
                ],
                axis=1,
            )

        x = x_ref[...]
        w_gate, w_up = columns(tile // 128 * step), columns(wide // 2 + tile // 128 * step)
        gate = jnp.dot(x, w_gate, preferred_element_type=f32) + bias_g_ref[...]
        up = jnp.dot(x, w_up, preferred_element_type=f32) + bias_u_ref[...]
        sigma = jax.nn.sigmoid(gate)
        silu = gate * sigma
        hid = (silu * up).astype(bf16)
        hid_ref[...] = hid
        groups = tile // 8
        low_rows = down_ref[pl.ds(step * groups * chunks, groups * chunks)]
        low_rows = low_rows.reshape(groups, chunks, 8, 128)
        w_down = jnp.concatenate([low_rows[:, j].reshape(tile, 128) for j in range(chunks)], axis=1)
        branch_ref[...] += jnp.dot(hid, w_down, preferred_element_type=f32)
        g_hid = lax.dot_general(g_ref[...], w_down, across, preferred_element_type=f32)
        g_gate = (g_hid * up * sigma * (1.0 + gate * (1.0 - sigma))).astype(bf16)
        g_up = (g_hid * silu).astype(bf16)
        gg_ref[...] = g_gate
        gu_ref[...] = g_up
        sum_g_ref[...] = jnp.sum(g_gate.astype(f32), axis=0, keepdims=True)
        sum_u_ref[...] = jnp.sum(g_up.astype(f32), axis=0, keepdims=True)
        gin_ref[...] += lax.dot_general(
            g_gate, w_gate, across, preferred_element_type=f32
        ) + lax.dot_general(g_up, w_up, across, preferred_element_type=f32)

    whole = pl.BlockSpec((rows, D), lambda t: (0, 0))
    part = pl.BlockSpec((rows, tile), lambda t: (0, t))
    line = pl.BlockSpec((1, tile), lambda t: (0, t))
    return pl.pallas_call(
        body,
        grid=(steps,),
        in_specs=[
            whole,
            whole,
            line,
            pl.BlockSpec((1, tile), lambda t: (0, steps + t)),
            pl.BlockSpec(memory_space=pl.ANY),
        ],
        out_specs=[part, part, part, whole, whole, line, line],
        out_shape=[jax.ShapeDtypeStruct((rows, FF), bf16)] * 3
        + [jax.ShapeDtypeStruct((rows, D), f32)] * 2
        + [jax.ShapeDtypeStruct((1, FF), f32)] * 2,
        scratch_shapes=[
            pltpu.VMEM((MLP_BLOCKS * full // wide, wide, 8, 128), bf16),
            pltpu.VMEM(((DEVICES - MLP_BLOCKS) * used, 8, 128), bf16),
            pltpu.SemaphoreType.DMA((DEVICES,)),
        ],
        cost_estimate=pl.CostEstimate(
            flops=12 * rows * D * FF, bytes_accessed=30_000_000, transcendentals=rows * FF
        ),
        compiler_params=pltpu.CompilerParams(vmem_limit_bytes=56 << 20),
        name="mlp_both_ways",
    )(x, g, bias, bias, gathered)


def pair_product(xo, xp, go, gp):
    down = (((0,), (0,)), ((), ()))
    total = lax.dot_general(xo[...], go[...], down, preferred_element_type=jnp.float32)
    total += lax.dot_general(xp[...], gp[...], down, preferred_element_type=jnp.float32)
    return total.astype(jnp.bfloat16)


def store_tiles(out_ref, lead, first, value):
    for j in range(value.shape[1] // 128):
        out_ref[(*lead, first + j)] = value[:, 128 * j : 128 * (j + 1)]


def grads_b_core_0(in_b, g_gate, g_up):
    def body(xo, xp, gog, gpg, gou, gpu, *outs):
        for out_ref, go, gp in ((outs[0], gog, gpg), (outs[1], gou, gpu)):
            value = pair_product(xo, xp, go, gp)
            for j in range(4):
                part = value[:, 128 * j : 128 * (j + 1)].reshape(16, 7, 8, 128)
                for block in range(16):
                    out_ref[PLACE_B[0][block], :, j] = part[block]

    rows = in_b[0].shape[0]
    high = 16 * 56
    x_spec = pl.BlockSpec((rows, high), lambda t: (0, 0))
    g_spec = pl.BlockSpec((rows, 512), lambda t: (0, t))
    out = pl.pallas_call(
        body,
        grid=(FF // 512,),
        in_specs=[x_spec] * 2 + [g_spec] * 4,
        out_specs=[pl.BlockSpec((16, 7, 4, 8, 128), lambda t: (0, 0, t, 0, 0))] * 2,
        out_shape=[jax.ShapeDtypeStruct((16, 7, FF // 128, 8, 128), jnp.bfloat16)] * 2,
        compiler_params=pltpu.CompilerParams(vmem_limit_bytes=44 << 20),
        name="grads_b_core_0",
    )(*in_b, *g_gate, *g_up)
    return [part.reshape(-1, 128) for part in out]


def grads_b_core_1(in_b, g_gate, g_up, hidden, g_branch):
    bf16 = jnp.bfloat16
    rows = in_b[0].shape[0]
    mlp_steps = FF // 512
    wide = 384
    down_steps = FF // wide
    half_tiles = BLOCK_B // 16
    mlp_groups = (D - 16 * 56) // 8
    groups = (MLP_BLOCKS - 16) * 7
    half_groups = USED_DOWN // 9 // 16
    down_blocks = DEVICES - MLP_BLOCKS

    place = PLACE_B[1]

    def body(place_ref, xo7, xo8, xp7, xp8, gog, gpg, gou, gpu, ho, hp, go, gp, *outs):
        step = pl.program_id(0)

        @pl.when(step == 0)
        def _():
            for group in range(mlp_groups, groups):
                first = place[16 + group // 7] * half_tiles + group % 7 * (FF // 128)
                for out_ref in outs:
                    out_ref[pl.ds(first, FF // 128)] = jnp.zeros((FF // 128, 8, 128), bf16)
            for block in range(down_blocks):
                for half in range(2):
                    used = min(half_groups, FF // 8 - (2 * block + half) * half_groups) * 9
                    first = place[MLP_BLOCKS + block] * half_tiles + used
                    rest = half_tiles - used
                    outs[half][pl.ds(first, rest)] = jnp.zeros((rest, 8, 128), bf16)

        @pl.when(step < mlp_steps)
        def _():
            xo = jnp.concatenate([xo7[...], xo8[...]], axis=1)
            xp = jnp.concatenate([xp7[...], xp8[...]], axis=1)
            for out_ref, g_own, g_par in ((outs[0], gog, gpg), (outs[1], gou, gpu)):
                value = pair_product(xo, xp, g_own, g_par)
                for group in range(mlp_groups):
                    first = place[16 + group // 7] * half_tiles + group % 7 * (FF // 128)
                    store_tiles(
                        out_ref,
                        (),
                        first + step * 4,
                        value[8 * group : 8 * group + 8],
                    )

        @pl.when(step >= mlp_steps)
        def _():
            value = pair_product(ho, hp, go, gp)
            for group in range(wide // 8):
                at = (step - mlp_steps) * (wide // 8) + group
                part = at // half_groups
                first = place_ref[part // 2] * half_tiles + (at % half_groups) * 9
                piece = value[8 * group : 8 * group + 8]

                def put(out_ref, first=first, piece=piece):
                    store_tiles(out_ref, (), first, piece)

                pl.when(part % 2 == 0)(lambda put=put: put(outs[0]))
                pl.when(part % 2 == 1)(lambda put=put: put(outs[1]))

    x_specs = [pl.BlockSpec((rows, 128), lambda t: (0, 7)), pl.BlockSpec((rows, 128), lambda t: (0, 8))]
    g_spec = pl.BlockSpec((rows, 512), lambda t: (0, jnp.minimum(t, mlp_steps - 1)))
    h_spec = pl.BlockSpec((rows, wide), lambda t: (0, jnp.maximum(t - mlp_steps, 0)))
    b_spec = pl.BlockSpec((rows, D), lambda t: (0, 0))
    shape = (16 * half_tiles, 8, 128)
    down_place = jnp.asarray([place[MLP_BLOCKS + i] for i in range(down_blocks)], jnp.int32)
    out = pl.pallas_call(
        body,
        grid=(mlp_steps + down_steps,),
        in_specs=[pl.BlockSpec(memory_space=pltpu.SMEM)]
        + x_specs * 2
        + [g_spec] * 4
        + [h_spec] * 2
        + [b_spec] * 2,
        out_specs=[pl.BlockSpec(shape, lambda t: (0, 0, 0))] * 2,
        out_shape=[jax.ShapeDtypeStruct(shape, bf16)] * 2,
        compiler_params=pltpu.CompilerParams(vmem_limit_bytes=44 << 20),
        name="grads_b_core_1",
    )(down_place, in_b[0], in_b[0], in_b[1], in_b[1], *g_gate, *g_up, *hidden, *g_branch)
    return [part.reshape(-1, 128) for part in out]


def grads_a(core, in_a, g_proj, att, g_branch):
    rows = in_a[0].shape[0]
    steps = 3 * D // 384
    place = PLACE_A[core]

    def store_qkv(value, first_block, step, outs):
        for group in range(48):
            block, half, low = first_block + group // 6, group // 3 % 2, group % 3
            store_tiles(
                outs[half],
                (place[block],),
                low * 27 + step * 3,
                value[8 * group : 8 * group + 8],
            )

    def body(xo, xp, go, gp, zo, zp, bo, bp, *outs):
        step = pl.program_id(0)

        @pl.when(step < steps)
        def _():
            store_qkv(pair_product(xo, xp, go, gp), 8 * core, step, outs)
            if core == 0:
                store_qkv(pair_product(zo, zp, go, gp), 16, step, outs)

        if core == 1:

            @pl.when(step >= steps)
            def _():
                value = pair_product(zo, zp, bo, bp)
                for group in range(144):
                    block, half, low = QKV_BLOCKS + group // 18, group // 9 % 2, group % 9
                    store_tiles(
                        outs[half],
                        (place[block],),
                        low * 9 + (step - steps) * 3,
                        value[8 * group : 8 * group + 8],
                    )

    x_spec = pl.BlockSpec((rows, 384), lambda t: (0, core))
    g_spec = pl.BlockSpec((rows, 384), lambda t: (0, jnp.minimum(t, steps - 1)))
    if core == 0:
        z_spec, z = pl.BlockSpec((rows, 384), lambda t: (0, 2)), in_a
        b_spec, count = pl.BlockSpec((rows, 384), lambda t: (0, 0)), steps
    else:
        z_spec, z = pl.BlockSpec((rows, D), lambda t: (0, 0)), att
        b_spec = pl.BlockSpec((rows, 384), lambda t: (0, jnp.maximum(t - steps, 0)))
        count = steps + D // 384
    shape = (16, 81, 8, 128)
    out = pl.pallas_call(
        body,
        grid=(count,),
        in_specs=[x_spec] * 2 + [g_spec] * 2 + [z_spec] * 2 + [b_spec] * 2,
        out_specs=[pl.BlockSpec(shape, lambda t: (0, 0, 0, 0))] * 2,
        out_shape=[jax.ShapeDtypeStruct(shape, jnp.bfloat16)] * 2,
        compiler_params=pltpu.CompilerParams(vmem_limit_bytes=44 << 20),
        name=f"grads_a_core_{core}",
    )(*in_a, *g_proj, *z, *g_branch)
    return [part.reshape(-1, 128) for part in out]


def gathered_weights(pieces_a, pieces_b):
    me = device_index()
    block_a = spread(pieces_a, PLAN_A)
    block_a = jnp.where(me < QKV_BLOCKS, to_tiles(block_a, 27), to_tiles(block_a, 9))
    block_b = spread(pieces_b, PLAN_B)
    block_b = jnp.where(
        me < MLP_BLOCKS,
        to_tiles(block_b, 48),
        jnp.pad(to_tiles(block_b[:USED_DOWN], 9), ((0, BLOCK_B - USED_DOWN), (0, 0))),
    )
    block = jnp.concatenate([block_a, block_b])
    return lax.all_gather(block, ("fsdp", "dp"), axis=0, tiled=True).reshape(-1, 8, 128)


def head_indicator():
    feature = lax.broadcasted_iota(jnp.int32, (D, 128), 0)
    head = lax.broadcasted_iota(jnp.int32, (D, 128), 1)
    return ((feature >= head * HEAD_DIM) & (feature < (head + 1) * HEAD_DIM)).astype(jnp.bfloat16)


def two_parts(value):
    high = value.astype(jnp.bfloat16)
    return high, (value - high.astype(jnp.float32)).astype(jnp.bfloat16)


def head_means(value, indicator):
    high, low = two_parts(value)
    total = jnp.dot(high, indicator, preferred_element_type=jnp.float32)
    total += jnp.dot(low, indicator, preferred_element_type=jnp.float32)
    return total * (1.0 / HEAD_DIM)


def over_heads(value, indicator):
    high, low = two_parts(value)
    across = (((1,), (1,)), ((), ()))
    total = lax.dot_general(high, indicator, across, preferred_element_type=jnp.float32)
    return total + lax.dot_general(low, indicator, across, preferred_element_type=jnp.float32)


def turned(value):
    quarter = HEAD_DIM // 4
    feature = lax.broadcasted_iota(jnp.int32, value.shape, 1) % (2 * quarter)
    ahead = pltpu.roll(value, D - quarter, 1)
    behind = pltpu.roll(value, quarter, 1)
    return jnp.where(feature < quarter, -ahead, behind)


def heads_of(ref):
    return [ref[:, HEAD_DIM * h : HEAD_DIM * (h + 1)] for h in range(HEADS)]


ACROSS = (((1,), (1,)), ((), ()))
DOWN = (((0,), (0,)), ((), ()))


def attention_forward(projected, cosines, sines):
    f32, bf16 = jnp.float32, jnp.bfloat16
    rows = projected.shape[0]
    length = cosines.shape[0]
    scale = 1.0 / math.sqrt(HEAD_DIM)

    def body(proj_ref, cos_ref, sin_ref, ind_ref, q_ref, k_ref, v_ref, att_ref, log_ref):
        indicator = ind_ref[...]
        for part, ref in ((0, q_ref), (1, k_ref)):
            value = proj_ref[:, D * part : D * (part + 1)]
            inverse = lax.rsqrt(head_means(value * value, indicator) + eps_norm)
            norm = value * over_heads(inverse, indicator)
            ref[...] = (norm * cos_ref[...] + turned(norm) * sin_ref[...]).astype(bf16)
        v_ref[...] = proj_ref[:, 2 * D :].astype(bf16)
        logs = []
        for h in range(HEADS):
            at = slice(HEAD_DIM * h, HEAD_DIM * (h + 1))
            scores = (
                lax.dot_general(q_ref[:, at], k_ref[:, at], ACROSS, preferred_element_type=f32)
                * scale
            )
            top = jnp.max(scores, axis=1, keepdims=True)
            log_total = top + jnp.log(jnp.sum(jnp.exp(scores - top), axis=1, keepdims=True))
            probs = jnp.exp(scores - log_total).astype(bf16)
            att_ref[:, at] = jnp.dot(probs, v_ref[:, at], preferred_element_type=f32).astype(bf16)
            log_ref[:, h : h + 1] = log_total

    wide = pl.BlockSpec((length, D), lambda i: (i, 0))
    table = pl.BlockSpec((length, D), lambda i: (0, 0))
    return pl.pallas_call(
        body,
        grid=(rows // length,),
        in_specs=[
            pl.BlockSpec((length, 3 * D), lambda i: (i, 0)),
            table,
            table,
            pl.BlockSpec((D, 128), lambda i: (0, 0)),
        ],
        out_specs=[wide] * 4 + [pl.BlockSpec((length, HEADS), lambda i: (i, 0))],
        out_shape=[jax.ShapeDtypeStruct((rows, D), bf16)] * 4
        + [jax.ShapeDtypeStruct((rows, HEADS), f32)],
        cost_estimate=pl.CostEstimate(
            flops=8 * rows * length * D, bytes_accessed=20_000_000, transcendentals=40_000_000
        ),
        compiler_params=pltpu.CompilerParams(vmem_limit_bytes=44 << 20),
        name="attention_forward",
    )(projected, cosines, sines, head_indicator())


def attention_backward(projected, queries, keys, values, log_total, g_attended, cosines, sines):
    f32, bf16 = jnp.float32, jnp.bfloat16
    rows = projected.shape[0]
    length = cosines.shape[0]
    scale = 1.0 / math.sqrt(HEAD_DIM)

    def body(proj_ref, q_ref, k_ref, v_ref, log_ref, g_ref, cos_ref, sin_ref, ind_ref, *rest):
        out_ref, sum_ref, gq_ref, gk_ref, gv_ref = rest
        for h in range(HEADS):
            at = slice(HEAD_DIM * h, HEAD_DIM * (h + 1))
            q, k, v, g = q_ref[:, at], k_ref[:, at], v_ref[:, at], g_ref[:, at]
            scores = lax.dot_general(q, k, ACROSS, preferred_element_type=f32) * scale
            probs = jnp.exp(scores - log_ref[:, h : h + 1])
            g_probs = lax.dot_general(g, v, ACROSS, preferred_element_type=f32)
            gv_ref[:, at] = lax.dot_general(
                probs.astype(bf16), g, DOWN, preferred_element_type=f32
            )
            inner = jnp.sum(probs * g_probs, axis=1, keepdims=True)
            g_scores = (probs * (g_probs - inner)).astype(bf16)
            gq_ref[:, at] = jnp.dot(g_scores, k, preferred_element_type=f32) * scale
            gk_ref[:, at] = (
                lax.dot_general(g_scores, q, DOWN, preferred_element_type=f32) * scale
            )
        indicator = ind_ref[...]
        for part, ref in ((0, gq_ref), (1, gk_ref)):
            value = proj_ref[:, D * part : D * (part + 1)]
            inverse = over_heads(
                lax.rsqrt(head_means(value * value, indicator) + eps_norm), indicator
            )
            norm = value * inverse
            back = ref[...] * cos_ref[...] - turned(ref[...]) * sin_ref[...]
            mean = over_heads(head_means(back * norm, indicator), indicator)
            out_ref[:, D * part : D * (part + 1)] = (inverse * (back - norm * mean)).astype(bf16)
        out_ref[:, 2 * D :] = gv_ref[...].astype(bf16)
        sum_ref[0] = jnp.sum(out_ref[...].astype(f32), axis=0, keepdims=True)

    wide = pl.BlockSpec((length, D), lambda i: (i, 0))
    table = pl.BlockSpec((length, D), lambda i: (0, 0))
    images = rows // length
    return pl.pallas_call(
        body,
        grid=(images,),
        in_specs=[
            pl.BlockSpec((length, 2 * D), lambda i: (i, 0)),
            wide,
            wide,
            wide,
            pl.BlockSpec((length, HEADS), lambda i: (i, 0)),
            wide,
            table,
            table,
            pl.BlockSpec((D, 128), lambda i: (0, 0)),
        ],
        out_specs=[
            pl.BlockSpec((length, 3 * D), lambda i: (i, 0)),
            pl.BlockSpec((1, 1, 3 * D), lambda i: (i, 0, 0)),
        ],
        out_shape=[
            jax.ShapeDtypeStruct((rows, 3 * D), bf16),
            jax.ShapeDtypeStruct((images, 1, 3 * D), f32),
        ],
        scratch_shapes=[pltpu.VMEM((length, D), f32)] * 3,
        cost_estimate=pl.CostEstimate(flops=1000, bytes_accessed=1000, transcendentals=0),
        compiler_params=pltpu.CompilerParams(vmem_limit_bytes=44 << 20),
        name="attention_backward",
    )(projected, queries, keys, values, log_total, g_attended, cosines, sines, head_indicator())


def split_a(gathered):
    block = BLOCK_A // 8

    def body(all_ref, qkv_ref, out_ref, sem):
        copies = []
        for i in range(DEVICES):
            ref, first = (qkv_ref, 0) if i < QKV_BLOCKS else (out_ref, QKV_BLOCKS)
            copies.append(
                pltpu.make_async_copy(
                    all_ref.at[pl.ds(i * (BLOCK_A + BLOCK_B) // 8, block)],
                    ref.at[pl.ds((i - first) * block, block)],
                    sem.at[i],
                )
            )
        for copy in copies:
            copy.start()
        for copy in copies:
            copy.wait()

    w_qkv, w_out = pl.pallas_call(
        body,
        in_specs=[pl.BlockSpec(memory_space=pl.ANY)],
        out_specs=[pl.BlockSpec(memory_space=pltpu.VMEM)] * 2,
        out_shape=[
            jax.ShapeDtypeStruct((ROWS_QKV // 8, 8, 128), jnp.bfloat16),
            jax.ShapeDtypeStruct((ROWS_OUT // 8, 8, 128), jnp.bfloat16),
        ],
        scratch_shapes=[pltpu.SemaphoreType.DMA((DEVICES,))],
        compiler_params=pltpu.CompilerParams(vmem_limit_bytes=40 << 20),
        name="split_a",
    )(gathered)
    return matrix_of_tiles(w_qkv, D, 3 * D), matrix_of_tiles(w_out, D, D)


def owned_rows(back_a, back_b, grad_ada):
    first_a, step_a = starts_a()
    first_b, step_b = starts_b()
    me = device_index()
    numbers = jnp.stack(
        [jnp.asarray(v, jnp.int32) for v in (first_a, step_a, first_b, step_b, me * SHARD)]
    )
    total = SHARD + 2 * BLOCK_B

    def body(numbers_ref, *refs):
        out_ref, sum_ref = refs[-2:]
        sum_ref[...] = jnp.zeros_like(sum_ref)
        for refs_of, at, rows in (
            (refs[: len(back_b)], 2, BLOCK_B),
            (refs[len(back_b) : len(back_b) + len(back_a)], 0, BLOCK_A),
        ):
            for k, ref in enumerate(refs_of):
                start = BLOCK_B + numbers_ref[at] + k * numbers_ref[at + 1]
                start = pl.multiple_of(jnp.clip(start, 0, total - rows), 8)
                sum_ref[pl.ds(start, rows)] += ref[...].astype(jnp.float32)
        row = numbers_ref[4] + lax.broadcasted_iota(jnp.int32, (SHARD, 128), 0)
        out_ref[...] = jnp.where(
            (row >= FIRST_ADA) & (row < FIRST_DOWN),
            refs[-3][...],
            sum_ref[pl.ds(BLOCK_B, SHARD)],
        )

    return pl.pallas_call(
        body,
        in_specs=[pl.BlockSpec(memory_space=pltpu.SMEM)]
        + [pl.BlockSpec(memory_space=pltpu.VMEM)] * (len(back_a) + len(back_b) + 1),
        out_specs=pl.BlockSpec(memory_space=pltpu.VMEM),
        out_shape=jax.ShapeDtypeStruct((SHARD, 128), jnp.float32),
        scratch_shapes=[pltpu.VMEM((total, 128), jnp.float32)],
        compiler_params=pltpu.CompilerParams(vmem_limit_bytes=40 << 20),
        name="owned_rows",
    )(numbers, *back_b, *back_a, grad_ada)


def on_device_32(tokens, conditions, cotangent, slot_mask, weight_flat, bias_flat):
    f32 = jnp.float32
    bf16 = jnp.bfloat16
    axes = ("fsdp", "dp")
    me = device_index()
    core = lax.axis_index("dp") % 2
    slots = conditions.shape[0]
    images = slots * DEVICES
    length = GRID * GRID
    rows_all = slots * length
    cond_count = slots * D
    bias_count = bias_flat.shape[0]
    packed_rows = -(-(cond_count + bias_count) // 128)
    packed = jnp.concatenate(
        [
            conditions.reshape(-1),
            bias_flat,
            jnp.zeros(packed_rows * 128 - cond_count - bias_count, bf16),
        ]
    ).reshape(packed_rows, 128)
    pieces = cut_pieces(weight_flat, PLAN_A), cut_pieces(weight_flat, PLAN_B)
    packed, pieces = lax.optimization_barrier((packed, pieces))
    gathered = gathered_weights(*pieces)
    packed_all = gather_columns(gather_column(packed)).reshape(DEVICES, -1)
    cond_all = packed_all[:, :cond_count].reshape(images, D).astype(f32)
    places = lax.broadcasted_iota(jnp.int32, (DEVICES, DEVICES), 0)
    others = lax.broadcasted_iota(jnp.int32, (DEVICES, DEVICES), 1)
    chosen = ((places ^ me) == others).astype(bf16)
    bias_all = jnp.dot(
        chosen, packed_all[:, cond_count : cond_count + bias_count], preferred_element_type=f32
    ).reshape(-1)
    b_qkv = bias_all[: 3 * D]
    b_out = bias_all[3 * D : 4 * D]
    b_mlp = bias_all[4 * D : 4 * D + 2 * FF]
    b_ada = bias_all[4 * D + 2 * FF :]
    ada_local = weight_flat.reshape(ADA_ROWS, 6 * D)
    ada_start = jnp.clip(
        me * ADA_ROWS - FIRST_ADA * 128 // (6 * D) + ADA_ROWS, 0, D + ADA_ROWS
    )
    cond_act = jax.nn.silu(cond_all).astype(bf16)
    cond_rows = lax.dynamic_slice_in_dim(
        jnp.pad(cond_act.T, ((ADA_ROWS, ADA_ROWS), (0, 0))), ada_start, ADA_ROWS, 0
    )
    cond_ordered = jnp.dot(
        chosen, cond_act.reshape(DEVICES, cond_count), preferred_element_type=f32
    ).astype(bf16)
    rows_ordered = lax.dynamic_slice_in_dim(
        jnp.pad(cond_ordered.reshape(images, D).T, ((ADA_ROWS, ADA_ROWS), (0, 0))),
        ada_start,
        ADA_ROWS,
        0,
    )
    terms = jnp.einsum("km,kn->mn", cond_rows, ada_local, preferred_element_type=f32)
    modulation = sum_to_owners(terms.reshape(DEVICES, slots, 6 * D)) + b_ada
    w_qkv, w_out = split_a(gathered)

    def share(array):
        return (array, lax.ppermute(array, "dp", SWAP_CORE))

    cosines, sines = [jnp.tile(table[:, 0], (1, HEADS)) for table in rope_tables()]
    mask_f = slot_mask.astype(f32)[:, None, None]
    x_f = tokens.astype(f32).reshape(slots, length, D)
    shift_a, scale_a, gate_a, shift_b, scale_b, gate_b = [
        modulation[:, None, place * D : (place + 1) * D] for place in range(6)
    ]
    g_out = cotangent.astype(f32).reshape(slots, length, D) * mask_f
    g_branch_b = (gate_b * g_out).astype(bf16).reshape(rows_all, D)
    normed_a, inv_a = norm_parts(x_f)
    input_a = (normed_a * (1.0 + scale_a) + shift_a).astype(bf16).reshape(rows_all, D)
    projected = jnp.dot(input_a, w_qkv, preferred_element_type=f32) + b_qkv
    queries, keys, values, attended, log_total = attention_forward(projected, cosines, sines)
    branch_a = (jnp.dot(attended, w_out, preferred_element_type=f32) + b_out).reshape(
        slots, length, D
    )
    middle = x_f + gate_a * branch_a
    normed_b, inv_b = norm_parts(middle)
    input_b = (normed_b * (1.0 + scale_b) + shift_b).astype(bf16).reshape(rows_all, D)
    early = [share(array) for array in (input_a, attended, input_b, g_branch_b)]
    input_b = after(input_b, early[0], early[3])
    hidden, g_gate, g_up, branch_b, g_input_b, sum_gate, sum_up = mlp_both_ways(
        input_b, g_branch_b, b_mlp.reshape(1, 2 * FF), gathered
    )
    shared_mlp = [share(array) for array in (g_gate, g_up, hidden)]
    branch_b = branch_b.reshape(slots, length, D)
    g_input_b = g_input_b.reshape(slots, length, D)
    out = ((middle + gate_b * branch_b) * mask_f).astype(bf16).reshape(rows_all, D)
    g_gate_b = jnp.sum(g_out * branch_b, axis=1)
    g_shift_b = jnp.sum(g_input_b, axis=1)
    g_scale_b = jnp.sum(g_input_b * normed_b, axis=1)
    g_middle = g_out + norm_back(g_input_b * (1.0 + scale_b), normed_b, inv_b)
    g_branch_a = (gate_a * g_middle).astype(bf16).reshape(rows_all, D)
    g_gate_a = jnp.sum(g_middle * branch_a, axis=1)
    grad_b_out = jnp.sum(g_branch_a.astype(f32), axis=0)
    shared_branch_a = share(g_branch_a)
    grads_b = lax.cond(
        core == 0,
        lambda: grads_b_core_0(early[2], shared_mlp[0], shared_mlp[1]),
        lambda: grads_b_core_1(early[2], *shared_mlp, early[3]),
    )
    orders = (SWAP_Y, SWAP_X), (SWAP_X, SWAP_Y)
    sends_b = first_sends(grads_b, BLOCK_B)
    arrived = over_planes(sends_b, orders[0])
    g_attended = jnp.einsum(
        "re,de->rd", after(g_branch_a, sends_b), w_out, preferred_element_type=f32
    )
    g_attended = g_attended.astype(bf16)
    g_projected, proj_sums = attention_backward(
        projected, queries, keys, values, log_total, g_attended, cosines, sines
    )
    grad_b_qkv = jnp.sum(proj_sums, axis=(0, 1))
    shared_proj = share(g_projected)
    g_input_a = jnp.einsum("re,de->rd", g_projected, w_qkv, preferred_element_type=f32)
    g_input_a = lax.optimization_barrier(g_input_a).reshape(slots, length, D)
    g_shift_a = jnp.sum(g_input_a, axis=1)
    g_scale_a = jnp.sum(g_input_a * normed_a, axis=1)
    g_modulation = jnp.concatenate(
        [g_shift_a, g_scale_a, g_gate_a, g_shift_b, g_scale_b, g_gate_b], axis=1
    ).astype(bf16)
    bias_sums = [grad_b_qkv, grad_b_out, sum_gate.reshape(-1), sum_up.reshape(-1)]
    small = jnp.concatenate([g_modulation.reshape(-1)] + [b.astype(bf16) for b in bias_sums])
    kept_b, sends_b = second_sends(grads_b, after(arrived, small), BLOCK_B)
    shared_proj = after(shared_proj, sends_b)
    small_all = lax.all_gather(small.reshape(-1, 128), axes, axis=0, tiled=True)
    made_a = lax.cond(
        core == 0,
        lambda: grads_a(0, early[0], shared_proj, early[1], shared_branch_a),
        lambda: grads_a(1, early[0], shared_proj, early[1], shared_branch_a),
    )
    sends_a = first_sends(made_a, BLOCK_A)
    planes_b = plane_sums(kept_b, after(over_planes(sends_b, orders[1]), sends_a))
    sends_b = line_sends(planes_b)
    arrived = after(over_planes(sends_a, orders[0]), sends_b)
    kept_a, sends_a = second_sends(made_a, arrived, BLOCK_A)
    line_b = after(from_line(sends_b), sends_a)
    grad_tokens = g_middle + norm_back(g_input_a * (1.0 + scale_a), normed_a, inv_a)
    sum_b = sum_line(sends_b[0], line_b).astype(bf16)
    halves = sum_b.reshape(2, BLOCK_B // 2, 128)
    sum_b = jnp.where(
        jnp.logical_not(is_kind(PLACE_B, MLP_BLOCKS)),
        jnp.concatenate(
            [from_tiles(half, 24).reshape(-1, 24, 128) for half in halves], axis=1
        ).reshape(-1, 128),
        jnp.pad(
            from_tiles(halves[:, : USED_DOWN // 2].reshape(-1, 128), 9),
            ((0, BLOCK_B - USED_DOWN), (0, 0)),
        ),
    )
    planes_a = plane_sums(kept_a, after(over_planes(sends_a, orders[1]), sum_b))
    sends_a = line_sends(planes_a)
    small_all = after(small_all, sends_a).reshape(DEVICES, -1)
    g_mod_all = small_all[:, : slots * 6 * D].reshape(images, 6 * D)
    g_cond_rows = jnp.einsum("mn,kn->mk", g_mod_all, ada_local, preferred_element_type=f32)
    back_b = send_back(after(sum_b, sends_a), PLAN_B, PLACE_B)
    sum_a = sum_line(sends_a[0], after(from_line(sends_a), back_b)).astype(bf16)
    sum_a = jnp.where(is_kind(PLACE_A, QKV_BLOCKS), from_tiles(sum_a, 9), from_tiles(sum_a, 27))
    back_a = send_back(sum_a, PLAN_A, PLACE_A)
    grad_biases = jnp.concatenate(
        [
            jnp.sum(small_all[:, slots * 6 * D :].astype(f32), axis=0),
            jnp.sum(g_mod_all.astype(f32), axis=0),
        ]
    )
    part_biases = lax.dynamic_slice_in_dim(grad_biases, me * bias_count, bias_count, 0)
    grad_ada = jnp.einsum("km,mn->kn", rows_ordered, g_mod_all, preferred_element_type=f32)
    came = lax.all_to_all(
        g_cond_rows.reshape(DEVICES, slots, ADA_ROWS), axes, split_axis=0, concat_axis=0, tiled=True
    )
    first = FIRST_ADA * 128 // (6 * D)
    g_cond = came.transpose(1, 0, 2).reshape(slots, DEVICES * ADA_ROWS)[:, first : first + D]
    cond_f = conditions.astype(f32)
    sigma_cond = jax.nn.sigmoid(cond_f)
    grad_conditions = g_cond * sigma_cond * (1.0 + cond_f * (1.0 - sigma_cond))
    part_weights = owned_rows(back_a, back_b, grad_ada.reshape(SHARD, 128))
    return (out, grad_tokens.reshape(rows_all, D), grad_conditions, part_weights, part_biases)


def solution(mesh):
    chosen = on_device_32 if dict(mesh.shape) == {"fsdp": 4, "dp": 8} else on_device_plain
    return jax.shard_map(
        chosen,
        mesh=mesh,
        in_specs=(
            P(("fsdp", "dp"), None),
            P(("fsdp", "dp"), None),
            P(("fsdp", "dp"), None),
            P(("fsdp", "dp")),
            P(("fsdp", "dp"), None),
            P(("fsdp", "dp")),
        ),
        out_specs=(
            P(("fsdp", "dp"), None),
            P(("fsdp", "dp"), None),
            P(("fsdp", "dp"), None),
            P(("fsdp", "dp"), None),
            P(("fsdp", "dp")),
        ),
        check_vma=False,
    )
```

```python
import math

import jax
import jax.numpy as jnp
from jax import lax
from jax.experimental import pallas as pl
from jax.experimental.pallas import tpu as pltpu
import numpy as np
from jax.sharding import PartitionSpec as P

D = 1152
HEADS = 16
HEAD_DIM = 72
FF = 3072
GRID = 16


eps_norm = 1e-06


def unpack_weights(weight_all, bias_all):
    flat = weight_all.reshape(-1)
    layouts = ((D, 3 * D), (D, D), (D, 2 * FF), (D, 6 * D), (FF, D))
    pieces = []
    offset = 0
    for layout in layouts:
        amount = layout[0] * layout[1]
        pieces.append(flat[offset : offset + amount].reshape(layout))
        offset = offset + amount
    offset = 0
    for amount in (3 * D, D, 2 * FF, 6 * D):
        pieces.append(bias_all[offset : offset + amount])
        offset = offset + amount
    return tuple(pieces)


def rope_tables():
    quarter = HEAD_DIM // 4
    places = jnp.arange(GRID * GRID, dtype=jnp.int32)
    rows_at = (places // GRID).astype(jnp.float32)
    cols_at = (places % GRID).astype(jnp.float32)
    freqs = 10000.0 ** (-jnp.arange(quarter, dtype=jnp.float32) / quarter)
    along_rows = rows_at[:, None] * freqs[None, :]
    along_cols = cols_at[:, None] * freqs[None, :]
    angles = jnp.concatenate([along_rows, along_rows, along_cols, along_cols], axis=1)
    return (jnp.cos(angles)[:, None, :], jnp.sin(angles)[:, None, :])


def turn_half(values):
    quarter = values.shape[-1] // 4
    first = values[..., :quarter]
    second = values[..., quarter : 2 * quarter]
    third = values[..., 2 * quarter : 3 * quarter]
    fourth = values[..., 3 * quarter :]
    return jnp.concatenate([-second, first, -fourth, third], axis=-1)


def norm_parts(values):
    centred = values - jnp.mean(values, -1, keepdims=True)
    inverse = lax.rsqrt(jnp.mean(centred * centred, -1, keepdims=True) + eps_norm)
    return (centred * inverse, inverse)


def norm_back(grad_normed, normed, inverse):
    return inverse * (
        grad_normed
        - jnp.mean(grad_normed, -1, keepdims=True)
        - normed * jnp.mean(grad_normed * normed, -1, keepdims=True)
    )


def rms_parts(values):
    inverse = lax.rsqrt(jnp.mean(values * values, -1, keepdims=True) + eps_norm)
    return (values * inverse, inverse)


def rms_back(grad_normed, normed, inverse):
    return inverse * (grad_normed - normed * jnp.mean(grad_normed * normed, -1, keepdims=True))


def compute_block(tokens, cotangent, slot_mask, modulation, weights, biases):
    f32 = jnp.float32
    bf16 = jnp.bfloat16
    w_qkv, w_out, w_mlp, w_down = weights
    b_qkv, b_out, b_mlp = biases
    slots = slot_mask.shape[0]
    length = GRID * GRID
    rows_all = slots * length
    scale = 1.0 / math.sqrt(HEAD_DIM)
    heads_shape = (slots, length, HEADS, HEAD_DIM)
    cosines, sines = rope_tables()
    mask_f = slot_mask.astype(f32)[:, None, None]
    x_f = tokens.astype(f32).reshape(slots, length, D)
    shift_a, scale_a, gate_a, shift_b, scale_b, gate_b = [
        modulation[:, None, place * D : (place + 1) * D] for place in range(6)
    ]
    normed_a, inv_a = norm_parts(x_f)
    attention_input = (normed_a * (1.0 + scale_a) + shift_a).astype(bf16).reshape(rows_all, D)
    projected_output = (
        jnp.dot(attention_input, w_qkv, preferred_element_type=f32) + b_qkv.astype(f32)
    ).reshape(slots, length, 3 * D)
    q_norm, inv_q = rms_parts(projected_output[..., :D].reshape(heads_shape))
    k_norm, inv_k = rms_parts(projected_output[..., D : 2 * D].reshape(heads_shape))
    queries = (q_norm * cosines + turn_half(q_norm) * sines).astype(bf16)
    keys = (k_norm * cosines + turn_half(k_norm) * sines).astype(bf16)
    values = projected_output[..., 2 * D :].reshape(heads_shape).astype(bf16)
    scores = jnp.einsum("slhe,smhe->shlm", queries, keys, preferred_element_type=f32) * scale
    row_max = jnp.max(scores, -1, keepdims=True)
    log_total = row_max + jnp.log(jnp.sum(jnp.exp(scores - row_max), -1, keepdims=True))
    probs_low = jnp.exp(scores - log_total).astype(bf16)
    attention_output = (
        jnp.einsum("shlm,smhe->slhe", probs_low, values, preferred_element_type=f32)
        .astype(bf16)
        .reshape(rows_all, D)
    )
    attention_branch = (
        jnp.dot(attention_output, w_out, preferred_element_type=f32) + b_out.astype(f32)
    ).reshape(slots, length, D)
    middle = x_f + gate_a * attention_branch
    normed_b, inv_b = norm_parts(middle)
    feedforward_input = (normed_b * (1.0 + scale_b) + shift_b).astype(bf16).reshape(rows_all, D)
    mixed_tokens = jnp.dot(feedforward_input, w_mlp, preferred_element_type=f32) + b_mlp.astype(
        f32
    )
    gate_part = mixed_tokens[:, :FF]
    up_part = mixed_tokens[:, FF:]
    hidden_state = (jax.nn.silu(gate_part) * up_part).astype(bf16)
    feedforward_branch = jnp.dot(hidden_state, w_down, preferred_element_type=f32).reshape(
        slots, length, D
    )
    out = ((middle + gate_b * feedforward_branch) * mask_f).astype(bf16).reshape(rows_all, D)
    g_out = cotangent.astype(f32).reshape(slots, length, D) * mask_f
    g_branch_b = (gate_b * g_out).astype(bf16).reshape(rows_all, D)
    g_gate_b = jnp.sum(g_out * feedforward_branch, axis=1)
    g_hidden = jnp.einsum("rd,fd->rf", g_branch_b, w_down, preferred_element_type=f32)
    sigma_gate = jax.nn.sigmoid(gate_part)
    g_mixed = jnp.concatenate(
        [
            g_hidden * up_part * sigma_gate * (1.0 + gate_part * (1.0 - sigma_gate)),
            g_hidden * (gate_part * sigma_gate),
        ],
        axis=1,
    ).astype(bf16)
    grad_b_mlp = jnp.sum(g_mixed.astype(f32), axis=0)
    g_input_b = jnp.einsum("rf,df->rd", g_mixed, w_mlp, preferred_element_type=f32).reshape(
        slots, length, D
    )
    g_shift_b = jnp.sum(g_input_b, axis=1)
    g_scale_b = jnp.sum(g_input_b * normed_b, axis=1)
    g_middle = g_out + norm_back(g_input_b * (1.0 + scale_b), normed_b, inv_b)
    g_branch_a = (gate_a * g_middle).astype(bf16).reshape(rows_all, D)
    g_gate_a = jnp.sum(g_middle * attention_branch, axis=1)
    grad_b_out = jnp.sum(g_branch_a.astype(f32), axis=0)
    g_attended = (
        jnp.einsum("re,de->rd", g_branch_a, w_out, preferred_element_type=f32)
        .astype(bf16)
        .reshape(heads_shape)
    )
    scores = jnp.einsum("slhe,smhe->shlm", queries, keys, preferred_element_type=f32) * scale
    probs = jnp.exp(scores - log_total)
    probs_low = probs.astype(bf16)
    g_probs = jnp.einsum("slhe,smhe->shlm", g_attended, values, preferred_element_type=f32)
    g_values = jnp.einsum("shlm,slhe->smhe", probs_low, g_attended, preferred_element_type=f32)
    g_scores = (probs * (g_probs - jnp.sum(probs * g_probs, -1, keepdims=True))).astype(bf16)
    g_queries = jnp.einsum("shlm,smhe->slhe", g_scores, keys, preferred_element_type=f32) * scale
    g_keys = jnp.einsum("shlm,slhe->smhe", g_scores, queries, preferred_element_type=f32) * scale
    g_q = rms_back(g_queries * cosines - turn_half(g_queries) * sines, q_norm, inv_q)
    g_k = rms_back(g_keys * cosines - turn_half(g_keys) * sines, k_norm, inv_k)
    g_projected = jnp.concatenate(
        [g_q.reshape(rows_all, D), g_k.reshape(rows_all, D), g_values.reshape(rows_all, D)], axis=1
    ).astype(bf16)
    grad_b_qkv = jnp.sum(g_projected.astype(f32), axis=0)
    g_input_a = jnp.einsum("re,de->rd", g_projected, w_qkv, preferred_element_type=f32).reshape(
        slots, length, D
    )
    g_shift_a = jnp.sum(g_input_a, axis=1)
    g_scale_a = jnp.sum(g_input_a * normed_a, axis=1)
    grad_tokens = g_middle + norm_back(g_input_a * (1.0 + scale_a), normed_a, inv_a)
    g_modulation = jnp.concatenate(
        [g_shift_a, g_scale_a, g_gate_a, g_shift_b, g_scale_b, g_gate_b], axis=1
    ).astype(bf16)
    pairs = (
        (attention_input, g_projected),
        (attention_output, g_branch_a),
        (feedforward_input, g_mixed),
        (hidden_state, g_branch_b),
    )
    return (
        out,
        grad_tokens.reshape(rows_all, D),
        g_modulation,
        (grad_b_qkv, grad_b_out, grad_b_mlp),
        pairs,
    )


def weight_grad(pair):
    return jnp.einsum("rd,re->de", pair[0], pair[1], preferred_element_type=jnp.float32)


def on_device_plain(tokens, conditions, cotangent, slot_mask, weight_flat, bias_flat):
    f32 = jnp.float32
    bf16 = jnp.bfloat16
    axes = ("fsdp", "dp")
    weight_all = lax.all_gather(weight_flat, axes, axis=0, tiled=True)
    bias_all = lax.all_gather(bias_flat, axes, axis=0, tiled=True)
    w_qkv, w_out, w_mlp, w_ada, w_down, b_qkv, b_out, b_mlp, b_ada = unpack_weights(
        weight_all, bias_all
    )
    cond_f = conditions.astype(f32)
    cond_act = jax.nn.silu(cond_f).astype(bf16)
    modulation = jnp.dot(cond_act, w_ada, preferred_element_type=f32) + b_ada.astype(f32)
    out, grad_tokens, g_modulation, bias_sums, pairs = compute_block(
        tokens,
        cotangent,
        slot_mask,
        modulation,
        (w_qkv, w_out, w_mlp, w_down),
        (b_qkv, b_out, b_mlp),
    )
    grad_b_ada = jnp.sum(g_modulation.astype(f32), axis=0)
    g_cond = jnp.einsum("se,de->sd", g_modulation, w_ada, preferred_element_type=f32)
    sigma_cond = jax.nn.sigmoid(cond_f)
    grad_conditions = g_cond * sigma_cond * (1.0 + cond_f * (1.0 - sigma_cond))
    grad_qkv, grad_out, grad_mlp, grad_down = [weight_grad(pair) for pair in pairs]
    grad_ada = weight_grad((cond_act, g_modulation))
    grads_big = jnp.concatenate(
        [
            grad.astype(bf16).reshape(-1)
            for grad in (grad_qkv, grad_out, grad_mlp, grad_ada, grad_down)
        ]
    ).reshape(-1, 128)
    grads_small = jnp.concatenate([*bias_sums, grad_b_ada])
    part_weights = lax.psum_scatter(grads_big, axes, scatter_dimension=0, tiled=True)
    part_biases = lax.psum_scatter(grads_small, axes, scatter_dimension=0, tiled=True)
    return (out, grad_tokens, grad_conditions, part_weights.astype(f32), part_biases)


ROWS_QKV = 3 * D * D // 128
ROWS_OUT = D * D // 128
ROWS_MLP = 2 * D * FF // 128
ROWS_ADA = 6 * D * D // 128
ROWS_DOWN = D * FF // 128
FIRST_MLP = ROWS_QKV + ROWS_OUT
FIRST_ADA = FIRST_MLP + ROWS_MLP
FIRST_DOWN = FIRST_ADA + ROWS_ADA
DEVICES = 32
SHARD = 5832
BLOCK_A = 1296
BLOCK_B = 2688
USED_DOWN = 2592
MLP_BLOCKS = 21
QKV_BLOCKS = 24
ADA_ROWS = SHARD * 128 // (6 * D)


def block_a_range(block):
    return (BLOCK_A * block, BLOCK_A * (block + 1))


def block_b_range(block):
    if block < MLP_BLOCKS:
        first = FIRST_MLP + BLOCK_B * block
        return (first, min(first + BLOCK_B, FIRST_ADA))
    first = FIRST_DOWN + USED_DOWN * (block - MLP_BLOCKS)
    return (first, min(first + USED_DOWN, FIRST_DOWN + ROWS_DOWN))


def plan_rounds(block_range, first_block, count, device_of_block):
    rounds = []
    for k in range(count):
        pairs = []
        for owner in range(DEVICES):
            block = first_block(owner) + k
            if 0 <= block < DEVICES:
                first, last = block_range(block)
                if first < (owner + 1) * SHARD and last > owner * SHARD:
                    pairs.append((owner, device_of_block(block)))
        rounds.append(pairs)
    return rounds


DOWN_OWNER = FIRST_DOWN // SHARD


def first_block_a(owner):
    return owner * SHARD // BLOCK_A


def first_block_b(owner):
    if owner < DOWN_OWNER:
        return (owner * SHARD - FIRST_MLP) // BLOCK_B
    return MLP_BLOCKS + max((owner * SHARD - FIRST_DOWN) // USED_DOWN, -1)


def starts_a():
    return -(device_index() * SHARD % BLOCK_A), BLOCK_A


def starts_b():
    me = device_index()
    low = me >= DOWN_OWNER
    first = jnp.where(low, FIRST_DOWN, FIRST_MLP)
    step = jnp.where(low, USED_DOWN, BLOCK_B)
    return -((me * SHARD - first) % step), step


PLAN_A = (BLOCK_A, block_a_range, first_block_a, 5, starts_a)
PLAN_B = (BLOCK_B, block_b_range, first_block_b, 4, starts_b)


def device_index():
    return lax.axis_index("fsdp") * lax.axis_size("dp") + lax.axis_index("dp")


def cut_pieces(shard, plan):
    block_rows, _, _, count, starts = plan
    padded = jnp.pad(shard, ((block_rows, block_rows), (0, 0)))
    first, step = starts()
    return [
        lax.dynamic_slice_in_dim(padded, block_rows + first + k * step, block_rows, 0)
        for k in range(count)
    ]


def spread(pieces, plan):
    _, block_range, first_block, count, _ = plan
    rounds = plan_rounds(block_range, first_block, count, lambda block: block)
    total = None
    for piece, pairs in zip(pieces, rounds, strict=True):
        got = lax.ppermute(piece, ("fsdp", "dp"), pairs)
        total = got if total is None else total + got
    return total


def send_back(block, plan, places):
    _, block_range, first_block, count, _ = plan
    rounds = plan_rounds(block_range, first_block, count, lambda block: device_of(places, block))
    return [
        lax.ppermute(block, ("fsdp", "dp"), [(device, owner) for owner, device in pairs])
        for pairs in rounds
    ]


def to_tiles(rows, chunks):
    return (
        rows.reshape(-1, 8, chunks, 128).transpose(0, 2, 1, 3).reshape(-1, 128)
    )


def from_tiles(rows, chunks):
    return (
        rows.reshape(-1, chunks, 8, 128).transpose(0, 2, 1, 3).reshape(-1, 128)
    )


def matrix_of_tiles(rows, height, width):
    return (
        rows.reshape(height // 8, width // 128, 8, 128)
        .transpose(0, 2, 1, 3)
        .reshape(height, width)
    )


def tiles_of_matrix(matrix):
    height, width = matrix.shape
    return (
        matrix.reshape(height // 8, 8, width // 128, 128)
        .transpose(0, 2, 1, 3)
        .reshape(-1, 128)
    )


SWAP_X = [(0, 1), (1, 0), (2, 3), (3, 2)]
SWAP_Y = [(0, 2), (2, 0), (1, 3), (3, 1)]
SWAP_CORE = [(d, d ^ 1) for d in range(8)]


def along_z(pairs):
    return [(2 * a + e, 2 * b + e) for a, b in pairs for e in range(2)]


def chips_of(*lines):
    place = {}
    for z, line in enumerate(lines):
        for f, block in enumerate(line):
            place[block] = 4 * f + z
    return place


PLACE_A = (
    chips_of((0, 1, 2, 3), (4, 5, 6, 7), (18, 19, 20, 21), (22, 23, 16, 17)),
    chips_of((8, 9, 10, 11), (12, 13, 14, 15), (24, 25, 26, 27), (28, 29, 30, 31)),
)
PLACE_B = (
    chips_of((2, 3, 4, 5), (6, 7, 8, 9), (10, 11, 12, 13), (14, 0, 15, 1)),
    chips_of((20, 16, 17, 18), (21, 22, 23, 24), (25, 26, 27, 28), (29, 19, 30, 31)),
)


def device_of(places, block):
    core = 0 if block in places[0] else 1
    return 2 * places[core][block] + core


def is_kind(places, first_of_second):
    mask = sum(1 << device_of(places, block) for block in range(first_of_second, DEVICES))
    bits = jnp.uint32(mask) >> device_index().astype(jnp.uint32)
    return bits % 2 == 1


def add_low(a, b):
    return (a.astype(jnp.float32) + b.astype(jnp.float32)).astype(jnp.bfloat16)


def pick(array, index, axis):
    return lax.dynamic_index_in_dim(array, index, axis, keepdims=False)


def first_sends(grads, block_rows):
    f = lax.axis_index("fsdp")
    y, x = f // 2, f % 2
    a, b = [part.reshape(2, 2, 4, block_rows // 2, 128) for part in grads]
    return pick(a, 1 - y, 0), pick(b, 1 - x, 1)


def over_planes(sends, axes):
    return [lax.ppermute(send, "fsdp", axis) for send, axis in zip(sends, axes, strict=True)]


def second_sends(grads, arrived, block_rows):
    f = lax.axis_index("fsdp")
    y, x = f // 2, f % 2
    a, b = [part.reshape(2, 2, 4, block_rows // 2, 128) for part in grads]
    a = add_low(pick(a, y, 0), arrived[0])
    b = add_low(pick(b, x, 1), arrived[1])
    return (pick(a, x, 0), pick(b, y, 0)), (pick(a, 1 - x, 0), pick(b, 1 - y, 0))


def plane_sums(kept, arrived):
    return jnp.concatenate([add_low(k, a) for k, a in zip(kept, arrived, strict=True)], axis=1)


def after(value, *others):
    return lax.optimization_barrier((value, others))[0]


def line_sends(planes):
    z = lax.axis_index("dp") // 2
    return [pick(planes, z ^ k, 0) for k in range(4)]


def from_line(sends):
    return [
        lax.ppermute(sends[k], "dp", [(d, d ^ (2 * k)) for d in range(8)]) for k in range(1, 4)
    ]


def sum_line(own, others):
    total = own.astype(jnp.float32)
    for other in others:
        total += other.astype(jnp.float32)
    return total


def gather_column(array):
    parts = [array] + [
        lax.ppermute(array, "dp", [(d, d ^ k) for d in range(8)]) for k in range(1, 8)
    ]
    return jnp.stack(parts)


def gather_columns(part):
    parts = [part] + [
        lax.ppermute(part, "fsdp", [(f, f ^ k) for f in range(4)]) for k in range(1, 4)
    ]
    return jnp.stack(parts).reshape(DEVICES, *part.shape[1:])


ADA_GROUPS = range(FIRST_ADA // (8 * SHARD), (FIRST_DOWN - 1) // (8 * SHARD) + 1)


def sum_to_owners(terms):
    def send(array, change, groups):
        pairs = [(8 * f + d, (8 * f + d) ^ change) for f in groups for d in range(8)]
        return lax.ppermute(array, ("fsdp", "dp"), pairs)

    terms = terms.reshape(4, 4, 2, *terms.shape[1:])
    terms = terms[:, :, 0] + send(terms[:, :, 1], 1, ADA_GROUPS)
    terms = terms[0] + sum(send(terms[k], 8 * k, ADA_GROUPS) for k in range(1, 4))
    return terms[0] + sum(send(terms[k], 2 * k, range(4)) for k in range(1, 4))


def mlp_both_ways(x, g, bias, gathered):
    f32, bf16 = jnp.float32, jnp.bfloat16
    rows = x.shape[0]
    tile = 512
    steps = FF // tile
    full = BLOCK_B // 8
    used = USED_DOWN // 8
    wide = 2 * FF // 128
    chunks = D // 128
    across = (((1,), (1,)), ((), ()))

    def body(x_ref, g_ref, bias_g_ref, bias_u_ref, source, *rest):
        hid_ref, gg_ref, gu_ref, branch_ref, gin_ref, sum_g_ref, sum_u_ref, *rest = rest
        mix_ref, down_ref, sem = rest
        step = pl.program_id(0)

        def each(act):
            stride = (BLOCK_A + BLOCK_B) // 8
            for i in range(DEVICES):
                first = i * stride + BLOCK_A // 8
                if i < MLP_BLOCKS:
                    piece = source.at[pl.ds(first, full)]
                    flat = mix_ref.reshape(MLP_BLOCKS * full, 8, 128)
                    target = flat.at[pl.ds(i * full, full)]
                else:
                    piece = source.at[pl.ds(first, used)]
                    target = down_ref.at[pl.ds((i - MLP_BLOCKS) * used, used)]
                act(pltpu.make_async_copy(piece, target, sem.at[i]))

        @pl.when(step == 0)
        def _():
            each(lambda copy: copy.start())
            branch_ref[...] = jnp.zeros_like(branch_ref)
            gin_ref[...] = jnp.zeros_like(gin_ref)
            each(lambda copy: copy.wait())

        def columns(first):
            return jnp.concatenate(
                [
                    mix_ref[: D // 8, first + i].reshape(D, 128)
                    for i in range(tile // 128)
                ],
                axis=1,
            )

        x = x_ref[...]
        w_gate, w_up = columns(tile // 128 * step), columns(wide // 2 + tile // 128 * step)
        gate = jnp.dot(x, w_gate, preferred_element_type=f32) + bias_g_ref[...]
        up = jnp.dot(x, w_up, preferred_element_type=f32) + bias_u_ref[...]
        sigma = jax.nn.sigmoid(gate)
        silu = gate * sigma
        hid = (silu * up).astype(bf16)
        hid_ref[...] = hid
        groups = tile // 8
        low_rows = down_ref[pl.ds(step * groups * chunks, groups * chunks)]
        low_rows = low_rows.reshape(groups, chunks, 8, 128)
        w_down = jnp.concatenate([low_rows[:, j].reshape(tile, 128) for j in range(chunks)], axis=1)
        branch_ref[...] += jnp.dot(hid, w_down, preferred_element_type=f32)
        g_hid = lax.dot_general(g_ref[...], w_down, across, preferred_element_type=f32)
        g_gate = (g_hid * up * sigma * (1.0 + gate * (1.0 - sigma))).astype(bf16)
        g_up = (g_hid * silu).astype(bf16)
        gg_ref[...] = g_gate
        gu_ref[...] = g_up
        sum_g_ref[...] = jnp.sum(g_gate.astype(f32), axis=0, keepdims=True)
        sum_u_ref[...] = jnp.sum(g_up.astype(f32), axis=0, keepdims=True)
        gin_ref[...] += lax.dot_general(
            g_gate, w_gate, across, preferred_element_type=f32
        ) + lax.dot_general(g_up, w_up, across, preferred_element_type=f32)

    whole = pl.BlockSpec((rows, D), lambda t: (0, 0))
    part = pl.BlockSpec((rows, tile), lambda t: (0, t))
    line = pl.BlockSpec((1, tile), lambda t: (0, t))
    return pl.pallas_call(
        body,
        grid=(steps,),
        in_specs=[
            whole,
            whole,
            line,
            pl.BlockSpec((1, tile), lambda t: (0, steps + t)),
            pl.BlockSpec(memory_space=pl.ANY),
        ],
        out_specs=[part, part, part, whole, whole, line, line],
        out_shape=[jax.ShapeDtypeStruct((rows, FF), bf16)] * 3
        + [jax.ShapeDtypeStruct((rows, D), f32)] * 2
        + [jax.ShapeDtypeStruct((1, FF), f32)] * 2,
        scratch_shapes=[
            pltpu.VMEM((MLP_BLOCKS * full // wide, wide, 8, 128), bf16),
            pltpu.VMEM(((DEVICES - MLP_BLOCKS) * used, 8, 128), bf16),
            pltpu.SemaphoreType.DMA((DEVICES,)),
        ],
        cost_estimate=pl.CostEstimate(
            flops=12 * rows * D * FF, bytes_accessed=30_000_000, transcendentals=rows * FF
        ),
        compiler_params=pltpu.CompilerParams(vmem_limit_bytes=56 << 20),
        name="mlp_both_ways",
    )(x, g, bias, bias, gathered)


def pair_product(xo, xp, go, gp):
    down = (((0,), (0,)), ((), ()))
    total = lax.dot_general(xo[...], go[...], down, preferred_element_type=jnp.float32)
    total += lax.dot_general(xp[...], gp[...], down, preferred_element_type=jnp.float32)
    return total.astype(jnp.bfloat16)


def store_tiles(out_ref, lead, first, value):
    for j in range(value.shape[1] // 128):
        out_ref[(*lead, first + j)] = value[:, 128 * j : 128 * (j + 1)]


def grads_b_core_0(in_b, g_gate, g_up):
    def body(xo, xp, gog, gpg, gou, gpu, *outs):
        for out_ref, go, gp in ((outs[0], gog, gpg), (outs[1], gou, gpu)):
            value = pair_product(xo, xp, go, gp)
            for j in range(4):
                part = value[:, 128 * j : 128 * (j + 1)].reshape(16, 7, 8, 128)
                for block in range(16):
                    out_ref[PLACE_B[0][block], :, j] = part[block]

    rows = in_b[0].shape[0]
    high = 16 * 56
    x_spec = pl.BlockSpec((rows, high), lambda t: (0, 0))
    g_spec = pl.BlockSpec((rows, 512), lambda t: (0, t))
    out = pl.pallas_call(
        body,
        grid=(FF // 512,),
        in_specs=[x_spec] * 2 + [g_spec] * 4,
        out_specs=[pl.BlockSpec((16, 7, 4, 8, 128), lambda t: (0, 0, t, 0, 0))] * 2,
        out_shape=[jax.ShapeDtypeStruct((16, 7, FF // 128, 8, 128), jnp.bfloat16)] * 2,
        compiler_params=pltpu.CompilerParams(vmem_limit_bytes=44 << 20),
        name="grads_b_core_0",
    )(*in_b, *g_gate, *g_up)
    return [part.reshape(-1, 128) for part in out]


def grads_b_core_1(in_b, g_gate, g_up, hidden, g_branch):
    bf16 = jnp.bfloat16
    rows = in_b[0].shape[0]
    mlp_steps = FF // 512
    wide = 384
    down_steps = FF // wide
    half_tiles = BLOCK_B // 16
    mlp_groups = (D - 16 * 56) // 8
    groups = (MLP_BLOCKS - 16) * 7
    half_groups = USED_DOWN // 9 // 16
    down_blocks = DEVICES - MLP_BLOCKS

    place = PLACE_B[1]

    def body(place_ref, xo7, xo8, xp7, xp8, gog, gpg, gou, gpu, ho, hp, go, gp, *outs):
        step = pl.program_id(0)

        @pl.when(step == 0)
        def _():
            for group in range(mlp_groups, groups):
                first = place[16 + group // 7] * half_tiles + group % 7 * (FF // 128)
                for out_ref in outs:
                    out_ref[pl.ds(first, FF // 128)] = jnp.zeros((FF // 128, 8, 128), bf16)
            for block in range(down_blocks):
                for half in range(2):
                    used = min(half_groups, FF // 8 - (2 * block + half) * half_groups) * 9
                    first = place[MLP_BLOCKS + block] * half_tiles + used
                    rest = half_tiles - used
                    outs[half][pl.ds(first, rest)] = jnp.zeros((rest, 8, 128), bf16)

        @pl.when(step < mlp_steps)
        def _():
            xo = jnp.concatenate([xo7[...], xo8[...]], axis=1)
            xp = jnp.concatenate([xp7[...], xp8[...]], axis=1)
            for out_ref, g_own, g_par in ((outs[0], gog, gpg), (outs[1], gou, gpu)):
                value = pair_product(xo, xp, g_own, g_par)
                for group in range(mlp_groups):
                    first = place[16 + group // 7] * half_tiles + group % 7 * (FF // 128)
                    store_tiles(
                        out_ref,
                        (),
                        first + step * 4,
                        value[8 * group : 8 * group + 8],
                    )

        def down_step(phase):
            value = pair_product(ho, hp, go, gp)
            for group in range(wide // 8):
                at = (step - mlp_steps) * (wide // 8) + group
                half = (phase * (wide // 8) + group) // half_groups % 2
                first = place_ref[at // (2 * half_groups)] * half_tiles + (at % half_groups) * 9
                store_tiles(outs[half], (), first, value[8 * group : 8 * group + 8])

        for phase in range(3):
            pl.when((step >= mlp_steps) & ((step - mlp_steps) % 3 == phase))(
                lambda phase=phase: down_step(phase)
            )

    x_specs = [pl.BlockSpec((rows, 128), lambda t: (0, 7)), pl.BlockSpec((rows, 128), lambda t: (0, 8))]
    g_spec = pl.BlockSpec((rows, 512), lambda t: (0, jnp.minimum(t, mlp_steps - 1)))
    h_spec = pl.BlockSpec((rows, wide), lambda t: (0, jnp.maximum(t - mlp_steps, 0)))
    b_spec = pl.BlockSpec((rows, D), lambda t: (0, 0))
    shape = (16 * half_tiles, 8, 128)
    down_place = jnp.asarray([place[MLP_BLOCKS + i] for i in range(down_blocks)], jnp.int32)
    out = pl.pallas_call(
        body,
        grid=(mlp_steps + down_steps,),
        in_specs=[pl.BlockSpec(memory_space=pltpu.SMEM)]
        + x_specs * 2
        + [g_spec] * 4
        + [h_spec] * 2
        + [b_spec] * 2,
        out_specs=[pl.BlockSpec(shape, lambda t: (0, 0, 0))] * 2,
        out_shape=[jax.ShapeDtypeStruct(shape, bf16)] * 2,
        compiler_params=pltpu.CompilerParams(vmem_limit_bytes=44 << 20),
        name="grads_b_core_1",
    )(down_place, in_b[0], in_b[0], in_b[1], in_b[1], *g_gate, *g_up, *hidden, *g_branch)
    return [part.reshape(-1, 128) for part in out]


def grads_a(core, in_a, g_proj, att, g_branch):
    rows = in_a[0].shape[0]
    steps = 3 * D // 384
    place = PLACE_A[core]

    def store_qkv(value, first_block, step, outs):
        for group in range(48):
            block, half, low = first_block + group // 6, group // 3 % 2, group % 3
            store_tiles(
                outs[half],
                (place[block],),
                low * 27 + step * 3,
                value[8 * group : 8 * group + 8],
            )

    def body(xo, xp, go, gp, zo, zp, bo, bp, *outs):
        step = pl.program_id(0)

        @pl.when(step < steps)
        def _():
            store_qkv(pair_product(xo, xp, go, gp), 8 * core, step, outs)
            if core == 0:
                store_qkv(pair_product(zo, zp, go, gp), 16, step, outs)

        if core == 1:

            @pl.when(step >= steps)
            def _():
                value = pair_product(zo, zp, bo, bp)
                for group in range(144):
                    block, half, low = QKV_BLOCKS + group // 18, group // 9 % 2, group % 9
                    store_tiles(
                        outs[half],
                        (place[block],),
                        low * 9 + (step - steps) * 3,
                        value[8 * group : 8 * group + 8],
                    )

    x_spec = pl.BlockSpec((rows, 384), lambda t: (0, core))
    g_spec = pl.BlockSpec((rows, 384), lambda t: (0, jnp.minimum(t, steps - 1)))
    if core == 0:
        z_spec, z = pl.BlockSpec((rows, 384), lambda t: (0, 2)), in_a
        b_spec, count = pl.BlockSpec((rows, 384), lambda t: (0, 0)), steps
    else:
        z_spec, z = pl.BlockSpec((rows, D), lambda t: (0, 0)), att
        b_spec = pl.BlockSpec((rows, 384), lambda t: (0, jnp.maximum(t - steps, 0)))
        count = steps + D // 384
    shape = (16, 81, 8, 128)
    out = pl.pallas_call(
        body,
        grid=(count,),
        in_specs=[x_spec] * 2 + [g_spec] * 2 + [z_spec] * 2 + [b_spec] * 2,
        out_specs=[pl.BlockSpec(shape, lambda t: (0, 0, 0, 0))] * 2,
        out_shape=[jax.ShapeDtypeStruct(shape, jnp.bfloat16)] * 2,
        compiler_params=pltpu.CompilerParams(vmem_limit_bytes=44 << 20),
        name=f"grads_a_core_{core}",
    )(*in_a, *g_proj, *z, *g_branch)
    return [part.reshape(-1, 128) for part in out]


def gathered_weights(pieces_a, pieces_b):
    me = device_index()
    block_a = spread(pieces_a, PLAN_A)
    block_a = jnp.where(me < QKV_BLOCKS, to_tiles(block_a, 27), to_tiles(block_a, 9))
    block_b = spread(pieces_b, PLAN_B)
    block_b = jnp.where(
        me < MLP_BLOCKS,
        to_tiles(block_b, 48),
        jnp.pad(to_tiles(block_b[:USED_DOWN], 9), ((0, BLOCK_B - USED_DOWN), (0, 0))),
    )
    block = jnp.concatenate([block_a, block_b])
    return lax.all_gather(block, ("fsdp", "dp"), axis=0, tiled=True).reshape(-1, 8, 128)


def head_indicator():
    feature = lax.broadcasted_iota(jnp.int32, (D, 128), 0)
    head = lax.broadcasted_iota(jnp.int32, (D, 128), 1)
    return ((feature >= head * HEAD_DIM) & (feature < (head + 1) * HEAD_DIM)).astype(jnp.bfloat16)


def two_parts(value):
    high = value.astype(jnp.bfloat16)
    return high, (value - high.astype(jnp.float32)).astype(jnp.bfloat16)


def head_means(value, indicator):
    high, low = two_parts(value)
    total = jnp.dot(high, indicator, preferred_element_type=jnp.float32)
    total += jnp.dot(low, indicator, preferred_element_type=jnp.float32)
    return total * (1.0 / HEAD_DIM)


def over_heads(value, indicator):
    high, low = two_parts(value)
    across = (((1,), (1,)), ((), ()))
    total = lax.dot_general(high, indicator, across, preferred_element_type=jnp.float32)
    return total + lax.dot_general(low, indicator, across, preferred_element_type=jnp.float32)


def turned(value):
    quarter = HEAD_DIM // 4
    feature = lax.broadcasted_iota(jnp.int32, value.shape, 1) % (2 * quarter)
    ahead = pltpu.roll(value, D - quarter, 1)
    behind = pltpu.roll(value, quarter, 1)
    return jnp.where(feature < quarter, -ahead, behind)


def heads_of(ref):
    return [ref[:, HEAD_DIM * h : HEAD_DIM * (h + 1)] for h in range(HEADS)]


ACROSS = (((1,), (1,)), ((), ()))
DOWN = (((0,), (0,)), ((), ()))


def attention_forward(projected, cosines, sines):
    f32, bf16 = jnp.float32, jnp.bfloat16
    rows = projected.shape[0]
    length = cosines.shape[0]
    scale = 1.0 / math.sqrt(HEAD_DIM)

    def body(proj_ref, cos_ref, sin_ref, ind_ref, q_ref, k_ref, v_ref, att_ref, log_ref):
        indicator = ind_ref[...]
        for part, ref in ((0, q_ref), (1, k_ref)):
            value = proj_ref[:, D * part : D * (part + 1)]
            inverse = lax.rsqrt(head_means(value * value, indicator) + eps_norm)
            norm = value * over_heads(inverse, indicator)
            ref[...] = (norm * cos_ref[...] + turned(norm) * sin_ref[...]).astype(bf16)
        v_ref[...] = proj_ref[:, 2 * D :].astype(bf16)
        logs = []
        for h in range(HEADS):
            at = slice(HEAD_DIM * h, HEAD_DIM * (h + 1))
            scores = (
                lax.dot_general(q_ref[:, at], k_ref[:, at], ACROSS, preferred_element_type=f32)
                * scale
            )
            top = jnp.max(scores, axis=1, keepdims=True)
            log_total = top + jnp.log(jnp.sum(jnp.exp(scores - top), axis=1, keepdims=True))
            probs = jnp.exp(scores - log_total).astype(bf16)
            att_ref[:, at] = jnp.dot(probs, v_ref[:, at], preferred_element_type=f32).astype(bf16)
            log_ref[:, h : h + 1] = log_total

    wide = pl.BlockSpec((length, D), lambda i: (i, 0))
    table = pl.BlockSpec((length, D), lambda i: (0, 0))
    return pl.pallas_call(
        body,
        grid=(rows // length,),
        in_specs=[
            pl.BlockSpec((length, 3 * D), lambda i: (i, 0)),
            table,
            table,
            pl.BlockSpec((D, 128), lambda i: (0, 0)),
        ],
        out_specs=[wide] * 4 + [pl.BlockSpec((length, HEADS), lambda i: (i, 0))],
        out_shape=[jax.ShapeDtypeStruct((rows, D), bf16)] * 4
        + [jax.ShapeDtypeStruct((rows, HEADS), f32)],
        cost_estimate=pl.CostEstimate(
            flops=8 * rows * length * D, bytes_accessed=20_000_000, transcendentals=40_000_000
        ),
        compiler_params=pltpu.CompilerParams(vmem_limit_bytes=44 << 20),
        name="attention_forward",
    )(projected, cosines, sines, head_indicator())


def attention_backward(projected, queries, keys, values, log_total, g_attended, cosines, sines):
    f32, bf16 = jnp.float32, jnp.bfloat16
    rows = projected.shape[0]
    length = cosines.shape[0]
    scale = 1.0 / math.sqrt(HEAD_DIM)

    def body(proj_ref, q_ref, k_ref, v_ref, log_ref, g_ref, cos_ref, sin_ref, ind_ref, *rest):
        out_ref, sum_ref, gq_ref, gk_ref, gv_ref = rest
        for h in range(HEADS):
            at = slice(HEAD_DIM * h, HEAD_DIM * (h + 1))
            q, k, v, g = q_ref[:, at], k_ref[:, at], v_ref[:, at], g_ref[:, at]
            scores = lax.dot_general(q, k, ACROSS, preferred_element_type=f32) * scale
            probs = jnp.exp(scores - log_ref[:, h : h + 1])
            g_probs = lax.dot_general(g, v, ACROSS, preferred_element_type=f32)
            gv_ref[:, at] = lax.dot_general(
                probs.astype(bf16), g, DOWN, preferred_element_type=f32
            )
            inner = jnp.sum(probs * g_probs, axis=1, keepdims=True)
            g_scores = (probs * (g_probs - inner)).astype(bf16)
            gq_ref[:, at] = jnp.dot(g_scores, k, preferred_element_type=f32) * scale
            gk_ref[:, at] = (
                lax.dot_general(g_scores, q, DOWN, preferred_element_type=f32) * scale
            )
        indicator = ind_ref[...]
        for part, ref in ((0, gq_ref), (1, gk_ref)):
            value = proj_ref[:, D * part : D * (part + 1)]
            inverse = over_heads(
                lax.rsqrt(head_means(value * value, indicator) + eps_norm), indicator
            )
            norm = value * inverse
            back = ref[...] * cos_ref[...] - turned(ref[...]) * sin_ref[...]
            mean = over_heads(head_means(back * norm, indicator), indicator)
            out_ref[:, D * part : D * (part + 1)] = (inverse * (back - norm * mean)).astype(bf16)
        out_ref[:, 2 * D :] = gv_ref[...].astype(bf16)
        sum_ref[0] = jnp.sum(out_ref[...].astype(f32), axis=0, keepdims=True)

    wide = pl.BlockSpec((length, D), lambda i: (i, 0))
    table = pl.BlockSpec((length, D), lambda i: (0, 0))
    images = rows // length
    return pl.pallas_call(
        body,
        grid=(images,),
        in_specs=[
            pl.BlockSpec((length, 2 * D), lambda i: (i, 0)),
            wide,
            wide,
            wide,
            pl.BlockSpec((length, HEADS), lambda i: (i, 0)),
            wide,
            table,
            table,
            pl.BlockSpec((D, 128), lambda i: (0, 0)),
        ],
        out_specs=[
            pl.BlockSpec((length, 3 * D), lambda i: (i, 0)),
            pl.BlockSpec((1, 1, 3 * D), lambda i: (i, 0, 0)),
        ],
        out_shape=[
            jax.ShapeDtypeStruct((rows, 3 * D), bf16),
            jax.ShapeDtypeStruct((images, 1, 3 * D), f32),
        ],
        scratch_shapes=[pltpu.VMEM((length, D), f32)] * 3,
        cost_estimate=pl.CostEstimate(flops=1000, bytes_accessed=1000, transcendentals=0),
        compiler_params=pltpu.CompilerParams(vmem_limit_bytes=44 << 20),
        name="attention_backward",
    )(projected, queries, keys, values, log_total, g_attended, cosines, sines, head_indicator())


def split_a(gathered):
    block = BLOCK_A // 8

    def body(all_ref, qkv_ref, out_ref, sem):
        copies = []
        for i in range(DEVICES):
            ref, first = (qkv_ref, 0) if i < QKV_BLOCKS else (out_ref, QKV_BLOCKS)
            copies.append(
                pltpu.make_async_copy(
                    all_ref.at[pl.ds(i * (BLOCK_A + BLOCK_B) // 8, block)],
                    ref.at[pl.ds((i - first) * block, block)],
                    sem.at[i],
                )
            )
        for copy in copies:
            copy.start()
        for copy in copies:
            copy.wait()

    w_qkv, w_out = pl.pallas_call(
        body,
        in_specs=[pl.BlockSpec(memory_space=pl.ANY)],
        out_specs=[pl.BlockSpec(memory_space=pltpu.VMEM)] * 2,
        out_shape=[
            jax.ShapeDtypeStruct((ROWS_QKV // 8, 8, 128), jnp.bfloat16),
            jax.ShapeDtypeStruct((ROWS_OUT // 8, 8, 128), jnp.bfloat16),
        ],
        scratch_shapes=[pltpu.SemaphoreType.DMA((DEVICES,))],
        compiler_params=pltpu.CompilerParams(vmem_limit_bytes=40 << 20),
        name="split_a",
    )(gathered)
    return matrix_of_tiles(w_qkv, D, 3 * D), matrix_of_tiles(w_out, D, D)


def owned_rows(back_a, back_b, grad_ada):
    first_a, step_a = starts_a()
    first_b, step_b = starts_b()
    me = device_index()
    numbers = jnp.stack(
        [jnp.asarray(v, jnp.int32) for v in (first_a, step_a, first_b, step_b, me * SHARD)]
    )
    total = SHARD + 2 * BLOCK_B

    def body(numbers_ref, *refs):
        out_ref, sum_ref = refs[-2:]
        sum_ref[...] = jnp.zeros_like(sum_ref)
        for refs_of, at, rows in (
            (refs[: len(back_b)], 2, BLOCK_B),
            (refs[len(back_b) : len(back_b) + len(back_a)], 0, BLOCK_A),
        ):
            for k, ref in enumerate(refs_of):
                start = BLOCK_B + numbers_ref[at] + k * numbers_ref[at + 1]
                start = pl.multiple_of(jnp.clip(start, 0, total - rows), 8)
                sum_ref[pl.ds(start, rows)] += ref[...].astype(jnp.float32)
        row = numbers_ref[4] + lax.broadcasted_iota(jnp.int32, (SHARD, 128), 0)
        out_ref[...] = jnp.where(
            (row >= FIRST_ADA) & (row < FIRST_DOWN),
            refs[-3][...],
            sum_ref[pl.ds(BLOCK_B, SHARD)],
        )

    return pl.pallas_call(
        body,
        in_specs=[pl.BlockSpec(memory_space=pltpu.SMEM)]
        + [pl.BlockSpec(memory_space=pltpu.VMEM)] * (len(back_a) + len(back_b) + 1),
        out_specs=pl.BlockSpec(memory_space=pltpu.VMEM),
        out_shape=jax.ShapeDtypeStruct((SHARD, 128), jnp.float32),
        scratch_shapes=[pltpu.VMEM((total, 128), jnp.float32)],
        compiler_params=pltpu.CompilerParams(vmem_limit_bytes=40 << 20),
        name="owned_rows",
    )(numbers, *back_b, *back_a, grad_ada)


def on_device_32(tokens, conditions, cotangent, slot_mask, weight_flat, bias_flat):
    f32 = jnp.float32
    bf16 = jnp.bfloat16
    axes = ("fsdp", "dp")
    me = device_index()
    core = lax.axis_index("dp") % 2
    slots = conditions.shape[0]
    images = slots * DEVICES
    length = GRID * GRID
    rows_all = slots * length
    cond_count = slots * D
    bias_count = bias_flat.shape[0]
    packed_rows = -(-(cond_count + bias_count) // 128)
    packed = jnp.concatenate(
        [
            conditions.reshape(-1),
            bias_flat,
            jnp.zeros(packed_rows * 128 - cond_count - bias_count, bf16),
        ]
    ).reshape(packed_rows, 128)
    pieces = cut_pieces(weight_flat, PLAN_A), cut_pieces(weight_flat, PLAN_B)
    packed, pieces = lax.optimization_barrier((packed, pieces))
    gathered = gathered_weights(*pieces)
    packed_all = gather_columns(gather_column(packed)).reshape(DEVICES, -1)
    cond_all = packed_all[:, :cond_count].reshape(images, D).astype(f32)
    places = lax.broadcasted_iota(jnp.int32, (DEVICES, DEVICES), 0)
    others = lax.broadcasted_iota(jnp.int32, (DEVICES, DEVICES), 1)
    chosen = ((places ^ me) == others).astype(bf16)
    bias_all = jnp.dot(
        chosen, packed_all[:, cond_count : cond_count + bias_count], preferred_element_type=f32
    ).reshape(-1)
    b_qkv = bias_all[: 3 * D]
    b_out = bias_all[3 * D : 4 * D]
    b_mlp = bias_all[4 * D : 4 * D + 2 * FF]
    b_ada = bias_all[4 * D + 2 * FF :]
    ada_local = weight_flat.reshape(ADA_ROWS, 6 * D)
    ada_start = jnp.clip(
        me * ADA_ROWS - FIRST_ADA * 128 // (6 * D) + ADA_ROWS, 0, D + ADA_ROWS
    )
    cond_act = jax.nn.silu(cond_all).astype(bf16)
    cond_rows = lax.dynamic_slice_in_dim(
        jnp.pad(cond_act.T, ((ADA_ROWS, ADA_ROWS), (0, 0))), ada_start, ADA_ROWS, 0
    )
    cond_ordered = jnp.dot(
        chosen, cond_act.reshape(DEVICES, cond_count), preferred_element_type=f32
    ).astype(bf16)
    rows_ordered = lax.dynamic_slice_in_dim(
        jnp.pad(cond_ordered.reshape(images, D).T, ((ADA_ROWS, ADA_ROWS), (0, 0))),
        ada_start,
        ADA_ROWS,
        0,
    )
    terms = jnp.einsum("km,kn->mn", cond_rows, ada_local, preferred_element_type=f32)
    modulation = sum_to_owners(terms.reshape(DEVICES, slots, 6 * D)) + b_ada
    w_qkv, w_out = split_a(gathered)

    def share(array):
        return (array, lax.ppermute(array, "dp", SWAP_CORE))

    cosines, sines = [jnp.tile(table[:, 0], (1, HEADS)) for table in rope_tables()]
    mask_f = slot_mask.astype(f32)[:, None, None]
    x_f = tokens.astype(f32).reshape(slots, length, D)
    shift_a, scale_a, gate_a, shift_b, scale_b, gate_b = [
        modulation[:, None, place * D : (place + 1) * D] for place in range(6)
    ]
    g_out = cotangent.astype(f32).reshape(slots, length, D) * mask_f
    g_branch_b = (gate_b * g_out).astype(bf16).reshape(rows_all, D)
    normed_a, inv_a = norm_parts(x_f)
    input_a = (normed_a * (1.0 + scale_a) + shift_a).astype(bf16).reshape(rows_all, D)
    projected = jnp.dot(input_a, w_qkv, preferred_element_type=f32) + b_qkv
    queries, keys, values, attended, log_total = attention_forward(projected, cosines, sines)
    branch_a = (jnp.dot(attended, w_out, preferred_element_type=f32) + b_out).reshape(
        slots, length, D
    )
    middle = x_f + gate_a * branch_a
    normed_b, inv_b = norm_parts(middle)
    input_b = (normed_b * (1.0 + scale_b) + shift_b).astype(bf16).reshape(rows_all, D)
    early = [share(array) for array in (input_a, attended, input_b, g_branch_b)]
    input_b = after(input_b, early[0], early[3])
    hidden, g_gate, g_up, branch_b, g_input_b, sum_gate, sum_up = mlp_both_ways(
        input_b, g_branch_b, b_mlp.reshape(1, 2 * FF), gathered
    )
    shared_mlp = [share(array) for array in (g_gate, g_up, hidden)]
    branch_b = branch_b.reshape(slots, length, D)
    g_input_b = g_input_b.reshape(slots, length, D)
    out = ((middle + gate_b * branch_b) * mask_f).astype(bf16).reshape(rows_all, D)
    g_gate_b = jnp.sum(g_out * branch_b, axis=1)
    g_shift_b = jnp.sum(g_input_b, axis=1)
    g_scale_b = jnp.sum(g_input_b * normed_b, axis=1)
    g_middle = g_out + norm_back(g_input_b * (1.0 + scale_b), normed_b, inv_b)
    g_branch_a = (gate_a * g_middle).astype(bf16).reshape(rows_all, D)
    g_gate_a = jnp.sum(g_middle * branch_a, axis=1)
    grad_b_out = jnp.sum(g_branch_a.astype(f32), axis=0)
    shared_branch_a = share(g_branch_a)
    grads_b = lax.cond(
        core == 0,
        lambda: grads_b_core_0(early[2], shared_mlp[0], shared_mlp[1]),
        lambda: grads_b_core_1(early[2], *shared_mlp, early[3]),
    )
    orders = (SWAP_Y, SWAP_X), (SWAP_X, SWAP_Y)
    sends_b = first_sends(grads_b, BLOCK_B)
    arrived = over_planes(sends_b, orders[0])
    g_attended = jnp.einsum(
        "re,de->rd", after(g_branch_a, sends_b), w_out, preferred_element_type=f32
    )
    g_attended = g_attended.astype(bf16)
    g_projected, proj_sums = attention_backward(
        projected, queries, keys, values, log_total, g_attended, cosines, sines
    )
    grad_b_qkv = jnp.sum(proj_sums, axis=(0, 1))
    shared_proj = share(g_projected)
    g_input_a = jnp.einsum("re,de->rd", g_projected, w_qkv, preferred_element_type=f32)
    g_input_a = lax.optimization_barrier(g_input_a).reshape(slots, length, D)
    g_shift_a = jnp.sum(g_input_a, axis=1)
    g_scale_a = jnp.sum(g_input_a * normed_a, axis=1)
    g_modulation = jnp.concatenate(
        [g_shift_a, g_scale_a, g_gate_a, g_shift_b, g_scale_b, g_gate_b], axis=1
    ).astype(bf16)
    bias_sums = [grad_b_qkv, grad_b_out, sum_gate.reshape(-1), sum_up.reshape(-1)]
    small = jnp.concatenate([g_modulation.reshape(-1)] + [b.astype(bf16) for b in bias_sums])
    kept_b, sends_b = second_sends(grads_b, after(arrived, small), BLOCK_B)
    shared_proj = after(shared_proj, sends_b)
    small_all = lax.all_gather(small.reshape(-1, 128), axes, axis=0, tiled=True)
    made_a = lax.cond(
        core == 0,
        lambda: grads_a(0, early[0], shared_proj, early[1], shared_branch_a),
        lambda: grads_a(1, early[0], shared_proj, early[1], shared_branch_a),
    )
    sends_a = first_sends(made_a, BLOCK_A)
    planes_b = plane_sums(kept_b, after(over_planes(sends_b, orders[1]), sends_a))
    sends_b = line_sends(planes_b)
    arrived = after(over_planes(sends_a, orders[0]), sends_b)
    kept_a, sends_a = second_sends(made_a, arrived, BLOCK_A)
    line_b = after(from_line(sends_b), sends_a)
    grad_tokens = g_middle + norm_back(g_input_a * (1.0 + scale_a), normed_a, inv_a)
    sum_b = sum_line(sends_b[0], line_b).astype(bf16)
    halves = sum_b.reshape(2, BLOCK_B // 2, 128)
    sum_b = jnp.where(
        jnp.logical_not(is_kind(PLACE_B, MLP_BLOCKS)),
        jnp.concatenate(
            [from_tiles(half, 24).reshape(-1, 24, 128) for half in halves], axis=1
        ).reshape(-1, 128),
        jnp.pad(
            from_tiles(halves[:, : USED_DOWN // 2].reshape(-1, 128), 9),
            ((0, BLOCK_B - USED_DOWN), (0, 0)),
        ),
    )
    planes_a = plane_sums(kept_a, after(over_planes(sends_a, orders[1]), sum_b))
    sends_a = line_sends(planes_a)
    small_all = after(small_all, sends_a).reshape(DEVICES, -1)
    g_mod_all = small_all[:, : slots * 6 * D].reshape(images, 6 * D)
    g_cond_rows = jnp.einsum("mn,kn->mk", g_mod_all, ada_local, preferred_element_type=f32)
    back_b = send_back(after(sum_b, sends_a), PLAN_B, PLACE_B)
    sum_a = sum_line(sends_a[0], after(from_line(sends_a), back_b)).astype(bf16)
    sum_a = jnp.where(is_kind(PLACE_A, QKV_BLOCKS), from_tiles(sum_a, 9), from_tiles(sum_a, 27))
    back_a = send_back(sum_a, PLAN_A, PLACE_A)
    grad_biases = jnp.concatenate(
        [
            jnp.sum(small_all[:, slots * 6 * D :].astype(f32), axis=0),
            jnp.sum(g_mod_all.astype(f32), axis=0),
        ]
    )
    part_biases = lax.dynamic_slice_in_dim(grad_biases, me * bias_count, bias_count, 0)
    grad_ada = jnp.einsum("km,mn->kn", rows_ordered, g_mod_all, preferred_element_type=f32)
    came = lax.all_to_all(
        g_cond_rows.reshape(DEVICES, slots, ADA_ROWS), axes, split_axis=0, concat_axis=0, tiled=True
    )
    first = FIRST_ADA * 128 // (6 * D)
    g_cond = came.transpose(1, 0, 2).reshape(slots, DEVICES * ADA_ROWS)[:, first : first + D]
    cond_f = conditions.astype(f32)
    sigma_cond = jax.nn.sigmoid(cond_f)
    grad_conditions = g_cond * sigma_cond * (1.0 + cond_f * (1.0 - sigma_cond))
    part_weights = owned_rows(back_a, back_b, grad_ada.reshape(SHARD, 128))
    return (out, grad_tokens.reshape(rows_all, D), grad_conditions, part_weights, part_biases)


def solution(mesh):
    chosen = on_device_32 if dict(mesh.shape) == {"fsdp": 4, "dp": 8} else on_device_plain
    return jax.shard_map(
        chosen,
        mesh=mesh,
        in_specs=(
            P(("fsdp", "dp"), None),
            P(("fsdp", "dp"), None),
            P(("fsdp", "dp"), None),
            P(("fsdp", "dp")),
            P(("fsdp", "dp"), None),
            P(("fsdp", "dp")),
        ),
        out_specs=(
            P(("fsdp", "dp"), None),
            P(("fsdp", "dp"), None),
            P(("fsdp", "dp"), None),
            P(("fsdp", "dp"), None),
            P(("fsdp", "dp")),
        ),
        check_vma=False,
    )
```

```python
import math

import jax
import jax.numpy as jnp
from jax import lax
from jax.experimental import pallas as pl
from jax.experimental.pallas import tpu as pltpu
import numpy as np
from jax.sharding import PartitionSpec as P

D = 1152
HEADS = 16
HEAD_DIM = 72
FF = 3072
GRID = 16


eps_norm = 1e-06


def unpack_weights(weight_all, bias_all):
    flat = weight_all.reshape(-1)
    layouts = ((D, 3 * D), (D, D), (D, 2 * FF), (D, 6 * D), (FF, D))
    pieces = []
    offset = 0
    for layout in layouts:
        amount = layout[0] * layout[1]
        pieces.append(flat[offset : offset + amount].reshape(layout))
        offset = offset + amount
    offset = 0
    for amount in (3 * D, D, 2 * FF, 6 * D):
        pieces.append(bias_all[offset : offset + amount])
        offset = offset + amount
    return tuple(pieces)


def rope_tables():
    quarter = HEAD_DIM // 4
    places = jnp.arange(GRID * GRID, dtype=jnp.int32)
    rows_at = (places // GRID).astype(jnp.float32)
    cols_at = (places % GRID).astype(jnp.float32)
    freqs = 10000.0 ** (-jnp.arange(quarter, dtype=jnp.float32) / quarter)
    along_rows = rows_at[:, None] * freqs[None, :]
    along_cols = cols_at[:, None] * freqs[None, :]
    angles = jnp.concatenate([along_rows, along_rows, along_cols, along_cols], axis=1)
    return (jnp.cos(angles)[:, None, :], jnp.sin(angles)[:, None, :])


def turn_half(values):
    quarter = values.shape[-1] // 4
    first = values[..., :quarter]
    second = values[..., quarter : 2 * quarter]
    third = values[..., 2 * quarter : 3 * quarter]
    fourth = values[..., 3 * quarter :]
    return jnp.concatenate([-second, first, -fourth, third], axis=-1)


def norm_parts(values):
    centred = values - jnp.mean(values, -1, keepdims=True)
    inverse = lax.rsqrt(jnp.mean(centred * centred, -1, keepdims=True) + eps_norm)
    return (centred * inverse, inverse)


def norm_back(grad_normed, normed, inverse):
    return inverse * (
        grad_normed
        - jnp.mean(grad_normed, -1, keepdims=True)
        - normed * jnp.mean(grad_normed * normed, -1, keepdims=True)
    )


def rms_parts(values):
    inverse = lax.rsqrt(jnp.mean(values * values, -1, keepdims=True) + eps_norm)
    return (values * inverse, inverse)


def rms_back(grad_normed, normed, inverse):
    return inverse * (grad_normed - normed * jnp.mean(grad_normed * normed, -1, keepdims=True))


def compute_block(tokens, cotangent, slot_mask, modulation, weights, biases):
    f32 = jnp.float32
    bf16 = jnp.bfloat16
    w_qkv, w_out, w_mlp, w_down = weights
    b_qkv, b_out, b_mlp = biases
    slots = slot_mask.shape[0]
    length = GRID * GRID
    rows_all = slots * length
    scale = 1.0 / math.sqrt(HEAD_DIM)
    heads_shape = (slots, length, HEADS, HEAD_DIM)
    cosines, sines = rope_tables()
    mask_f = slot_mask.astype(f32)[:, None, None]
    x_f = tokens.astype(f32).reshape(slots, length, D)
    shift_a, scale_a, gate_a, shift_b, scale_b, gate_b = [
        modulation[:, None, place * D : (place + 1) * D] for place in range(6)
    ]
    normed_a, inv_a = norm_parts(x_f)
    attention_input = (normed_a * (1.0 + scale_a) + shift_a).astype(bf16).reshape(rows_all, D)
    projected_output = (
        jnp.dot(attention_input, w_qkv, preferred_element_type=f32) + b_qkv.astype(f32)
    ).reshape(slots, length, 3 * D)
    q_norm, inv_q = rms_parts(projected_output[..., :D].reshape(heads_shape))
    k_norm, inv_k = rms_parts(projected_output[..., D : 2 * D].reshape(heads_shape))
    queries = (q_norm * cosines + turn_half(q_norm) * sines).astype(bf16)
    keys = (k_norm * cosines + turn_half(k_norm) * sines).astype(bf16)
    values = projected_output[..., 2 * D :].reshape(heads_shape).astype(bf16)
    scores = jnp.einsum("slhe,smhe->shlm", queries, keys, preferred_element_type=f32) * scale
    row_max = jnp.max(scores, -1, keepdims=True)
    log_total = row_max + jnp.log(jnp.sum(jnp.exp(scores - row_max), -1, keepdims=True))
    probs_low = jnp.exp(scores - log_total).astype(bf16)
    attention_output = (
        jnp.einsum("shlm,smhe->slhe", probs_low, values, preferred_element_type=f32)
        .astype(bf16)
        .reshape(rows_all, D)
    )
    attention_branch = (
        jnp.dot(attention_output, w_out, preferred_element_type=f32) + b_out.astype(f32)
    ).reshape(slots, length, D)
    middle = x_f + gate_a * attention_branch
    normed_b, inv_b = norm_parts(middle)
    feedforward_input = (normed_b * (1.0 + scale_b) + shift_b).astype(bf16).reshape(rows_all, D)
    mixed_tokens = jnp.dot(feedforward_input, w_mlp, preferred_element_type=f32) + b_mlp.astype(
        f32
    )
    gate_part = mixed_tokens[:, :FF]
    up_part = mixed_tokens[:, FF:]
    hidden_state = (jax.nn.silu(gate_part) * up_part).astype(bf16)
    feedforward_branch = jnp.dot(hidden_state, w_down, preferred_element_type=f32).reshape(
        slots, length, D
    )
    out = ((middle + gate_b * feedforward_branch) * mask_f).astype(bf16).reshape(rows_all, D)
    g_out = cotangent.astype(f32).reshape(slots, length, D) * mask_f
    g_branch_b = (gate_b * g_out).astype(bf16).reshape(rows_all, D)
    g_gate_b = jnp.sum(g_out * feedforward_branch, axis=1)
    g_hidden = jnp.einsum("rd,fd->rf", g_branch_b, w_down, preferred_element_type=f32)
    sigma_gate = jax.nn.sigmoid(gate_part)
    g_mixed = jnp.concatenate(
        [
            g_hidden * up_part * sigma_gate * (1.0 + gate_part * (1.0 - sigma_gate)),
            g_hidden * (gate_part * sigma_gate),
        ],
        axis=1,
    ).astype(bf16)
    grad_b_mlp = jnp.sum(g_mixed.astype(f32), axis=0)
    g_input_b = jnp.einsum("rf,df->rd", g_mixed, w_mlp, preferred_element_type=f32).reshape(
        slots, length, D
    )
    g_shift_b = jnp.sum(g_input_b, axis=1)
    g_scale_b = jnp.sum(g_input_b * normed_b, axis=1)
    g_middle = g_out + norm_back(g_input_b * (1.0 + scale_b), normed_b, inv_b)
    g_branch_a = (gate_a * g_middle).astype(bf16).reshape(rows_all, D)
    g_gate_a = jnp.sum(g_middle * attention_branch, axis=1)
    grad_b_out = jnp.sum(g_branch_a.astype(f32), axis=0)
    g_attended = (
        jnp.einsum("re,de->rd", g_branch_a, w_out, preferred_element_type=f32)
        .astype(bf16)
        .reshape(heads_shape)
    )
    scores = jnp.einsum("slhe,smhe->shlm", queries, keys, preferred_element_type=f32) * scale
    probs = jnp.exp(scores - log_total)
    probs_low = probs.astype(bf16)
    g_probs = jnp.einsum("slhe,smhe->shlm", g_attended, values, preferred_element_type=f32)
    g_values = jnp.einsum("shlm,slhe->smhe", probs_low, g_attended, preferred_element_type=f32)
    g_scores = (probs * (g_probs - jnp.sum(probs * g_probs, -1, keepdims=True))).astype(bf16)
    g_queries = jnp.einsum("shlm,smhe->slhe", g_scores, keys, preferred_element_type=f32) * scale
    g_keys = jnp.einsum("shlm,slhe->smhe", g_scores, queries, preferred_element_type=f32) * scale
    g_q = rms_back(g_queries * cosines - turn_half(g_queries) * sines, q_norm, inv_q)
    g_k = rms_back(g_keys * cosines - turn_half(g_keys) * sines, k_norm, inv_k)
    g_projected = jnp.concatenate(
        [g_q.reshape(rows_all, D), g_k.reshape(rows_all, D), g_values.reshape(rows_all, D)], axis=1
    ).astype(bf16)
    grad_b_qkv = jnp.sum(g_projected.astype(f32), axis=0)
    g_input_a = jnp.einsum("re,de->rd", g_projected, w_qkv, preferred_element_type=f32).reshape(
        slots, length, D
    )
    g_shift_a = jnp.sum(g_input_a, axis=1)
    g_scale_a = jnp.sum(g_input_a * normed_a, axis=1)
    grad_tokens = g_middle + norm_back(g_input_a * (1.0 + scale_a), normed_a, inv_a)
    g_modulation = jnp.concatenate(
        [g_shift_a, g_scale_a, g_gate_a, g_shift_b, g_scale_b, g_gate_b], axis=1
    ).astype(bf16)
    pairs = (
        (attention_input, g_projected),
        (attention_output, g_branch_a),
        (feedforward_input, g_mixed),
        (hidden_state, g_branch_b),
    )
    return (
        out,
        grad_tokens.reshape(rows_all, D),
        g_modulation,
        (grad_b_qkv, grad_b_out, grad_b_mlp),
        pairs,
    )


def weight_grad(pair):
    return jnp.einsum("rd,re->de", pair[0], pair[1], preferred_element_type=jnp.float32)


def on_device_plain(tokens, conditions, cotangent, slot_mask, weight_flat, bias_flat):
    f32 = jnp.float32
    bf16 = jnp.bfloat16
    axes = ("fsdp", "dp")
    weight_all = lax.all_gather(weight_flat, axes, axis=0, tiled=True)
    bias_all = lax.all_gather(bias_flat, axes, axis=0, tiled=True)
    w_qkv, w_out, w_mlp, w_ada, w_down, b_qkv, b_out, b_mlp, b_ada = unpack_weights(
        weight_all, bias_all
    )
    cond_f = conditions.astype(f32)
    cond_act = jax.nn.silu(cond_f).astype(bf16)
    modulation = jnp.dot(cond_act, w_ada, preferred_element_type=f32) + b_ada.astype(f32)
    out, grad_tokens, g_modulation, bias_sums, pairs = compute_block(
        tokens,
        cotangent,
        slot_mask,
        modulation,
        (w_qkv, w_out, w_mlp, w_down),
        (b_qkv, b_out, b_mlp),
    )
    grad_b_ada = jnp.sum(g_modulation.astype(f32), axis=0)
    g_cond = jnp.einsum("se,de->sd", g_modulation, w_ada, preferred_element_type=f32)
    sigma_cond = jax.nn.sigmoid(cond_f)
    grad_conditions = g_cond * sigma_cond * (1.0 + cond_f * (1.0 - sigma_cond))
    grad_qkv, grad_out, grad_mlp, grad_down = [weight_grad(pair) for pair in pairs]
    grad_ada = weight_grad((cond_act, g_modulation))
    grads_big = jnp.concatenate(
        [
            grad.astype(bf16).reshape(-1)
            for grad in (grad_qkv, grad_out, grad_mlp, grad_ada, grad_down)
        ]
    ).reshape(-1, 128)
    grads_small = jnp.concatenate([*bias_sums, grad_b_ada])
    part_weights = lax.psum_scatter(grads_big, axes, scatter_dimension=0, tiled=True)
    part_biases = lax.psum_scatter(grads_small, axes, scatter_dimension=0, tiled=True)
    return (out, grad_tokens, grad_conditions, part_weights.astype(f32), part_biases)


ROWS_QKV = 3 * D * D // 128
ROWS_OUT = D * D // 128
ROWS_MLP = 2 * D * FF // 128
ROWS_ADA = 6 * D * D // 128
ROWS_DOWN = D * FF // 128
FIRST_MLP = ROWS_QKV + ROWS_OUT
FIRST_ADA = FIRST_MLP + ROWS_MLP
FIRST_DOWN = FIRST_ADA + ROWS_ADA
DEVICES = 32
SHARD = 5832
BLOCK_A = 1296
BLOCK_B = 2688
USED_DOWN = 2592
MLP_BLOCKS = 21
QKV_BLOCKS = 24
ADA_ROWS = SHARD * 128 // (6 * D)


def block_a_range(block):
    return (BLOCK_A * block, BLOCK_A * (block + 1))


def block_b_range(block):
    if block < MLP_BLOCKS:
        first = FIRST_MLP + BLOCK_B * block
        return (first, min(first + BLOCK_B, FIRST_ADA))
    first = FIRST_DOWN + USED_DOWN * (block - MLP_BLOCKS)
    return (first, min(first + USED_DOWN, FIRST_DOWN + ROWS_DOWN))


def plan_rounds(block_range, first_block, count, device_of_block):
    rounds = []
    for k in range(count):
        pairs = []
        for owner in range(DEVICES):
            block = first_block(owner) + k
            if 0 <= block < DEVICES:
                first, last = block_range(block)
                if first < (owner + 1) * SHARD and last > owner * SHARD:
                    pairs.append((owner, device_of_block(block)))
        rounds.append(pairs)
    return rounds


DOWN_OWNER = FIRST_DOWN // SHARD


def first_block_a(owner):
    return owner * SHARD // BLOCK_A


def first_block_b(owner):
    if owner < DOWN_OWNER:
        return (owner * SHARD - FIRST_MLP) // BLOCK_B
    return MLP_BLOCKS + max((owner * SHARD - FIRST_DOWN) // USED_DOWN, -1)


def starts_a():
    return -(device_index() * SHARD % BLOCK_A), BLOCK_A


def starts_b():
    me = device_index()
    low = me >= DOWN_OWNER
    first = jnp.where(low, FIRST_DOWN, FIRST_MLP)
    step = jnp.where(low, USED_DOWN, BLOCK_B)
    return -((me * SHARD - first) % step), step


PLAN_A = (BLOCK_A, block_a_range, first_block_a, 5, starts_a)
PLAN_B = (BLOCK_B, block_b_range, first_block_b, 4, starts_b)


def device_index():
    return lax.axis_index("fsdp") * lax.axis_size("dp") + lax.axis_index("dp")


def cut_pieces(shard, plan):
    block_rows, _, _, count, starts = plan
    padded = jnp.pad(shard, ((block_rows, block_rows), (0, 0)))
    first, step = starts()
    return [
        lax.dynamic_slice_in_dim(padded, block_rows + first + k * step, block_rows, 0)
        for k in range(count)
    ]


def spread(pieces, plan):
    _, block_range, first_block, count, _ = plan
    rounds = plan_rounds(block_range, first_block, count, lambda block: block)
    total = None
    for piece, pairs in zip(pieces, rounds, strict=True):
        got = lax.ppermute(piece, ("fsdp", "dp"), pairs)
        total = got if total is None else total + got
    return total


def send_back(block, plan, places):
    _, block_range, first_block, count, _ = plan
    rounds = plan_rounds(block_range, first_block, count, lambda block: device_of(places, block))
    return [
        lax.ppermute(block, ("fsdp", "dp"), [(device, owner) for owner, device in pairs])
        for pairs in rounds
    ]


def to_tiles(rows, chunks):
    return (
        rows.reshape(-1, 8, chunks, 128).transpose(0, 2, 1, 3).reshape(-1, 128)
    )


def from_tiles(rows, chunks):
    return (
        rows.reshape(-1, chunks, 8, 128).transpose(0, 2, 1, 3).reshape(-1, 128)
    )


def matrix_of_tiles(rows, height, width):
    return (
        rows.reshape(height // 8, width // 128, 8, 128)
        .transpose(0, 2, 1, 3)
        .reshape(height, width)
    )


def tiles_of_matrix(matrix):
    height, width = matrix.shape
    return (
        matrix.reshape(height // 8, 8, width // 128, 128)
        .transpose(0, 2, 1, 3)
        .reshape(-1, 128)
    )


SWAP_X = [(0, 1), (1, 0), (2, 3), (3, 2)]
SWAP_Y = [(0, 2), (2, 0), (1, 3), (3, 1)]
SWAP_CORE = [(d, d ^ 1) for d in range(8)]


def along_z(pairs):
    return [(2 * a + e, 2 * b + e) for a, b in pairs for e in range(2)]


def chips_of(*lines):
    place = {}
    for z, line in enumerate(lines):
        for f, block in enumerate(line):
            place[block] = 4 * f + z
    return place


PLACE_A = (
    chips_of((0, 1, 2, 3), (4, 5, 6, 7), (18, 19, 20, 21), (22, 23, 16, 17)),
    chips_of((8, 9, 10, 11), (12, 13, 14, 15), (24, 25, 26, 27), (28, 29, 30, 31)),
)
PLACE_B = (
    chips_of((2, 3, 4, 5), (6, 7, 8, 9), (10, 11, 12, 13), (14, 0, 15, 1)),
    chips_of((20, 16, 17, 18), (21, 22, 23, 24), (25, 26, 27, 28), (29, 19, 30, 31)),
)


def device_of(places, block):
    core = 0 if block in places[0] else 1
    return 2 * places[core][block] + core


def is_kind(places, first_of_second):
    mask = sum(1 << device_of(places, block) for block in range(first_of_second, DEVICES))
    bits = jnp.uint32(mask) >> device_index().astype(jnp.uint32)
    return bits % 2 == 1


def add_low(a, b):
    return (a.astype(jnp.float32) + b.astype(jnp.float32)).astype(jnp.bfloat16)


def pick(array, index, axis):
    return lax.dynamic_index_in_dim(array, index, axis, keepdims=False)


def first_sends(grads, block_rows):
    f = lax.axis_index("fsdp")
    y, x = f // 2, f % 2
    a, b = [part.reshape(2, 2, 4, block_rows // 2, 128) for part in grads]
    return pick(a, 1 - y, 0), pick(b, 1 - x, 1)


def over_planes(sends, axes):
    return [lax.ppermute(send, "fsdp", axis) for send, axis in zip(sends, axes, strict=True)]


def second_sends(grads, arrived, block_rows):
    f = lax.axis_index("fsdp")
    y, x = f // 2, f % 2
    a, b = [part.reshape(2, 2, 4, block_rows // 2, 128) for part in grads]
    a = add_low(pick(a, y, 0), arrived[0])
    b = add_low(pick(b, x, 1), arrived[1])
    return (pick(a, x, 0), pick(b, y, 0)), (pick(a, 1 - x, 0), pick(b, 1 - y, 0))


def plane_sums(kept, arrived):
    return jnp.concatenate([add_low(k, a) for k, a in zip(kept, arrived, strict=True)], axis=1)


def after(value, *others):
    return lax.optimization_barrier((value, others))[0]


def line_sends(planes):
    z = lax.axis_index("dp") // 2
    return [pick(planes, z ^ k, 0) for k in range(4)]


def from_line(sends):
    return [
        lax.ppermute(sends[k], "dp", [(d, d ^ (2 * k)) for d in range(8)]) for k in range(1, 4)
    ]


def sum_line(own, others):
    total = own.astype(jnp.float32)
    for other in others:
        total += other.astype(jnp.float32)
    return total


def gather_column(array):
    parts = [array] + [
        lax.ppermute(array, "dp", [(d, d ^ k) for d in range(8)]) for k in range(1, 8)
    ]
    return jnp.stack(parts)


def gather_columns(part):
    parts = [part] + [
        lax.ppermute(part, "fsdp", [(f, f ^ k) for f in range(4)]) for k in range(1, 4)
    ]
    return jnp.stack(parts).reshape(DEVICES, *part.shape[1:])


ADA_GROUPS = range(FIRST_ADA // (8 * SHARD), (FIRST_DOWN - 1) // (8 * SHARD) + 1)


def sum_to_owners(terms):
    def send(array, change, groups):
        pairs = [(8 * f + d, (8 * f + d) ^ change) for f in groups for d in range(8)]
        return lax.ppermute(array, ("fsdp", "dp"), pairs)

    terms = terms.reshape(4, 4, 2, *terms.shape[1:])
    terms = terms[:, :, 0] + send(terms[:, :, 1], 1, ADA_GROUPS)
    terms = terms[0] + sum(send(terms[k], 8 * k, ADA_GROUPS) for k in range(1, 4))
    return terms[0] + sum(send(terms[k], 2 * k, range(4)) for k in range(1, 4))


def mlp_both_ways(x, g, bias, gathered):
    f32, bf16 = jnp.float32, jnp.bfloat16
    rows = x.shape[0]
    tile = 512
    steps = FF // tile
    full = BLOCK_B // 8
    used = USED_DOWN // 8
    wide = 2 * FF // 128
    chunks = D // 128
    across = (((1,), (1,)), ((), ()))

    def body(x_ref, g_ref, bias_g_ref, bias_u_ref, source, *rest):
        hid_ref, gg_ref, gu_ref, branch_ref, gin_ref, sum_g_ref, sum_u_ref, *rest = rest
        mix_ref, down_ref, sem = rest
        step = pl.program_id(0)

        def each(act, blocks=range(DEVICES)):
            stride = (BLOCK_A + BLOCK_B) // 8
            for i in blocks:
                first = i * stride + BLOCK_A // 8
                if i < MLP_BLOCKS:
                    piece = source.at[pl.ds(first, full)]
                    flat = mix_ref.reshape(MLP_BLOCKS * full, 8, 128)
                    target = flat.at[pl.ds(i * full, full)]
                else:
                    piece = source.at[pl.ds(first, used)]
                    target = down_ref.at[pl.ds((i - MLP_BLOCKS) * used, used)]
                act(pltpu.make_async_copy(piece, target, sem.at[i]))

        @pl.when(step == 0)
        def _():
            each(lambda copy: copy.start())
            branch_ref[...] = jnp.zeros_like(branch_ref)
            gin_ref[...] = jnp.zeros_like(gin_ref)
            each(lambda copy: copy.wait(), range(MLP_BLOCKS))

        def columns(first):
            return jnp.concatenate(
                [
                    mix_ref[: D // 8, first + i].reshape(D, 128)
                    for i in range(tile // 128)
                ],
                axis=1,
            )

        x = x_ref[...]
        w_gate, w_up = columns(tile // 128 * step), columns(wide // 2 + tile // 128 * step)
        gate = jnp.dot(x, w_gate, preferred_element_type=f32) + bias_g_ref[...]
        up = jnp.dot(x, w_up, preferred_element_type=f32) + bias_u_ref[...]
        sigma = jax.nn.sigmoid(gate)
        silu = gate * sigma
        hid = (silu * up).astype(bf16)
        hid_ref[...] = hid
        @pl.when(step == 0)
        def _():
            each(lambda copy: copy.wait(), range(MLP_BLOCKS, DEVICES))

        groups = tile // 8
        low_rows = down_ref[pl.ds(step * groups * chunks, groups * chunks)]
        low_rows = low_rows.reshape(groups, chunks, 8, 128)
        w_down = jnp.concatenate([low_rows[:, j].reshape(tile, 128) for j in range(chunks)], axis=1)
        branch_ref[...] += jnp.dot(hid, w_down, preferred_element_type=f32)
        g_hid = lax.dot_general(g_ref[...], w_down, across, preferred_element_type=f32)
        g_gate = (g_hid * up * sigma * (1.0 + gate * (1.0 - sigma))).astype(bf16)
        g_up = (g_hid * silu).astype(bf16)
        gg_ref[...] = g_gate
        gu_ref[...] = g_up
        sum_g_ref[...] = jnp.sum(g_gate.astype(f32), axis=0, keepdims=True)
        sum_u_ref[...] = jnp.sum(g_up.astype(f32), axis=0, keepdims=True)
        gin_ref[...] += lax.dot_general(
            g_gate, w_gate, across, preferred_element_type=f32
        ) + lax.dot_general(g_up, w_up, across, preferred_element_type=f32)

    whole = pl.BlockSpec((rows, D), lambda t: (0, 0))
    part = pl.BlockSpec((rows, tile), lambda t: (0, t))
    line = pl.BlockSpec((1, tile), lambda t: (0, t))
    return pl.pallas_call(
        body,
        grid=(steps,),
        in_specs=[
            whole,
            whole,
            line,
            pl.BlockSpec((1, tile), lambda t: (0, steps + t)),
            pl.BlockSpec(memory_space=pl.ANY),
        ],
        out_specs=[part, part, part, whole, whole, line, line],
        out_shape=[jax.ShapeDtypeStruct((rows, FF), bf16)] * 3
        + [jax.ShapeDtypeStruct((rows, D), f32)] * 2
        + [jax.ShapeDtypeStruct((1, FF), f32)] * 2,
        scratch_shapes=[
            pltpu.VMEM((MLP_BLOCKS * full // wide, wide, 8, 128), bf16),
            pltpu.VMEM(((DEVICES - MLP_BLOCKS) * used, 8, 128), bf16),
            pltpu.SemaphoreType.DMA((DEVICES,)),
        ],
        cost_estimate=pl.CostEstimate(
            flops=12 * rows * D * FF, bytes_accessed=30_000_000, transcendentals=rows * FF
        ),
        compiler_params=pltpu.CompilerParams(vmem_limit_bytes=56 << 20),
        name="mlp_both_ways",
    )(x, g, bias, bias, gathered)


def pair_product(xo, xp, go, gp):
    down = (((0,), (0,)), ((), ()))
    total = lax.dot_general(xo[...], go[...], down, preferred_element_type=jnp.float32)
    total += lax.dot_general(xp[...], gp[...], down, preferred_element_type=jnp.float32)
    return total.astype(jnp.bfloat16)


def store_tiles(out_ref, lead, first, value):
    for j in range(value.shape[1] // 128):
        out_ref[(*lead, first + j)] = value[:, 128 * j : 128 * (j + 1)]


def grads_b_core_0(in_b, g_gate, g_up):
    def body(xo, xp, gog, gpg, gou, gpu, *outs):
        for out_ref, go, gp in ((outs[0], gog, gpg), (outs[1], gou, gpu)):
            value = pair_product(xo, xp, go, gp)
            for j in range(4):
                part = value[:, 128 * j : 128 * (j + 1)].reshape(16, 7, 8, 128)
                for block in range(16):
                    out_ref[PLACE_B[0][block], :, j] = part[block]

    rows = in_b[0].shape[0]
    high = 16 * 56
    x_spec = pl.BlockSpec((rows, high), lambda t: (0, 0))
    g_spec = pl.BlockSpec((rows, 512), lambda t: (0, t))
    out = pl.pallas_call(
        body,
        grid=(FF // 512,),
        in_specs=[x_spec] * 2 + [g_spec] * 4,
        out_specs=[pl.BlockSpec((16, 7, 4, 8, 128), lambda t: (0, 0, t, 0, 0))] * 2,
        out_shape=[jax.ShapeDtypeStruct((16, 7, FF // 128, 8, 128), jnp.bfloat16)] * 2,
        compiler_params=pltpu.CompilerParams(vmem_limit_bytes=44 << 20),
        name="grads_b_core_0",
    )(*in_b, *g_gate, *g_up)
    return [part.reshape(-1, 128) for part in out]


def grads_b_core_1(in_b, g_gate, g_up, hidden, g_branch):
    bf16 = jnp.bfloat16
    rows = in_b[0].shape[0]
    mlp_steps = FF // 512
    wide = 384
    down_steps = FF // wide
    half_tiles = BLOCK_B // 16
    mlp_groups = (D - 16 * 56) // 8
    groups = (MLP_BLOCKS - 16) * 7
    half_groups = USED_DOWN // 9 // 16
    down_blocks = DEVICES - MLP_BLOCKS

    place = PLACE_B[1]

    def body(place_ref, xo7, xo8, xp7, xp8, gog, gpg, gou, gpu, ho, hp, go, gp, *outs):
        step = pl.program_id(0)

        @pl.when(step == 0)
        def _():
            for group in range(mlp_groups, groups):
                first = place[16 + group // 7] * half_tiles + group % 7 * (FF // 128)
                for out_ref in outs:
                    out_ref[pl.ds(first, FF // 128)] = jnp.zeros((FF // 128, 8, 128), bf16)
            for block in range(down_blocks):
                for half in range(2):
                    used = min(half_groups, FF // 8 - (2 * block + half) * half_groups) * 9
                    first = place[MLP_BLOCKS + block] * half_tiles + used
                    rest = half_tiles - used
                    outs[half][pl.ds(first, rest)] = jnp.zeros((rest, 8, 128), bf16)

        @pl.when(step < mlp_steps)
        def _():
            xo = jnp.concatenate([xo7[...], xo8[...]], axis=1)
            xp = jnp.concatenate([xp7[...], xp8[...]], axis=1)
            for out_ref, g_own, g_par in ((outs[0], gog, gpg), (outs[1], gou, gpu)):
                value = pair_product(xo, xp, g_own, g_par)
                for group in range(mlp_groups):
                    first = place[16 + group // 7] * half_tiles + group % 7 * (FF // 128)
                    store_tiles(
                        out_ref,
                        (),
                        first + step * 4,
                        value[8 * group : 8 * group + 8],
                    )

        @pl.when(step >= mlp_steps)
        def _():
            value = pair_product(ho, hp, go, gp)
            for group in range(wide // 8):
                at = (step - mlp_steps) * (wide // 8) + group
                part = at // half_groups
                first = place_ref[part // 2] * half_tiles + (at % half_groups) * 9
                piece = value[8 * group : 8 * group + 8]

                def put(out_ref, first=first, piece=piece):
                    store_tiles(out_ref, (), first, piece)

                pl.when(part % 2 == 0)(lambda put=put: put(outs[0]))
                pl.when(part % 2 == 1)(lambda put=put: put(outs[1]))

    x_specs = [pl.BlockSpec((rows, 128), lambda t: (0, 7)), pl.BlockSpec((rows, 128), lambda t: (0, 8))]
    g_spec = pl.BlockSpec((rows, 512), lambda t: (0, jnp.minimum(t, mlp_steps - 1)))
    h_spec = pl.BlockSpec((rows, wide), lambda t: (0, jnp.maximum(t - mlp_steps, 0)))
    b_spec = pl.BlockSpec((rows, D), lambda t: (0, 0))
    shape = (16 * half_tiles, 8, 128)
    down_place = jnp.asarray([place[MLP_BLOCKS + i] for i in range(down_blocks)], jnp.int32)
    out = pl.pallas_call(
        body,
        grid=(mlp_steps + down_steps,),
        in_specs=[pl.BlockSpec(memory_space=pltpu.SMEM)]
        + x_specs * 2
        + [g_spec] * 4
        + [h_spec] * 2
        + [b_spec] * 2,
        out_specs=[pl.BlockSpec(shape, lambda t: (0, 0, 0))] * 2,
        out_shape=[jax.ShapeDtypeStruct(shape, bf16)] * 2,
        compiler_params=pltpu.CompilerParams(vmem_limit_bytes=44 << 20),
        name="grads_b_core_1",
    )(down_place, in_b[0], in_b[0], in_b[1], in_b[1], *g_gate, *g_up, *hidden, *g_branch)
    return [part.reshape(-1, 128) for part in out]


def grads_a(core, in_a, g_proj, att, g_branch):
    rows = in_a[0].shape[0]
    steps = 3 * D // 384
    place = PLACE_A[core]

    def store_qkv(value, first_block, step, outs):
        for group in range(48):
            block, half, low = first_block + group // 6, group // 3 % 2, group % 3
            store_tiles(
                outs[half],
                (place[block],),
                low * 27 + step * 3,
                value[8 * group : 8 * group + 8],
            )

    def body(xo, xp, go, gp, zo, zp, bo, bp, *outs):
        step = pl.program_id(0)

        @pl.when(step < steps)
        def _():
            store_qkv(pair_product(xo, xp, go, gp), 8 * core, step, outs)
            if core == 0:
                store_qkv(pair_product(zo, zp, go, gp), 16, step, outs)

        if core == 1:

            @pl.when(step >= steps)
            def _():
                value = pair_product(zo, zp, bo, bp)
                for group in range(144):
                    block, half, low = QKV_BLOCKS + group // 18, group // 9 % 2, group % 9
                    store_tiles(
                        outs[half],
                        (place[block],),
                        low * 9 + (step - steps) * 3,
                        value[8 * group : 8 * group + 8],
                    )

    x_spec = pl.BlockSpec((rows, 384), lambda t: (0, core))
    g_spec = pl.BlockSpec((rows, 384), lambda t: (0, jnp.minimum(t, steps - 1)))
    if core == 0:
        z_spec, z = pl.BlockSpec((rows, 384), lambda t: (0, 2)), in_a
        b_spec, count = pl.BlockSpec((rows, 384), lambda t: (0, 0)), steps
    else:
        z_spec, z = pl.BlockSpec((rows, D), lambda t: (0, 0)), att
        b_spec = pl.BlockSpec((rows, 384), lambda t: (0, jnp.maximum(t - steps, 0)))
        count = steps + D // 384
    shape = (16, 81, 8, 128)
    out = pl.pallas_call(
        body,
        grid=(count,),
        in_specs=[x_spec] * 2 + [g_spec] * 2 + [z_spec] * 2 + [b_spec] * 2,
        out_specs=[pl.BlockSpec(shape, lambda t: (0, 0, 0, 0))] * 2,
        out_shape=[jax.ShapeDtypeStruct(shape, jnp.bfloat16)] * 2,
        compiler_params=pltpu.CompilerParams(vmem_limit_bytes=44 << 20),
        name=f"grads_a_core_{core}",
    )(*in_a, *g_proj, *z, *g_branch)
    return [part.reshape(-1, 128) for part in out]


def gathered_weights(pieces_a, pieces_b):
    me = device_index()
    block_a = spread(pieces_a, PLAN_A)
    block_a = jnp.where(me < QKV_BLOCKS, to_tiles(block_a, 27), to_tiles(block_a, 9))
    block_b = spread(pieces_b, PLAN_B)
    block_b = jnp.where(
        me < MLP_BLOCKS,
        to_tiles(block_b, 48),
        jnp.pad(to_tiles(block_b[:USED_DOWN], 9), ((0, BLOCK_B - USED_DOWN), (0, 0))),
    )
    block = jnp.concatenate([block_a, block_b])
    return lax.all_gather(block, ("fsdp", "dp"), axis=0, tiled=True).reshape(-1, 8, 128)


def head_indicator():
    feature = lax.broadcasted_iota(jnp.int32, (D, 128), 0)
    head = lax.broadcasted_iota(jnp.int32, (D, 128), 1)
    return ((feature >= head * HEAD_DIM) & (feature < (head + 1) * HEAD_DIM)).astype(jnp.bfloat16)


def two_parts(value):
    high = value.astype(jnp.bfloat16)
    return high, (value - high.astype(jnp.float32)).astype(jnp.bfloat16)


def head_means(value, indicator):
    high, low = two_parts(value)
    total = jnp.dot(high, indicator, preferred_element_type=jnp.float32)
    total += jnp.dot(low, indicator, preferred_element_type=jnp.float32)
    return total * (1.0 / HEAD_DIM)


def over_heads(value, indicator):
    high, low = two_parts(value)
    across = (((1,), (1,)), ((), ()))
    total = lax.dot_general(high, indicator, across, preferred_element_type=jnp.float32)
    return total + lax.dot_general(low, indicator, across, preferred_element_type=jnp.float32)


def turned(value):
    quarter = HEAD_DIM // 4
    feature = lax.broadcasted_iota(jnp.int32, value.shape, 1) % (2 * quarter)
    ahead = pltpu.roll(value, D - quarter, 1)
    behind = pltpu.roll(value, quarter, 1)
    return jnp.where(feature < quarter, -ahead, behind)


def heads_of(ref):
    return [ref[:, HEAD_DIM * h : HEAD_DIM * (h + 1)] for h in range(HEADS)]


ACROSS = (((1,), (1,)), ((), ()))
DOWN = (((0,), (0,)), ((), ()))


def attention_forward(projected, cosines, sines):
    f32, bf16 = jnp.float32, jnp.bfloat16
    rows = projected.shape[0]
    length = cosines.shape[0]
    scale = 1.0 / math.sqrt(HEAD_DIM)

    def body(proj_ref, cos_ref, sin_ref, ind_ref, q_ref, k_ref, v_ref, att_ref, log_ref):
        indicator = ind_ref[...]
        for part, ref in ((0, q_ref), (1, k_ref)):
            value = proj_ref[:, D * part : D * (part + 1)]
            inverse = lax.rsqrt(head_means(value * value, indicator) + eps_norm)
            norm = value * over_heads(inverse, indicator)
            ref[...] = (norm * cos_ref[...] + turned(norm) * sin_ref[...]).astype(bf16)
        v_ref[...] = proj_ref[:, 2 * D :].astype(bf16)
        logs = []
        for h in range(HEADS):
            at = slice(HEAD_DIM * h, HEAD_DIM * (h + 1))
            scores = (
                lax.dot_general(q_ref[:, at], k_ref[:, at], ACROSS, preferred_element_type=f32)
                * scale
            )
            top = jnp.max(scores, axis=1, keepdims=True)
            raised = jnp.exp(scores - top)
            total = jnp.sum(raised, axis=1, keepdims=True)
            log_total = top + jnp.log(total)
            probs = (raised * (1.0 / total)).astype(bf16)
            att_ref[:, at] = jnp.dot(probs, v_ref[:, at], preferred_element_type=f32).astype(bf16)
            log_ref[:, h : h + 1] = log_total

    wide = pl.BlockSpec((length, D), lambda i: (i, 0))
    table = pl.BlockSpec((length, D), lambda i: (0, 0))
    return pl.pallas_call(
        body,
        grid=(rows // length,),
        in_specs=[
            pl.BlockSpec((length, 3 * D), lambda i: (i, 0)),
            table,
            table,
            pl.BlockSpec((D, 128), lambda i: (0, 0)),
        ],
        out_specs=[wide] * 4 + [pl.BlockSpec((length, HEADS), lambda i: (i, 0))],
        out_shape=[jax.ShapeDtypeStruct((rows, D), bf16)] * 4
        + [jax.ShapeDtypeStruct((rows, HEADS), f32)],
        cost_estimate=pl.CostEstimate(
            flops=8 * rows * length * D, bytes_accessed=20_000_000, transcendentals=40_000_000
        ),
        compiler_params=pltpu.CompilerParams(vmem_limit_bytes=44 << 20),
        name="attention_forward",
    )(projected, cosines, sines, head_indicator())


def attention_backward(projected, queries, keys, values, log_total, g_attended, cosines, sines):
    f32, bf16 = jnp.float32, jnp.bfloat16
    rows = projected.shape[0]
    length = cosines.shape[0]
    scale = 1.0 / math.sqrt(HEAD_DIM)

    def body(proj_ref, q_ref, k_ref, v_ref, log_ref, g_ref, cos_ref, sin_ref, ind_ref, *rest):
        out_ref, sum_ref, gq_ref, gk_ref, gv_ref = rest
        for h in range(HEADS):
            at = slice(HEAD_DIM * h, HEAD_DIM * (h + 1))
            q, k, v, g = q_ref[:, at], k_ref[:, at], v_ref[:, at], g_ref[:, at]
            scores = lax.dot_general(q, k, ACROSS, preferred_element_type=f32) * scale
            probs = jnp.exp(scores - log_ref[:, h : h + 1])
            g_probs = lax.dot_general(g, v, ACROSS, preferred_element_type=f32)
            gv_ref[:, at] = lax.dot_general(
                probs.astype(bf16), g, DOWN, preferred_element_type=f32
            )
            inner = jnp.sum(probs * g_probs, axis=1, keepdims=True)
            g_scores = (probs * (g_probs - inner)).astype(bf16)
            gq_ref[:, at] = jnp.dot(g_scores, k, preferred_element_type=f32) * scale
            gk_ref[:, at] = (
                lax.dot_general(g_scores, q, DOWN, preferred_element_type=f32) * scale
            )
        indicator = ind_ref[...]
        for part, ref in ((0, gq_ref), (1, gk_ref)):
            value = proj_ref[:, D * part : D * (part + 1)]
            inverse = over_heads(
                lax.rsqrt(head_means(value * value, indicator) + eps_norm), indicator
            )
            norm = value * inverse
            back = ref[...] * cos_ref[...] - turned(ref[...]) * sin_ref[...]
            mean = over_heads(head_means(back * norm, indicator), indicator)
            out_ref[:, D * part : D * (part + 1)] = (inverse * (back - norm * mean)).astype(bf16)
        out_ref[:, 2 * D :] = gv_ref[...].astype(bf16)
        sum_ref[0] = jnp.sum(out_ref[...].astype(f32), axis=0, keepdims=True)

    wide = pl.BlockSpec((length, D), lambda i: (i, 0))
    table = pl.BlockSpec((length, D), lambda i: (0, 0))
    images = rows // length
    return pl.pallas_call(
        body,
        grid=(images,),
        in_specs=[
            pl.BlockSpec((length, 2 * D), lambda i: (i, 0)),
            wide,
            wide,
            wide,
            pl.BlockSpec((length, HEADS), lambda i: (i, 0)),
            wide,
            table,
            table,
            pl.BlockSpec((D, 128), lambda i: (0, 0)),
        ],
        out_specs=[
            pl.BlockSpec((length, 3 * D), lambda i: (i, 0)),
            pl.BlockSpec((1, 1, 3 * D), lambda i: (i, 0, 0)),
        ],
        out_shape=[
            jax.ShapeDtypeStruct((rows, 3 * D), bf16),
            jax.ShapeDtypeStruct((images, 1, 3 * D), f32),
        ],
        scratch_shapes=[pltpu.VMEM((length, D), f32)] * 3,
        cost_estimate=pl.CostEstimate(flops=1000, bytes_accessed=1000, transcendentals=0),
        compiler_params=pltpu.CompilerParams(vmem_limit_bytes=44 << 20),
        name="attention_backward",
    )(projected, queries, keys, values, log_total, g_attended, cosines, sines, head_indicator())


def split_a(gathered):
    block = BLOCK_A // 8

    def body(all_ref, qkv_ref, out_ref, sem):
        copies = []
        for i in range(DEVICES):
            ref, first = (qkv_ref, 0) if i < QKV_BLOCKS else (out_ref, QKV_BLOCKS)
            copies.append(
                pltpu.make_async_copy(
                    all_ref.at[pl.ds(i * (BLOCK_A + BLOCK_B) // 8, block)],
                    ref.at[pl.ds((i - first) * block, block)],
                    sem.at[i],
                )
            )
        for copy in copies:
            copy.start()
        for copy in copies:
            copy.wait()

    w_qkv, w_out = pl.pallas_call(
        body,
        in_specs=[pl.BlockSpec(memory_space=pl.ANY)],
        out_specs=[pl.BlockSpec(memory_space=pltpu.VMEM)] * 2,
        out_shape=[
            jax.ShapeDtypeStruct((ROWS_QKV // 8, 8, 128), jnp.bfloat16),
            jax.ShapeDtypeStruct((ROWS_OUT // 8, 8, 128), jnp.bfloat16),
        ],
        scratch_shapes=[pltpu.SemaphoreType.DMA((DEVICES,))],
        compiler_params=pltpu.CompilerParams(vmem_limit_bytes=40 << 20),
        name="split_a",
    )(gathered)
    return matrix_of_tiles(w_qkv, D, 3 * D), matrix_of_tiles(w_out, D, D)


def owned_rows(back_a, back_b, grad_ada):
    first_a, step_a = starts_a()
    first_b, step_b = starts_b()
    me = device_index()
    numbers = jnp.stack(
        [jnp.asarray(v, jnp.int32) for v in (first_a, step_a, first_b, step_b, me * SHARD)]
    )
    total = SHARD + 2 * BLOCK_B

    def body(numbers_ref, *refs):
        out_ref, sum_ref = refs[-2:]
        sum_ref[...] = jnp.zeros_like(sum_ref)
        for refs_of, at, rows in (
            (refs[: len(back_b)], 2, BLOCK_B),
            (refs[len(back_b) : len(back_b) + len(back_a)], 0, BLOCK_A),
        ):
            for k, ref in enumerate(refs_of):
                start = BLOCK_B + numbers_ref[at] + k * numbers_ref[at + 1]
                start = pl.multiple_of(jnp.clip(start, 0, total - rows), 8)
                sum_ref[pl.ds(start, rows)] += ref[...].astype(jnp.float32)
        row = numbers_ref[4] + lax.broadcasted_iota(jnp.int32, (SHARD, 128), 0)
        out_ref[...] = jnp.where(
            (row >= FIRST_ADA) & (row < FIRST_DOWN),
            refs[-3][...],
            sum_ref[pl.ds(BLOCK_B, SHARD)],
        )

    return pl.pallas_call(
        body,
        in_specs=[pl.BlockSpec(memory_space=pltpu.SMEM)]
        + [pl.BlockSpec(memory_space=pltpu.VMEM)] * (len(back_a) + len(back_b) + 1),
        out_specs=pl.BlockSpec(memory_space=pltpu.VMEM),
        out_shape=jax.ShapeDtypeStruct((SHARD, 128), jnp.float32),
        scratch_shapes=[pltpu.VMEM((total, 128), jnp.float32)],
        compiler_params=pltpu.CompilerParams(vmem_limit_bytes=40 << 20),
        name="owned_rows",
    )(numbers, *back_b, *back_a, grad_ada)


def on_device_32(tokens, conditions, cotangent, slot_mask, weight_flat, bias_flat):
    f32 = jnp.float32
    bf16 = jnp.bfloat16
    axes = ("fsdp", "dp")
    me = device_index()
    core = lax.axis_index("dp") % 2
    slots = conditions.shape[0]
    images = slots * DEVICES
    length = GRID * GRID
    rows_all = slots * length
    cond_count = slots * D
    bias_count = bias_flat.shape[0]
    packed_rows = -(-(cond_count + bias_count) // 128)
    packed = jnp.concatenate(
        [
            conditions.reshape(-1),
            bias_flat,
            jnp.zeros(packed_rows * 128 - cond_count - bias_count, bf16),
        ]
    ).reshape(packed_rows, 128)
    pieces = cut_pieces(weight_flat, PLAN_A), cut_pieces(weight_flat, PLAN_B)
    packed, pieces = lax.optimization_barrier((packed, pieces))
    gathered = gathered_weights(*pieces)
    packed_all = gather_columns(gather_column(packed)).reshape(DEVICES, -1)
    cond_all = packed_all[:, :cond_count].reshape(images, D).astype(f32)
    places = lax.broadcasted_iota(jnp.int32, (DEVICES, DEVICES), 0)
    others = lax.broadcasted_iota(jnp.int32, (DEVICES, DEVICES), 1)
    chosen = ((places ^ me) == others).astype(bf16)
    bias_all = jnp.dot(
        chosen, packed_all[:, cond_count : cond_count + bias_count], preferred_element_type=f32
    ).reshape(-1)
    b_qkv = bias_all[: 3 * D]
    b_out = bias_all[3 * D : 4 * D]
    b_mlp = bias_all[4 * D : 4 * D + 2 * FF]
    b_ada = bias_all[4 * D + 2 * FF :]
    ada_local = weight_flat.reshape(ADA_ROWS, 6 * D)
    ada_start = jnp.clip(
        me * ADA_ROWS - FIRST_ADA * 128 // (6 * D) + ADA_ROWS, 0, D + ADA_ROWS
    )
    cond_act = jax.nn.silu(cond_all).astype(bf16)
    cond_rows = lax.dynamic_slice_in_dim(
        jnp.pad(cond_act.T, ((ADA_ROWS, ADA_ROWS), (0, 0))), ada_start, ADA_ROWS, 0
    )
    cond_ordered = jnp.dot(
        chosen, cond_act.reshape(DEVICES, cond_count), preferred_element_type=f32
    ).astype(bf16)
    rows_ordered = lax.dynamic_slice_in_dim(
        jnp.pad(cond_ordered.reshape(images, D).T, ((ADA_ROWS, ADA_ROWS), (0, 0))),
        ada_start,
        ADA_ROWS,
        0,
    )
    terms = jnp.einsum("km,kn->mn", cond_rows, ada_local, preferred_element_type=f32)
    modulation = sum_to_owners(terms.reshape(DEVICES, slots, 6 * D)) + b_ada
    w_qkv, w_out = split_a(gathered)

    def share(array):
        return (array, lax.ppermute(array, "dp", SWAP_CORE))

    cosines, sines = [jnp.tile(table[:, 0], (1, HEADS)) for table in rope_tables()]
    mask_f = slot_mask.astype(f32)[:, None, None]
    x_f = tokens.astype(f32).reshape(slots, length, D)
    shift_a, scale_a, gate_a, shift_b, scale_b, gate_b = [
        modulation[:, None, place * D : (place + 1) * D] for place in range(6)
    ]
    g_out = cotangent.astype(f32).reshape(slots, length, D) * mask_f
    g_branch_b = (gate_b * g_out).astype(bf16).reshape(rows_all, D)
    normed_a, inv_a = norm_parts(x_f)
    input_a = (normed_a * (1.0 + scale_a) + shift_a).astype(bf16).reshape(rows_all, D)
    projected = jnp.dot(input_a, w_qkv, preferred_element_type=f32) + b_qkv
    queries, keys, values, attended, log_total = attention_forward(projected, cosines, sines)
    branch_a = (jnp.dot(attended, w_out, preferred_element_type=f32) + b_out).reshape(
        slots, length, D
    )
    middle = x_f + gate_a * branch_a
    normed_b, inv_b = norm_parts(middle)
    input_b = (normed_b * (1.0 + scale_b) + shift_b).astype(bf16).reshape(rows_all, D)
    early = [share(array) for array in (input_a, attended, input_b, g_branch_b)]
    input_b = after(input_b, early[0], early[3])
    hidden, g_gate, g_up, branch_b, g_input_b, sum_gate, sum_up = mlp_both_ways(
        input_b, g_branch_b, b_mlp.reshape(1, 2 * FF), gathered
    )
    shared_mlp = [share(array) for array in (g_gate, g_up, hidden)]
    branch_b = branch_b.reshape(slots, length, D)
    g_input_b = g_input_b.reshape(slots, length, D)
    out = ((middle + gate_b * branch_b) * mask_f).astype(bf16).reshape(rows_all, D)
    g_gate_b = jnp.sum(g_out * branch_b, axis=1)
    g_shift_b = jnp.sum(g_input_b, axis=1)
    g_scale_b = jnp.sum(g_input_b * normed_b, axis=1)
    g_middle = g_out + norm_back(g_input_b * (1.0 + scale_b), normed_b, inv_b)
    g_branch_a = (gate_a * g_middle).astype(bf16).reshape(rows_all, D)
    g_gate_a = jnp.sum(g_middle * branch_a, axis=1)
    grad_b_out = jnp.sum(g_branch_a.astype(f32), axis=0)
    shared_branch_a = share(g_branch_a)
    grads_b = lax.cond(
        core == 0,
        lambda: grads_b_core_0(early[2], shared_mlp[0], shared_mlp[1]),
        lambda: grads_b_core_1(early[2], *shared_mlp, early[3]),
    )
    orders = (SWAP_Y, SWAP_X), (SWAP_X, SWAP_Y)
    sends_b = first_sends(grads_b, BLOCK_B)
    arrived = over_planes(sends_b, orders[0])
    g_attended = jnp.einsum(
        "re,de->rd", after(g_branch_a, sends_b), w_out, preferred_element_type=f32
    )
    g_attended = g_attended.astype(bf16)
    g_projected, proj_sums = attention_backward(
        projected, queries, keys, values, log_total, g_attended, cosines, sines
    )
    grad_b_qkv = jnp.sum(proj_sums, axis=(0, 1))
    shared_proj = share(g_projected)
    g_input_a = jnp.einsum("re,de->rd", g_projected, w_qkv, preferred_element_type=f32)
    g_input_a = lax.optimization_barrier(g_input_a).reshape(slots, length, D)
    g_shift_a = jnp.sum(g_input_a, axis=1)
    g_scale_a = jnp.sum(g_input_a * normed_a, axis=1)
    g_modulation = jnp.concatenate(
        [g_shift_a, g_scale_a, g_gate_a, g_shift_b, g_scale_b, g_gate_b], axis=1
    ).astype(bf16)
    bias_sums = [grad_b_qkv, grad_b_out, sum_gate.reshape(-1), sum_up.reshape(-1)]
    small = jnp.concatenate([g_modulation.reshape(-1)] + [b.astype(bf16) for b in bias_sums])
    kept_b, sends_b = second_sends(grads_b, after(arrived, small), BLOCK_B)
    shared_proj = after(shared_proj, sends_b)
    small_all = lax.all_gather(small.reshape(-1, 128), axes, axis=0, tiled=True)
    made_a = lax.cond(
        core == 0,
        lambda: grads_a(0, early[0], shared_proj, early[1], shared_branch_a),
        lambda: grads_a(1, early[0], shared_proj, early[1], shared_branch_a),
    )
    sends_a = first_sends(made_a, BLOCK_A)
    planes_b = plane_sums(kept_b, after(over_planes(sends_b, orders[1]), sends_a))
    sends_b = line_sends(planes_b)
    arrived = after(over_planes(sends_a, orders[0]), sends_b)
    kept_a, sends_a = second_sends(made_a, arrived, BLOCK_A)
    line_b = after(from_line(sends_b), sends_a)
    grad_tokens = g_middle + norm_back(g_input_a * (1.0 + scale_a), normed_a, inv_a)
    sum_b = sum_line(sends_b[0], line_b).astype(bf16)
    halves = sum_b.reshape(2, BLOCK_B // 2, 128)
    sum_b = jnp.where(
        jnp.logical_not(is_kind(PLACE_B, MLP_BLOCKS)),
        jnp.concatenate(
            [from_tiles(half, 24).reshape(-1, 24, 128) for half in halves], axis=1
        ).reshape(-1, 128),
        jnp.pad(
            from_tiles(halves[:, : USED_DOWN // 2].reshape(-1, 128), 9),
            ((0, BLOCK_B - USED_DOWN), (0, 0)),
        ),
    )
    planes_a = plane_sums(kept_a, after(over_planes(sends_a, orders[1]), sum_b))
    sends_a = line_sends(planes_a)
    small_all = after(small_all, sends_a).reshape(DEVICES, -1)
    g_mod_all = small_all[:, : slots * 6 * D].reshape(images, 6 * D)
    g_cond_rows = jnp.einsum("mn,kn->mk", g_mod_all, ada_local, preferred_element_type=f32)
    back_b = send_back(after(sum_b, sends_a), PLAN_B, PLACE_B)
    sum_a = sum_line(sends_a[0], after(from_line(sends_a), back_b)).astype(bf16)
    sum_a = jnp.where(is_kind(PLACE_A, QKV_BLOCKS), from_tiles(sum_a, 9), from_tiles(sum_a, 27))
    back_a = send_back(sum_a, PLAN_A, PLACE_A)
    grad_biases = jnp.concatenate(
        [
            jnp.sum(small_all[:, slots * 6 * D :].astype(f32), axis=0),
            jnp.sum(g_mod_all.astype(f32), axis=0),
        ]
    )
    part_biases = lax.dynamic_slice_in_dim(grad_biases, me * bias_count, bias_count, 0)
    grad_ada = jnp.einsum("km,mn->kn", rows_ordered, g_mod_all, preferred_element_type=f32)
    came = lax.all_to_all(
        g_cond_rows.reshape(DEVICES, slots, ADA_ROWS), axes, split_axis=0, concat_axis=0, tiled=True
    )
    first = FIRST_ADA * 128 // (6 * D)
    g_cond = came.transpose(1, 0, 2).reshape(slots, DEVICES * ADA_ROWS)[:, first : first + D]
    cond_f = conditions.astype(f32)
    sigma_cond = jax.nn.sigmoid(cond_f)
    grad_conditions = g_cond * sigma_cond * (1.0 + cond_f * (1.0 - sigma_cond))
    part_weights = owned_rows(back_a, back_b, grad_ada.reshape(SHARD, 128))
    return (out, grad_tokens.reshape(rows_all, D), grad_conditions, part_weights, part_biases)


def solution(mesh):
    chosen = on_device_32 if dict(mesh.shape) == {"fsdp": 4, "dp": 8} else on_device_plain
    return jax.shard_map(
        chosen,
        mesh=mesh,
        in_specs=(
            P(("fsdp", "dp"), None),
            P(("fsdp", "dp"), None),
            P(("fsdp", "dp"), None),
            P(("fsdp", "dp")),
            P(("fsdp", "dp"), None),
            P(("fsdp", "dp")),
        ),
        out_specs=(
            P(("fsdp", "dp"), None),
            P(("fsdp", "dp"), None),
            P(("fsdp", "dp"), None),
            P(("fsdp", "dp"), None),
            P(("fsdp", "dp")),
        ),
        check_vma=False,
    )
```
